32 devices in a mesh: fsdp: 4 (over z), ctx: 2 (over y), tp: 4 (over x, core).
Axes of the slice: x: 2, y: 2, z: 4, core: 2. Of those that a mesh axis runs over, the one named last changes fastest.
Arguments:
- inputs: bfloat16 [8, 2048, 512], P('fsdp', ('ctx', 'tp')), may hold values from -6 to 6
- memory: bfloat16 [8, 512, 512], P('fsdp', ('ctx', 'tp')), may hold values from -6 to 6
- cotangent: bfloat16 [8, 2048, 512], P('fsdp', ('ctx', 'tp')), may hold values from -6 to 6
- positions: int32 [8, 2048], P('fsdp'), may hold values from 0 to 2047, each once within a row
- lengths: int32 [8], P('fsdp'), may hold values from 1024 to 2048, as said below
- memory_lengths: int32 [8], P('fsdp'), may hold values from 128 to 512, as said below
- query_weight: bfloat16 [512, 512], P(('fsdp', 'ctx'), 'tp'), may hold values from -0.375 to 0.375
- key_weight: bfloat16 [512, 512], P(('fsdp', 'ctx'), 'tp'), may hold values from -0.375 to 0.375
- value_weight: bfloat16 [512, 512], P(('fsdp', 'ctx'), 'tp'), may hold values from -0.25 to 0.25
- output_weight: bfloat16 [512, 512], P('tp', ('fsdp', 'ctx')), may hold values from -1 to 1
- cross_query_weight: bfloat16 [512, 512], P(('fsdp', 'ctx'), 'tp'), may hold values from -0.375 to 0.375
- cross_key_weight: bfloat16 [512, 512], P(('fsdp', 'ctx'), 'tp'), may hold values from -0.375 to 0.375
- cross_value_weight: bfloat16 [512, 512], P(('fsdp', 'ctx'), 'tp'), may hold values from -0.25 to 0.25
- cross_output_weight: bfloat16 [512, 512], P('tp', ('fsdp', 'ctx')), may hold values from -1 to 1
- expand_weight: bfloat16 [512, 2048], P(('fsdp', 'ctx'), 'tp'), may hold values from -0.25 to 0.25
- reduce_weight: bfloat16 [2048, 512], P('tp', ('fsdp', 'ctx')), may hold values from -0.1875 to 0.1875
- query_bias: float32 [512], replicated, may hold values from -1.5 to 1.5
- value_bias: float32 [512], replicated, may hold values from -1.5 to 1.5
- output_bias: float32 [512], replicated, may hold values from -1.5 to 1.5
- first_gain: float32 [512], replicated, may hold values from 0.5 to 1.5
- first_shift: float32 [512], replicated, may hold values from -1.5 to 1.5
- cross_query_bias: float32 [512], replicated, may hold values from -1.5 to 1.5
- cross_value_bias: float32 [512], replicated, may hold values from -1.5 to 1.5
- cross_output_bias: float32 [512], replicated, may hold values from -1.5 to 1.5
- second_gain: float32 [512], replicated, may hold values from 0.5 to 1.5
- second_shift: float32 [512], replicated, may hold values from -1.5 to 1.5
- expand_bias: float32 [2048], replicated, may hold values from -2.5 to 2.5
- reduce_bias: float32 [512], replicated, may hold values from -1.5 to 1.5
- third_gain: float32 [512], replicated, may hold values from 0.5 to 1.5
- third_shift: float32 [512], replicated, may hold values from -1.5 to 1.5
Outputs:
- outputs: float32 [8, 2048, 512], P('fsdp', ('ctx', 'tp'))
- input_grad: float32 [8, 2048, 512], P('fsdp', ('ctx', 'tp'))
- memory_grad: float32 [8, 512, 512], P('fsdp', ('ctx', 'tp'))
- query_weight_grad: float32 [512, 512], P(('fsdp', 'ctx'), 'tp')
- key_weight_grad: float32 [512, 512], P(('fsdp', 'ctx'), 'tp')
- value_weight_grad: float32 [512, 512], P(('fsdp', 'ctx'), 'tp')
- output_weight_grad: float32 [512, 512], P('tp', ('fsdp', 'ctx'))
- cross_query_weight_grad: float32 [512, 512], P(('fsdp', 'ctx'), 'tp')
- cross_key_weight_grad: float32 [512, 512], P(('fsdp', 'ctx'), 'tp')
- cross_value_weight_grad: float32 [512, 512], P(('fsdp', 'ctx'), 'tp')
- cross_output_weight_grad: float32 [512, 512], P('tp', ('fsdp', 'ctx'))
- expand_weight_grad: float32 [512, 2048], P(('fsdp', 'ctx'), 'tp')
- reduce_weight_grad: float32 [2048, 512], P('tp', ('fsdp', 'ctx'))
- query_bias_grad: float32 [512], replicated
- value_bias_grad: float32 [512], replicated
- output_bias_grad: float32 [512], replicated
- first_gain_grad: float32 [512], replicated
- first_shift_grad: float32 [512], replicated
- cross_query_bias_grad: float32 [512], replicated
- cross_value_bias_grad: float32 [512], replicated
- cross_output_bias_grad: float32 [512], replicated
- second_gain_grad: float32 [512], replicated
- second_shift_grad: float32 [512], replicated
- expand_bias_grad: float32 [2048], replicated
- reduce_bias_grad: float32 [512], replicated
- third_gain_grad: float32 [512], replicated
- third_shift_grad: float32 [512], replicated
The draws below stay inside these ranges and needn't reach their ends.
Inputs may be any that keep to these rules, and one draw needn't show every extreme that they name: `lengths`: some sequence has 2048 tokens in every draw. `memory_lengths`: some memory has 512 tokens in every draw. Each row is a permutation of the positions 0 to 2047.
All inputs are finite; a program needn't handle non-finite values.
Results may differ from the reference program's by a relative error of at most 0.025.
The reference program's roundings to bfloat16 on the way count: a program that leaves them out, or rounds other values in their place, can miss the bound.
Values may be sent and summed in bfloat16 or wider, within the bound.
No kernel may reach another device: no remote copies, remote signals or barrier semaphores. Data moves between devices by JAX's collectives and lax.ppermute only.
A program may use at most 192 MiB of HBM per device.

```python
import math
import jax
import jax.numpy as jnp
from jax import lax

D = 512
HEAD_DIM = 64
FF = 2048
SEQ_LEN = 2048
MIN_LEN = 1024
MEM = 512
MIN_MEM = 128
SEQS = 8


def draw_lengths(key, part):
    drawn = jax.random.randint(jax.random.fold_in(key, 11), (SEQS,), MIN_LEN, SEQ_LEN + 1)
    longest = jax.random.randint(jax.random.fold_in(key, 12), (), 0, SEQS)
    return jnp.where(jnp.arange(SEQS) == longest, SEQ_LEN, drawn).astype(jnp.int32)


def draw_memory_lengths(key, part):
    drawn = jax.random.randint(jax.random.fold_in(key, 21), (SEQS,), MIN_MEM, MEM + 1)
    longest = jax.random.randint(jax.random.fold_in(key, 22), (), 0, SEQS)
    return jnp.where(jnp.arange(SEQS) == longest, MEM, drawn).astype(jnp.int32)


def levels(own_key, dims, split, low, top_value):
    level = 1.0
    for axis_at, blocks in split:
        draws = jax.random.uniform(jax.random.fold_in(jax.random.fold_in(own_key, 6), axis_at), (blocks,), jnp.float32, low / len(split), top_value / len(split))
        level = level * jnp.repeat(jnp.exp(draws), dims[axis_at] // blocks).reshape((-1,) + (1,) * (len(dims) - 1 - axis_at))
    return level


def centred(own_key, dims, deviation, most, pieces=(), dtype=jnp.bfloat16):
    array = deviation * jax.random.normal(own_key, dims, jnp.float32)
    if pieces:
        array = array * levels(own_key, dims, pieces, -0.22, 0.18)
    return jnp.clip(array, -most, most).astype(dtype)


def setup_inputs(seed: int = 0) -> dict:
    arg_keys = jax.random.split(jax.random.key(seed), 31)
    return {
        "inputs": centred(arg_keys[0], (SEQS, SEQ_LEN, D), 1.0, 6.0, ((0, 4), (1, 8))),
        "memory": centred(arg_keys[1], (SEQS, MEM, D), 1.0, 6.0, ((0, 4), (1, 8))),
        "cotangent": centred(arg_keys[2], (SEQS, SEQ_LEN, D), 1.0, 6.0, ((0, 4), (1, 8))),
        "positions": jax.vmap(lambda own: jax.random.permutation(own, SEQ_LEN))(jax.random.split(arg_keys[3], SEQS)).reshape((SEQS, SEQ_LEN)).astype(jnp.int32),
        "lengths": draw_lengths(jax.random.fold_in(arg_keys[30], 71), 0),
        "memory_lengths": draw_memory_lengths(jax.random.fold_in(arg_keys[30], 71), 0),
        "query_weight": centred(arg_keys[6], (D, D), (D // 2) ** -0.5, 0.375, ((0, 8), (1, 4))),
        "key_weight": centred(arg_keys[7], (D, D), (D // 2) ** -0.5, 0.375, ((0, 8), (1, 4))),
        "value_weight": centred(arg_keys[8], (D, D), D ** -0.5, 0.25, ((0, 8), (1, 4))),
        "output_weight": centred(arg_keys[9], (D, D), 32 ** -0.5, 1.0, ((0, 4), (1, 8))),
        "cross_query_weight": centred(arg_keys[10], (D, D), (D // 2) ** -0.5, 0.375, ((0, 8), (1, 4))),
        "cross_key_weight": centred(arg_keys[11], (D, D), (D // 2) ** -0.5, 0.375, ((0, 8), (1, 4))),
        "cross_value_weight": centred(arg_keys[12], (D, D), D ** -0.5, 0.25, ((0, 8), (1, 4))),
        "cross_output_weight": centred(arg_keys[13], (D, D), 32 ** -0.5, 1.0, ((0, 4), (1, 8))),
        "expand_weight": centred(arg_keys[14], (D, FF), D ** -0.5, 0.25, ((0, 8), (1, 4))),
        "reduce_weight": centred(arg_keys[15], (FF, D), (FF // 2) ** -0.5, 0.1875, ((0, 4), (1, 8))),
        "query_bias": centred(arg_keys[16], (D,), 0.3, 1.5, (), jnp.float32),
        "value_bias": centred(arg_keys[17], (D,), 0.3, 1.5, (), jnp.float32),
        "output_bias": centred(arg_keys[18], (D,), 0.3, 1.5, (), jnp.float32),
        "first_gain": jnp.clip(1.0 + 0.1 * jax.random.normal(arg_keys[19], (D,), jnp.float32), 0.5, 1.5),
        "first_shift": centred(arg_keys[20], (D,), 0.3, 1.5, (), jnp.float32),
        "cross_query_bias": centred(arg_keys[21], (D,), 0.3, 1.5, (), jnp.float32),
        "cross_value_bias": centred(arg_keys[22], (D,), 0.3, 1.5, (), jnp.float32),
        "cross_output_bias": centred(arg_keys[23], (D,), 0.3, 1.5, (), jnp.float32),
        "second_gain": jnp.clip(1.0 + 0.1 * jax.random.normal(arg_keys[24], (D,), jnp.float32), 0.5, 1.5),
        "second_shift": centred(arg_keys[25], (D,), 0.3, 1.5, (), jnp.float32),
        "expand_bias": centred(arg_keys[26], (FF,), 0.5, 2.5, (), jnp.float32),
        "reduce_bias": centred(arg_keys[27], (D,), 0.3, 1.5, (), jnp.float32),
        "third_gain": jnp.clip(1.0 + 0.1 * jax.random.normal(arg_keys[28], (D,), jnp.float32), 0.5, 1.5),
        "third_shift": centred(arg_keys[29], (D,), 0.3, 1.5, (), jnp.float32),
    }


EPSILON = 1e-05
NEGATIVE = -1e+30

@jax.custom_vjp
def low(v):
    return lax.optimization_barrier(v.astype(jnp.bfloat16)).astype(jnp.float32)

@jax.custom_vjp
def low_back(v):
    return v

def low_keep(v):
    return (low(v), None)

def low_pass(kept, grad):
    return (grad,)

def back_keep(v):
    return (v, None)

def back_low(kept, grad):
    return (low(grad),)
low.defvjp(low_keep, low_pass)
low_back.defvjp(back_keep, back_low)

def product(left, right):
    return jnp.dot(left, right, preferred_element_type=jnp.float32, precision=lax.Precision.HIGHEST)

def layer_norm(values, gain, shift):
    center = values - lax.optimization_barrier(jnp.mean(values, axis=-1, keepdims=True))
    spread = lax.optimization_barrier(jnp.mean(center * center, axis=-1, keepdims=True))
    return center * lax.rsqrt(spread + EPSILON) * gain + shift

def attention(query, keys, values, allowed):
    query_heads = query.reshape(query.shape[0], -1, HEAD_DIM)
    key_heads = keys.reshape(keys.shape[0], -1, HEAD_DIM)
    value_heads = values.reshape(values.shape[0], -1, HEAD_DIM)
    scores = jnp.einsum('qhd,khd->hqk', query_heads, key_heads, precision=lax.Precision.HIGHEST) / math.sqrt(HEAD_DIM)
    scores = low_back(scores)
    scores = jnp.where(allowed[None], scores, NEGATIVE)
    probs = jax.nn.softmax(scores, axis=-1)
    mixed = jnp.einsum('hqk,khd->qhd', low(probs), value_heads, precision=lax.Precision.HIGHEST)
    return mixed.reshape(query.shape[0], -1)

def sequence(weights, source, memory_rows, slot_positions, length, memory_length):
    query_weight, key_weight, value_weight, output_weight, cross_query_weight, cross_key_weight, cross_value_weight, cross_output_weight, expand_weight, reduce_weight, query_bias, value_bias, output_bias, first_gain, first_shift, cross_query_bias, cross_value_bias, cross_output_bias, second_gain, second_shift, expand_bias, reduce_bias, third_gain, third_shift = weights
    allowed = (slot_positions[None, :] <= slot_positions[:, None]) & (slot_positions[None, :] < length)
    query = low_back(low(product(source, query_weight) + query_bias))
    key = low_back(low(product(source, key_weight)))
    value = low_back(low(product(source, value_weight) + value_bias))
    attended = low_back(low(attention(query, key, value, allowed)))
    first_in = source + low_back(product(attended, output_weight)) + output_bias
    first_out = layer_norm(first_in, first_gain, first_shift)
    cross_query = low_back(low(product(low(first_out), cross_query_weight) + cross_query_bias))
    memory_key = low_back(low(product(memory_rows, cross_key_weight)))
    memory_value = low_back(low(product(memory_rows, cross_value_weight) + cross_value_bias))
    cross_allowed = jnp.broadcast_to((jnp.arange(MEM) < memory_length)[None, :], (SEQ_LEN, MEM))
    cross_attended = low_back(low(attention(cross_query, memory_key, memory_value, cross_allowed)))
    second_in = first_out + low_back(product(cross_attended, cross_output_weight)) + cross_output_bias
    second_out = layer_norm(second_in, second_gain, second_shift)
    expanded = low_back(product(low(second_out), expand_weight) + expand_bias)
    activated = low(jax.nn.silu(expanded))
    third_in = second_out + low_back(product(activated, reduce_weight)) + reduce_bias
    return layer_norm(third_in, third_gain, third_shift)

def reference(inputs, memory, cotangent, positions, lengths, memory_lengths, query_weight, key_weight, value_weight, output_weight, cross_query_weight, cross_key_weight, cross_value_weight, cross_output_weight, expand_weight, reduce_weight, query_bias, value_bias, output_bias, first_gain, first_shift, cross_query_bias, cross_value_bias, cross_output_bias, second_gain, second_shift, expand_bias, reduce_bias, third_gain, third_shift):
    params = tuple((item.astype(jnp.float32) for item in (query_weight, key_weight, value_weight, output_weight, cross_query_weight, cross_key_weight, cross_value_weight, cross_output_weight, expand_weight, reduce_weight, query_bias, value_bias, output_bias, first_gain, first_shift, cross_query_bias, cross_value_bias, cross_output_bias, second_gain, second_shift, expand_bias, reduce_bias, third_gain, third_shift)))
    sources = inputs.astype(jnp.float32)
    memories = memory.astype(jnp.float32)
    valid = positions < lengths[:, None]
    masked_grad = jnp.where(valid[:, :, None], cotangent.astype(jnp.float32), jnp.zeros((), jnp.float32))

    def forward(weights, source_all, memory_all):

        def single(item):
            return sequence(weights, item[0], item[1], item[2], item[3], item[4])
        return lax.map(jax.checkpoint(single), (source_all, memory_all, positions, lengths, memory_lengths))
    result, pullback = jax.vjp(forward, params, sources, memories)
    grads, input_grad, memory_grad = pullback(masked_grad)
    return (result.astype(jnp.float32), input_grad.astype(jnp.float32), memory_grad.astype(jnp.float32), grads[0], grads[1], grads[2], grads[3], grads[4], grads[5], grads[6], grads[7], grads[8], grads[9], grads[10], grads[11], grads[12], grads[13], grads[14], grads[15], grads[16], grads[17], grads[18], grads[19], grads[20], grads[21], grads[22], grads[23])
```

```python
import functools

import jax
import jax.numpy as jnp
from jax import lax
from jax.experimental import pallas as pl
from jax.experimental.pallas import tpu as pltpu
from jax.sharding import PartitionSpec as P

HEAD_DIM = 64
EPSILON = 1e-05
NEGATIVE = -1e30
F32 = jnp.float32
BF16 = jnp.bfloat16
SCALE = HEAD_DIM ** -0.5
VMEM_BYTES = 58 * 2 ** 20


def contract(left, right, left_dim, right_dim):
    return lax.dot_general(
        left, right, (((left_dim,), (right_dim,)), ((), ())), preferred_element_type=F32
    )


def product(left, right):
    return contract(left, right, 1, 0)


def product_left(left, right):
    return contract(left, right, 0, 0)


def product_right(left, right):
    return contract(left, right, 1, 1)


def layer_norm(values, gain, shift):
    center = values - jnp.mean(values, axis=-1, keepdims=True)
    spread = jnp.mean(center * center, axis=-1, keepdims=True)
    return center * lax.rsqrt(spread + EPSILON) * gain + shift


def norm_back(values, gain, grad):
    center = values - jnp.mean(values, axis=-1, keepdims=True)
    spread = jnp.mean(center * center, axis=-1, keepdims=True)
    rate = lax.rsqrt(spread + EPSILON)
    normal = center * rate
    scaled = grad * gain
    back = rate * (
        scaled
        - jnp.mean(scaled, axis=-1, keepdims=True)
        - normal * jnp.mean(scaled * normal, axis=-1, keepdims=True)
    )
    return back, jnp.sum(grad * normal, axis=0), jnp.sum(grad, axis=0)


def attend_kernel(heads, q, k, v, qp, kp, out, weights, inverse):
    allowed = kp[...] <= qp[...]
    for head in range(heads):
        cols = slice(head * HEAD_DIM, (head + 1) * HEAD_DIM)
        scores = contract(k[:, cols], q[:, cols] * SCALE, 1, 1)
        scores = jnp.where(allowed, scores, NEGATIVE)
        largest = jnp.max(scores, axis=0, keepdims=True)
        power = jnp.exp(scores - largest)
        rate = 1.0 / jnp.sum(power, axis=0, keepdims=True)
        low = power.astype(BF16)
        weights[head] = low
        inverse[head] = rate
        out[:, cols] = (contract(v[:, cols], low, 0, 0) * rate).T.astype(BF16)


def attend_back_kernel(heads, q, k, v, weights, inverse, out, grad, dq, dk, dv):
    for head in range(heads):
        cols = slice(head * HEAD_DIM, (head + 1) * HEAD_DIM)
        grads = grad[:, cols].astype(F32).T
        outs = out[:, cols].astype(F32).T
        inner = jnp.sum(grads * outs, axis=0, keepdims=True) * inverse[head]
        scaled = (grads * inverse[head]).astype(BF16)
        weight = weights[head]
        grad_weight = contract(v[:, cols], scaled, 1, 0)
        grad_scores = (weight.astype(F32) * (grad_weight - inner)).astype(BF16)
        dq[:, cols] = (contract(k[:, cols], grad_scores, 0, 0) * SCALE).T.astype(BF16)
        dv[:, cols] = contract(weight, scaled, 1, 1).astype(BF16)
        dk[:, cols] = (contract(grad_scores, q[:, cols], 1, 0) * SCALE).astype(BF16)


HEADS_PER_STEP = 2


def column_block(rows):
    return pl.BlockSpec((rows, HEADS_PER_STEP * HEAD_DIM), lambda i: (0, i))


def head_block(*dims):
    return pl.BlockSpec((HEADS_PER_STEP,) + dims, lambda i: (i, 0, 0))


def attend(q, k, v, qp, kp):
    rows, width = q.shape
    keys = k.shape[0]
    heads = width // HEAD_DIM
    return pl.pallas_call(
        functools.partial(attend_kernel, HEADS_PER_STEP),
        grid=(heads // HEADS_PER_STEP,),
        in_specs=[
            column_block(rows),
            column_block(keys),
            column_block(keys),
            pl.BlockSpec((1, rows), lambda i: (0, 0)),
            pl.BlockSpec((keys, 1), lambda i: (0, 0)),
        ],
        out_specs=[column_block(rows), head_block(keys, rows), head_block(1, rows)],
        out_shape=[
            jax.ShapeDtypeStruct((rows, width), BF16),
            jax.ShapeDtypeStruct((heads, keys, rows), BF16),
            jax.ShapeDtypeStruct((heads, 1, rows), F32),
        ],
        compiler_params=pltpu.CompilerParams(vmem_limit_bytes=VMEM_BYTES),
        cost_estimate=pl.CostEstimate(
            flops=4 * rows * keys * width * 4,
            transcendentals=heads * rows * keys,
            bytes_accessed=2 * heads * rows * keys,
        ),
        name="attend",
    )(q, k, v, qp, kp)


def attend_back(q, k, v, weights, inverse, out, grad):
    rows, width = q.shape
    keys = k.shape[0]
    heads = width // HEAD_DIM
    return pl.pallas_call(
        functools.partial(attend_back_kernel, HEADS_PER_STEP),
        grid=(heads // HEADS_PER_STEP,),
        in_specs=[
            column_block(rows),
            column_block(keys),
            column_block(keys),
            head_block(keys, rows),
            head_block(1, rows),
            column_block(rows),
            column_block(rows),
        ],
        out_specs=[column_block(rows), column_block(keys), column_block(keys)],
        out_shape=[
            jax.ShapeDtypeStruct((rows, width), BF16),
            jax.ShapeDtypeStruct((keys, width), BF16),
            jax.ShapeDtypeStruct((keys, width), BF16),
        ],
        compiler_params=pltpu.CompilerParams(vmem_limit_bytes=VMEM_BYTES),
        cost_estimate=pl.CostEstimate(
            flops=8 * rows * keys * width * 4,
            transcendentals=0,
            bytes_accessed=2 * heads * rows * keys,
        ),
        name="attend_back",
    )(q, k, v, weights, inverse, out, grad)


def move(sources, shapes, plan, name):
    def body(*refs):
        given = refs[: len(sources)]
        made = refs[len(sources) : len(sources) + len(shapes)]
        sems = refs[-1]
        copies = []
        for at, (i, a, j, b) in enumerate(plan()):
            copies.append(pltpu.make_async_copy(given[i].at[a], made[j].at[b], sems.at[at]))
        for copy in copies:
            copy.start()
        for copy in copies:
            copy.wait()

    count = move_count(plan)
    return pl.pallas_call(
        body,
        in_specs=[pl.BlockSpec(memory_space=pl.ANY)] * len(sources),
        out_specs=[pl.BlockSpec(memory_space=pl.ANY)] * len(shapes),
        out_shape=[jax.ShapeDtypeStruct(shape, BF16) for shape in shapes],
        scratch_shapes=[pltpu.SemaphoreType.DMA((count,))],
        name=name,
    )(*sources)


def move_count(plan):
    return len(plan())


def sizes():
    return lax.axis_size("fsdp"), lax.axis_size("ctx"), lax.axis_size("tp") // 2


def places():
    tp = lax.axis_index("tp")
    return lax.axis_index("fsdp"), lax.axis_index("ctx"), tp // 2, tp % 2


def swap(value):
    total = lax.axis_size("tp")
    return lax.ppermute(value, "tp", [(i, i ^ 1) for i in range(total)])


def shift_x(value, step):
    total = lax.axis_size("tp")
    return lax.ppermute(value, "tp", [(i, (i + 2 * step) % total) for i in range(total)])


def shift(value, axis, step):
    total = lax.axis_size(axis)
    return lax.ppermute(value, axis, [(i, (i + step) % total) for i in range(total)])


def offsets():
    unused, high, wide = sizes()
    return [(dx, dy) for dy in range(high) for dx in range(wide)]


def is_square():
    unused, high, wide = sizes()
    return high == 2 and wide == 2


def gather_plane(first, second):
    if is_square():
        side = (shift_x(first, 1), shift_x(second, 1))
        front = (shift(first, "ctx", 1), shift(second, "ctx", 1))
        far = (shift(side[0], "ctx", 1), shift_x(front[1], 1))
        return [(first, second), side, front, far]
    unused, high, wide = sizes()
    row = [(first, second)] + [(shift_x(first, k), shift_x(second, k)) for k in range(1, wide)]
    blocks = list(row)
    for step in range(1, high):
        blocks += [(shift(a, "ctx", step), shift(b, "ctx", step)) for a, b in row]
    return blocks


def add(left, right):
    return (left.astype(F32) + right.astype(F32)).astype(BF16)


def scatter_plane(blocks):
    if is_square():
        own, side, front, far = blocks
        side_first = add(side[0], shift(far[0], "ctx", 1))
        front_second = add(front[1], shift_x(far[1], 1))
        from_side = (shift_x(side_first, 1), shift_x(side[1], 1))
        from_front = (shift(front[0], "ctx", 1), shift(front_second, "ctx", 1))
        return [own, from_side, from_front]
    unused, high, wide = sizes()
    row = []
    for dx in range(wide):
        total = blocks[dx]
        for dy in range(1, high):
            other = blocks[dy * wide + dx]
            total = tuple(add(a, shift(b, "ctx", -dy)) for a, b in zip(total, other))
        row.append(total)
    return [row[0]] + [
        (shift_x(row[dx][0], -dx), shift_x(row[dx][1], -dx)) for dx in range(1, wide)
    ]


def summed(parts):
    return sum(part.astype(F32) for part in parts)


def gather_weights(packed, widths):
    deep, high, wide = sizes()
    rows, total = packed.shape
    half = deep // 2
    pieces = [packed] + [shift(packed, "fsdp", k) for k in range(1, deep)]

    def by_depth():
        at = lax.axis_index("fsdp")
        return [(k, slice(None), 0, (at - k + deep) % deep) for k in range(deep)]

    stacked = move(pieces, [(deep, rows, total)], by_depth, "stack_depth")[0]
    blocks = gather_plane(stacked[:half], stacked[half:])
    order = offsets()

    def side_by_side():
        steps = []
        for n in range(len(order)):
            steps.append((2 * n, slice(None), 0, (n, slice(0, half))))
            steps.append((2 * n + 1, slice(None), 0, (n, slice(half, deep))))
        return steps

    own = move(
        [part for block in blocks for part in block],
        [(len(order), deep, rows, total)],
        side_by_side,
        "stack_plane",
    )[0]
    other = swap(own)
    starts = [sum(widths[:i]) for i in range(len(widths))]
    if all(width % 128 == 0 for width in widths):

        def into_place():
            unused, y, x, core = places()
            steps = []
            for n, (dx, dy) in enumerate(order):
                at_y = (y - dy + high) % high
                at_x = (x - dx + wide) % wide
                for who in range(2):
                    at = 2 * at_x + (core if who == 0 else 1 - core)
                    for j, width in enumerate(widths):
                        cols = slice(starts[j], starts[j] + width)
                        here = pl.ds(pl.multiple_of(at * width, 128), width)
                        steps.append(
                            (
                                who,
                                (n, slice(None), slice(None), cols),
                                j,
                                (slice(None), at_y, slice(None), here),
                            )
                        )
            return steps

        made = move(
            [own, other],
            [(deep, high, rows, 2 * wide * width) for width in widths],
            into_place,
            "place_weights",
        )
        return [m.reshape(deep * high * rows, -1) for m in made]
    unused, y, x, core = places()
    whole = jnp.zeros((high, wide, 2, deep, rows, total), BF16)
    for n, (dx, dy) in enumerate(order):
        for who, part in ((core, own), (1 - core, other)):
            at = ((y - dy + high) % high, (x - dx + wide) % wide, who, 0, 0, 0)
            whole = lax.dynamic_update_slice(whole, part[n][None, None, None], at)
    made = []
    for start, width in zip(starts, widths):
        part = whole[..., start : start + width]
        part = part.transpose(3, 0, 4, 1, 2, 5)
        made.append(part.reshape(deep * high * rows, 2 * wide * width))
    return made


def scatter_weights(grads, widths):
    deep, high, wide = sizes()
    rows = grads[0].shape[0] // (deep * high)
    total = sum(widths)
    half = deep // 2
    order = offsets()
    starts = [sum(widths[:i]) for i in range(len(widths))]
    shaped = [g.reshape(deep, high, rows, 2 * wide * w) for g, w in zip(grads, widths)]
    if all(width % 128 == 0 for width in widths):

        def into_blocks():
            unused, y, x, core = places()
            steps = []
            for n, (dx, dy) in enumerate(order):
                at_y = (y - dy + high) % high
                at_x = (x - dx + wide) % wide
                for who in range(2):
                    at = 2 * at_x + (core if who == 0 else 1 - core)
                    for j, width in enumerate(widths):
                        cols = slice(starts[j], starts[j] + width)
                        here = pl.ds(pl.multiple_of(at * width, 128), width)
                        steps.append(
                            (
                                j,
                                (slice(None), at_y, slice(None), here),
                                who,
                                (n, slice(None), slice(None), cols),
                            )
                        )
            return steps

        keep, send = move(
            shaped, [(len(order), deep, rows, total)] * 2, into_blocks, "split_weights"
        )
    else:
        unused, y, x, core = places()
        whole = jnp.concatenate(
            [g.reshape(deep, high, rows, wide, 2, w) for g, w in zip(shaped, widths)], axis=-1
        ).transpose(1, 3, 4, 0, 2, 5)
        size = (1, 1, 1, deep, rows, total)

        def pick(dx, dy, who):
            at = ((y - dy + high) % high, (x - dx + wide) % wide, who, 0, 0, 0)
            return lax.dynamic_slice(whole, at, size).reshape(size[3:])

        keep = jnp.stack([pick(dx, dy, core) for dx, dy in order])
        send = jnp.stack([pick(dx, dy, 1 - core) for dx, dy in order])
    other = swap(send)
    blocks = [
        (add(keep[n, :half], other[n, :half]), add(keep[n, half:], other[n, half:]))
        for n in range(len(order))
    ]
    left = scatter_plane(blocks)
    own = jnp.concatenate([summed([part[h] for part in left]) for h in range(2)], axis=0)
    low = own.astype(BF16)
    at = lax.axis_index("fsdp")
    result = lax.dynamic_index_in_dim(own, at, 0, keepdims=False)
    for k in range(1, deep):
        piece = lax.dynamic_index_in_dim(low, (at + k) % deep, 0, keepdims=False)
        result = result + shift(piece, "fsdp", k).astype(F32)
    return result


def all_sum(value):
    for axis in ("tp", "ctx", "fsdp"):
        total = lax.axis_size(axis)
        step = 1
        while step < total:
            pairs = [(i, i ^ step) for i in range(total)]
            value = value + lax.ppermute(value, axis, pairs)
            step *= 2
    return value


def per_device(
    inputs,
    memory,
    cotangent,
    positions,
    lengths,
    memory_lengths,
    query_weight,
    key_weight,
    value_weight,
    output_weight,
    cross_query_weight,
    cross_key_weight,
    cross_value_weight,
    cross_output_weight,
    expand_weight,
    reduce_weight,
    query_bias,
    value_bias,
    output_bias,
    first_gain,
    first_shift,
    cross_query_bias,
    cross_value_bias,
    cross_output_bias,
    second_gain,
    second_shift,
    expand_bias,
    reduce_bias,
    third_gain,
    third_shift,
):
    deep, high, wide = sizes()
    z, y, x, core = places()
    own_rows, width = inputs.shape[1:]
    own_memory = memory.shape[1]
    rows = 2 * own_rows
    head_width = query_weight.shape[1]
    hidden_width = expand_weight.shape[1]

    def exchange(value):
        keep = lax.dynamic_index_in_dim(value, core, 0, keepdims=False)
        give = lax.dynamic_index_in_dim(value, 1 - core, 0, keepdims=False)
        return keep, swap(give)

    input_pair = exchange(inputs)
    memory_pair = exchange(memory)
    cotangent_pair = exchange(cotangent)
    blocks = gather_plane(
        jnp.concatenate([input_pair[0], memory_pair[0]], axis=0),
        jnp.concatenate([input_pair[1], memory_pair[1]], axis=0),
    )
    rows_in = jnp.concatenate(input_pair, axis=0)
    wide_rows = jnp.concatenate([p[:own_rows] for b in blocks for p in b], axis=0)
    wide_memory = jnp.concatenate([p[own_rows:] for b in blocks for p in b], axis=0)

    slots = lax.dynamic_index_in_dim(positions, core, 0, keepdims=False)
    length = lax.dynamic_index_in_dim(lengths, core, 0, keepdims=False)
    memory_length = lax.dynamic_index_in_dim(memory_lengths, core, 0, keepdims=False)
    key_positions = []
    memory_slots = []
    for dx, dy in offsets():
        at_y = (y - dy + high) % high
        at_x = (x - dx + wide) % wide
        for who in (core, 1 - core):
            block = (at_y * wide + at_x) * 2 + who
            key_positions.append(lax.dynamic_slice_in_dim(slots, block * own_rows, own_rows))
            memory_slots.append(block * own_memory + jnp.arange(own_memory, dtype=jnp.int32))
    own_positions = jnp.concatenate(key_positions[:2])
    key_positions = jnp.concatenate(key_positions)
    last = positions.shape[1]
    key_positions = jnp.where(key_positions < length, key_positions, last)[:, None]
    query_positions = own_positions[None, :]
    memory_slots = jnp.concatenate(memory_slots)[:, None]
    memory_limit = jnp.broadcast_to(memory_length - 1, (1, rows))

    first_widths = [head_width] * 3
    second_widths = [head_width] * 5
    third_widths = [hidden_width] * 2
    full_query, full_key, full_value = gather_weights(
        jnp.concatenate([query_weight, key_weight, value_weight], axis=1), first_widths
    )
    full_cross_key, full_cross_value, full_output, full_cross_query, full_cross_output = (
        gather_weights(
            jnp.concatenate(
                [
                    cross_key_weight,
                    cross_value_weight,
                    output_weight.T,
                    cross_query_weight,
                    cross_output_weight.T,
                ],
                axis=1,
            ),
            second_widths,
        )
    )
    full_expand, full_reduce = gather_weights(
        jnp.concatenate([expand_weight, reduce_weight.T], axis=1), third_widths
    )

    query_low = (product(rows_in, full_query) + query_bias).astype(BF16)
    keys = product(wide_rows, full_key).astype(BF16)
    values = (product(wide_rows, full_value) + value_bias).astype(BF16)
    attended, weights, inverse = attend(query_low, keys, values, query_positions, key_positions)
    memory_key = product(wide_memory, full_cross_key).astype(BF16)
    memory_value = (product(wide_memory, full_cross_value) + cross_value_bias).astype(BF16)

    first_in = rows_in.astype(F32) + product_right(attended, full_output) + output_bias
    first_out = layer_norm(first_in, first_gain, first_shift)
    first_low = first_out.astype(BF16)
    cross_query = (product(first_low, full_cross_query) + cross_query_bias).astype(BF16)
    cross_attended, cross_weights, cross_inverse = attend(
        cross_query, memory_key, memory_value, memory_limit, memory_slots
    )
    second_in = first_out + product_right(cross_attended, full_cross_output) + cross_output_bias
    second_out = layer_norm(second_in, second_gain, second_shift)
    second_low = second_out.astype(BF16)
    expanded = product(second_low, full_expand) + expand_bias
    gate = jax.nn.sigmoid(expanded)
    activated = (expanded * gate).astype(BF16)
    third_in = second_out + product_right(activated, full_reduce) + reduce_bias
    outputs = layer_norm(third_in, third_gain, third_shift)

    grad_in = jnp.concatenate(cotangent_pair, axis=0).astype(F32)
    masked_grad = jnp.where((own_positions < length)[:, None], grad_in, 0.0)
    third_grad, third_gain_part, third_shift_part = norm_back(third_in, third_gain, masked_grad)
    third_low = third_grad.astype(BF16)
    activated_grad = product(third_low, full_reduce)
    expanded_grad = (activated_grad * gate * (1.0 + expanded * (1.0 - gate))).astype(BF16)
    third_part = [
        product_left(second_low, expanded_grad).astype(BF16),
        product_left(third_low, activated).astype(BF16),
    ]
    third_shard = scatter_weights(third_part, third_widths)

    second_grad = third_grad + product_right(expanded_grad, full_expand)
    second_in_grad, second_gain_part, second_shift_part = norm_back(
        second_in, second_gain, second_grad
    )
    second_grad_low = second_in_grad.astype(BF16)
    cross_attended_grad = product(second_grad_low, full_cross_output).astype(BF16)
    cross_query_grad, memory_key_grad, memory_value_grad = attend_back(
        cross_query,
        memory_key,
        memory_value,
        cross_weights,
        cross_inverse,
        cross_attended,
        cross_attended_grad,
    )
    first_grad = second_in_grad + product_right(cross_query_grad, full_cross_query)
    first_in_grad, first_gain_part, first_shift_part = norm_back(first_in, first_gain, first_grad)
    first_grad_low = first_in_grad.astype(BF16)
    attended_grad = product(first_grad_low, full_output).astype(BF16)
    second_part = [
        product_left(wide_memory, memory_key_grad).astype(BF16),
        product_left(wide_memory, memory_value_grad).astype(BF16),
        product_left(first_grad_low, attended).astype(BF16),
        product_left(first_low, cross_query_grad).astype(BF16),
        product_left(second_grad_low, cross_attended).astype(BF16),
    ]
    second_shard = scatter_weights(second_part, second_widths)
    memory_part = product_right(memory_key_grad, full_cross_key) + product_right(
        memory_value_grad, full_cross_value
    )

    query_grad, key_grad, value_grad = attend_back(
        query_low, keys, values, weights, inverse, attended, attended_grad
    )
    input_part = product_right(key_grad, full_key) + product_right(value_grad, full_value)
    input_own = first_in_grad + product_right(query_grad, full_query)
    first_part = [
        product_left(rows_in, query_grad).astype(BF16),
        product_left(wide_rows, key_grad).astype(BF16),
        product_left(wide_rows, value_grad).astype(BF16),
    ]
    first_shard = scatter_weights(first_part, first_widths)

    def halves(part, block_rows):
        return [
            tuple(
                part[(2 * n + h) * block_rows : (2 * n + h + 1) * block_rows] for h in range(2)
            )
            for n in range(len(offsets()))
        ]

    row_blocks = halves(input_part, own_rows)
    memory_blocks = halves(memory_part, own_memory)
    low_blocks = [
        tuple(jnp.concatenate([r, m], axis=0).astype(BF16) for r, m in zip(rb, mb))
        for rb, mb in zip(row_blocks, memory_blocks)
    ]
    left = scatter_plane(low_blocks)[1:]
    pair = [summed([part[h] for part in left]) for h in range(2)]
    input_pair = [
        input_own[h * own_rows : (h + 1) * own_rows] + row_blocks[0][h] + pair[h][:own_rows]
        for h in range(2)
    ]
    memory_pair = [memory_blocks[0][h] + pair[h][own_rows:] for h in range(2)]

    def restore(pair):
        other = swap(pair[1])
        return jnp.where(
            core == 0, jnp.stack([pair[0], other]), jnp.stack([other, pair[0]])
        )

    output_result = restore([outputs[:own_rows], outputs[own_rows:]])
    input_result = restore(input_pair)
    memory_result = restore(memory_pair)

    vectors = [
        jnp.sum(query_grad.astype(F32), axis=0),
        jnp.sum(value_grad.astype(F32), axis=0),
        jnp.sum(first_in_grad, axis=0),
        first_gain_part,
        first_shift_part,
        jnp.sum(cross_query_grad.astype(F32), axis=0),
        jnp.sum(memory_value_grad.astype(F32), axis=0),
        jnp.sum(second_in_grad, axis=0),
        second_gain_part,
        second_shift_part,
        jnp.sum(expanded_grad.astype(F32), axis=0),
        jnp.sum(third_grad, axis=0),
        third_gain_part,
        third_shift_part,
    ]
    joined = all_sum(jnp.concatenate(vectors))
    split = []
    start = 0
    for vector in vectors:
        split.append(joined[start : start + vector.shape[0]])
        start += vector.shape[0]

    def shards(packed, widths):
        start = 0
        parts = []
        for one in widths:
            parts.append(packed[:, start : start + one])
            start += one
        return parts

    g_query, g_key, g_value = shards(first_shard, first_widths)
    g_cross_key, g_cross_value, g_output, g_cross_query, g_cross_output = shards(
        second_shard, second_widths
    )
    g_expand, g_reduce = shards(third_shard, third_widths)
    return (
        output_result,
        input_result,
        memory_result,
        g_query,
        g_key,
        g_value,
        g_output.T,
        g_cross_query,
        g_cross_key,
        g_cross_value,
        g_cross_output.T,
        g_expand,
        g_reduce.T,
        *split,
    )


def solution(mesh):
    rows = P("fsdp", ("ctx", "tp"), None)
    tall = P(("fsdp", "ctx"), "tp")
    flat = P("tp", ("fsdp", "ctx"))
    weights = (tall, tall, tall, flat, tall, tall, tall, flat, tall, flat)
    return jax.shard_map(
        per_device,
        mesh=mesh,
        in_specs=(rows, rows, rows, P("fsdp", None), P("fsdp"), P("fsdp"))
        + weights
        + (P(),) * 14,
        out_specs=(rows, rows, rows) + weights + (P(),) * 14,
        check_vma=False,
    )
```

```python
import functools

import jax
import jax.numpy as jnp
from jax import lax
from jax.experimental import pallas as pl
from jax.experimental.pallas import tpu as pltpu
from jax.sharding import PartitionSpec as P

HEAD_DIM = 64
EPSILON = 1e-05
NEGATIVE = -1e30
F32 = jnp.float32
BF16 = jnp.bfloat16
SCALE = HEAD_DIM ** -0.5
VMEM_BYTES = 58 * 2 ** 20


def contract(left, right, left_dim, right_dim):
    return lax.dot_general(
        left, right, (((left_dim,), (right_dim,)), ((), ())), preferred_element_type=F32
    )


def product(left, right):
    return contract(left, right, 1, 0)


def product_left(left, right):
    return contract(left, right, 0, 0)


def product_right(left, right):
    return contract(left, right, 1, 1)


def layer_norm(values, gain, shift):
    center = values - jnp.mean(values, axis=-1, keepdims=True)
    spread = jnp.mean(center * center, axis=-1, keepdims=True)
    return center * lax.rsqrt(spread + EPSILON) * gain + shift


def norm_back(values, gain, grad):
    center = values - jnp.mean(values, axis=-1, keepdims=True)
    spread = jnp.mean(center * center, axis=-1, keepdims=True)
    rate = lax.rsqrt(spread + EPSILON)
    normal = center * rate
    scaled = grad * gain
    back = rate * (
        scaled
        - jnp.mean(scaled, axis=-1, keepdims=True)
        - normal * jnp.mean(scaled * normal, axis=-1, keepdims=True)
    )
    return back, jnp.sum(grad * normal, axis=0), jnp.sum(grad, axis=0)


def attend_kernel(heads, q, k, v, qp, kp, out, weights, inverse):
    allowed = kp[...] <= qp[...]
    for head in range(heads):
        cols = slice(head * HEAD_DIM, (head + 1) * HEAD_DIM)
        scores = contract(k[:, cols], q[:, cols] * SCALE, 1, 1)
        scores = jnp.where(allowed, scores, NEGATIVE)
        largest = jnp.max(scores, axis=0, keepdims=True)
        power = jnp.exp(scores - largest)
        rate = 1.0 / jnp.sum(power, axis=0, keepdims=True)
        low = power.astype(BF16)
        weights[head] = low
        inverse[head] = rate
        out[:, cols] = (contract(v[:, cols], low, 0, 0) * rate).T.astype(BF16)


def attend_back_kernel(heads, q, k, v, weights, inverse, out, grad, dq, dk, dv):
    for head in range(heads):
        cols = slice(head * HEAD_DIM, (head + 1) * HEAD_DIM)
        grads = grad[:, cols].astype(F32).T
        outs = out[:, cols].astype(F32).T
        inner = jnp.sum(grads * outs, axis=0, keepdims=True) * inverse[head]
        scaled = (grads * inverse[head]).astype(BF16)
        weight = weights[head]
        grad_weight = contract(v[:, cols], scaled, 1, 0)
        grad_scores = (weight.astype(F32) * (grad_weight - inner)).astype(BF16)
        dq[:, cols] = (contract(k[:, cols], grad_scores, 0, 0) * SCALE).T.astype(BF16)
        dv[:, cols] = contract(weight, scaled, 1, 1).astype(BF16)
        dk[:, cols] = (contract(grad_scores, q[:, cols], 1, 0) * SCALE).astype(BF16)


HEADS_PER_STEP = 2


def column_block(rows):
    return pl.BlockSpec((rows, HEADS_PER_STEP * HEAD_DIM), lambda i: (0, i))


def head_block(*dims):
    return pl.BlockSpec((HEADS_PER_STEP,) + dims, lambda i: (i, 0, 0))


def attend(q, k, v, qp, kp):
    rows, width = q.shape
    keys = k.shape[0]
    heads = width // HEAD_DIM
    return pl.pallas_call(
        functools.partial(attend_kernel, HEADS_PER_STEP),
        grid=(heads // HEADS_PER_STEP,),
        in_specs=[
            column_block(rows),
            column_block(keys),
            column_block(keys),
            pl.BlockSpec((1, rows), lambda i: (0, 0)),
            pl.BlockSpec((keys, 1), lambda i: (0, 0)),
        ],
        out_specs=[column_block(rows), head_block(keys, rows), head_block(1, rows)],
        out_shape=[
            jax.ShapeDtypeStruct((rows, width), BF16),
            jax.ShapeDtypeStruct((heads, keys, rows), BF16),
            jax.ShapeDtypeStruct((heads, 1, rows), F32),
        ],
        compiler_params=pltpu.CompilerParams(vmem_limit_bytes=VMEM_BYTES),
        cost_estimate=pl.CostEstimate(
            flops=4 * rows * keys * width * 4,
            transcendentals=heads * rows * keys,
            bytes_accessed=2 * heads * rows * keys,
        ),
        name="attend",
    )(q, k, v, qp, kp)


def attend_back(q, k, v, weights, inverse, out, grad):
    rows, width = q.shape
    keys = k.shape[0]
    heads = width // HEAD_DIM
    return pl.pallas_call(
        functools.partial(attend_back_kernel, HEADS_PER_STEP),
        grid=(heads // HEADS_PER_STEP,),
        in_specs=[
            column_block(rows),
            column_block(keys),
            column_block(keys),
            head_block(keys, rows),
            head_block(1, rows),
            column_block(rows),
            column_block(rows),
        ],
        out_specs=[column_block(rows), column_block(keys), column_block(keys)],
        out_shape=[
            jax.ShapeDtypeStruct((rows, width), BF16),
            jax.ShapeDtypeStruct((keys, width), BF16),
            jax.ShapeDtypeStruct((keys, width), BF16),
        ],
        compiler_params=pltpu.CompilerParams(vmem_limit_bytes=VMEM_BYTES),
        cost_estimate=pl.CostEstimate(
            flops=8 * rows * keys * width * 4,
            transcendentals=0,
            bytes_accessed=2 * heads * rows * keys,
        ),
        name="attend_back",
    )(q, k, v, weights, inverse, out, grad)


def move(sources, shapes, plan, name):
    def body(*refs):
        given = refs[: len(sources)]
        made = refs[len(sources) : len(sources) + len(shapes)]
        sems = refs[-1]
        copies = []
        for at, (i, a, j, b) in enumerate(plan()):
            copies.append(pltpu.make_async_copy(given[i].at[a], made[j].at[b], sems.at[at]))
        for copy in copies:
            copy.start()
        for copy in copies:
            copy.wait()

    count = move_count(plan)
    return pl.pallas_call(
        body,
        in_specs=[pl.BlockSpec(memory_space=pl.ANY)] * len(sources),
        out_specs=[pl.BlockSpec(memory_space=pltpu.VMEM)] * len(shapes),
        out_shape=[jax.ShapeDtypeStruct(shape, BF16) for shape in shapes],
        scratch_shapes=[pltpu.SemaphoreType.DMA((count,))],
        compiler_params=pltpu.CompilerParams(vmem_limit_bytes=VMEM_BYTES),
        name=name,
    )(*sources)


def move_count(plan):
    return len(plan())


def sizes():
    return lax.axis_size("fsdp"), lax.axis_size("ctx"), lax.axis_size("tp") // 2


def places():
    tp = lax.axis_index("tp")
    return lax.axis_index("fsdp"), lax.axis_index("ctx"), tp // 2, tp % 2


def swap(value):
    total = lax.axis_size("tp")
    return lax.ppermute(value, "tp", [(i, i ^ 1) for i in range(total)])


def shift_x(value, step):
    total = lax.axis_size("tp")
    return lax.ppermute(value, "tp", [(i, (i + 2 * step) % total) for i in range(total)])


def shift(value, axis, step):
    total = lax.axis_size(axis)
    return lax.ppermute(value, axis, [(i, (i + step) % total) for i in range(total)])


def offsets():
    unused, high, wide = sizes()
    return [(dx, dy) for dy in range(high) for dx in range(wide)]


def is_square():
    unused, high, wide = sizes()
    return high == 2 and wide == 2


def gather_plane(first, second):
    if is_square():
        side = (shift_x(first, 1), shift_x(second, 1))
        front = (shift(first, "ctx", 1), shift(second, "ctx", 1))
        far = (shift(side[0], "ctx", 1), shift_x(front[1], 1))
        return [(first, second), side, front, far]
    unused, high, wide = sizes()
    row = [(first, second)] + [(shift_x(first, k), shift_x(second, k)) for k in range(1, wide)]
    blocks = list(row)
    for step in range(1, high):
        blocks += [(shift(a, "ctx", step), shift(b, "ctx", step)) for a, b in row]
    return blocks


def add(left, right):
    return (left.astype(F32) + right.astype(F32)).astype(BF16)


def scatter_plane(blocks):
    if is_square():
        own, side, front, far = blocks
        side_first = add(side[0], shift(far[0], "ctx", 1))
        front_second = add(front[1], shift_x(far[1], 1))
        from_side = (shift_x(side_first, 1), shift_x(side[1], 1))
        from_front = (shift(front[0], "ctx", 1), shift(front_second, "ctx", 1))
        return [own, from_side, from_front]
    unused, high, wide = sizes()
    row = []
    for dx in range(wide):
        total = blocks[dx]
        for dy in range(1, high):
            other = blocks[dy * wide + dx]
            total = tuple(add(a, shift(b, "ctx", -dy)) for a, b in zip(total, other))
        row.append(total)
    return [row[0]] + [
        (shift_x(row[dx][0], -dx), shift_x(row[dx][1], -dx)) for dx in range(1, wide)
    ]


def summed(parts):
    return sum(part.astype(F32) for part in parts)


def gather_weights(packed, widths):
    deep, high, wide = sizes()
    rows, total = packed.shape
    half = deep // 2
    pieces = [packed] + [shift(packed, "fsdp", k) for k in range(1, deep)]

    def by_depth():
        at = lax.axis_index("fsdp")
        return [(k, slice(None), 0, (at - k + deep) % deep) for k in range(deep)]

    stacked = move(pieces, [(deep, rows, total)], by_depth, "stack_depth")[0]
    blocks = gather_plane(stacked[:half], stacked[half:])
    order = offsets()

    def side_by_side():
        steps = []
        for n in range(len(order)):
            steps.append((2 * n, slice(None), 0, (n, slice(0, half))))
            steps.append((2 * n + 1, slice(None), 0, (n, slice(half, deep))))
        return steps

    own = move(
        [part for block in blocks for part in block],
        [(len(order), deep, rows, total)],
        side_by_side,
        "stack_plane",
    )[0]
    other = swap(own)
    starts = [sum(widths[:i]) for i in range(len(widths))]
    if all(width % 128 == 0 for width in widths):

        def into_place():
            unused, y, x, core = places()
            steps = []
            for n, (dx, dy) in enumerate(order):
                at_y = (y - dy + high) % high
                at_x = (x - dx + wide) % wide
                for who in range(2):
                    at = 2 * at_x + (core if who == 0 else 1 - core)
                    for j, width in enumerate(widths):
                        cols = slice(starts[j], starts[j] + width)
                        here = pl.ds(pl.multiple_of(at * width, 128), width)
                        steps.append(
                            (
                                who,
                                (n, slice(None), slice(None), cols),
                                j,
                                (slice(None), at_y, slice(None), here),
                            )
                        )
            return steps

        made = move(
            [own, other],
            [(deep, high, rows, 2 * wide * width) for width in widths],
            into_place,
            "place_weights",
        )
        return [m.reshape(deep * high * rows, -1) for m in made]
    unused, y, x, core = places()
    whole = jnp.zeros((high, wide, 2, deep, rows, total), BF16)
    for n, (dx, dy) in enumerate(order):
        for who, part in ((core, own), (1 - core, other)):
            at = ((y - dy + high) % high, (x - dx + wide) % wide, who, 0, 0, 0)
            whole = lax.dynamic_update_slice(whole, part[n][None, None, None], at)
    made = []
    for start, width in zip(starts, widths):
        part = whole[..., start : start + width]
        part = part.transpose(3, 0, 4, 1, 2, 5)
        made.append(part.reshape(deep * high * rows, 2 * wide * width))
    return made


def scatter_weights(grads, widths):
    deep, high, wide = sizes()
    rows = grads[0].shape[0] // (deep * high)
    total = sum(widths)
    half = deep // 2
    order = offsets()
    starts = [sum(widths[:i]) for i in range(len(widths))]
    shaped = [g.reshape(deep, high, rows, 2 * wide * w) for g, w in zip(grads, widths)]
    if all(width % 128 == 0 for width in widths):

        def into_blocks():
            unused, y, x, core = places()
            steps = []
            for n, (dx, dy) in enumerate(order):
                at_y = (y - dy + high) % high
                at_x = (x - dx + wide) % wide
                for who in range(2):
                    at = 2 * at_x + (core if who == 0 else 1 - core)
                    for j, width in enumerate(widths):
                        cols = slice(starts[j], starts[j] + width)
                        here = pl.ds(pl.multiple_of(at * width, 128), width)
                        steps.append(
                            (
                                j,
                                (slice(None), at_y, slice(None), here),
                                who,
                                (n, slice(None), slice(None), cols),
                            )
                        )
            return steps

        keep, send = move(
            shaped, [(len(order), deep, rows, total)] * 2, into_blocks, "split_weights"
        )
    else:
        unused, y, x, core = places()
        whole = jnp.concatenate(
            [g.reshape(deep, high, rows, wide, 2, w) for g, w in zip(shaped, widths)], axis=-1
        ).transpose(1, 3, 4, 0, 2, 5)
        size = (1, 1, 1, deep, rows, total)

        def pick(dx, dy, who):
            at = ((y - dy + high) % high, (x - dx + wide) % wide, who, 0, 0, 0)
            return lax.dynamic_slice(whole, at, size).reshape(size[3:])

        keep = jnp.stack([pick(dx, dy, core) for dx, dy in order])
        send = jnp.stack([pick(dx, dy, 1 - core) for dx, dy in order])
    other = swap(send)
    blocks = [
        (add(keep[n, :half], other[n, :half]), add(keep[n, half:], other[n, half:]))
        for n in range(len(order))
    ]
    left = scatter_plane(blocks)
    own = jnp.concatenate([summed([part[h] for part in left]) for h in range(2)], axis=0)
    low = own.astype(BF16)
    at = lax.axis_index("fsdp")
    result = lax.dynamic_index_in_dim(own, at, 0, keepdims=False)
    for k in range(1, deep):
        piece = lax.dynamic_index_in_dim(low, (at + k) % deep, 0, keepdims=False)
        result = result + shift(piece, "fsdp", k).astype(F32)
    return result


def all_sum(value):
    for axis in ("tp", "ctx", "fsdp"):
        total = lax.axis_size(axis)
        step = 1
        while step < total:
            pairs = [(i, i ^ step) for i in range(total)]
            value = value + lax.ppermute(value, axis, pairs)
            step *= 2
    return value


def per_device(
    inputs,
    memory,
    cotangent,
    positions,
    lengths,
    memory_lengths,
    query_weight,
    key_weight,
    value_weight,
    output_weight,
    cross_query_weight,
    cross_key_weight,
    cross_value_weight,
    cross_output_weight,
    expand_weight,
    reduce_weight,
    query_bias,
    value_bias,
    output_bias,
    first_gain,
    first_shift,
    cross_query_bias,
    cross_value_bias,
    cross_output_bias,
    second_gain,
    second_shift,
    expand_bias,
    reduce_bias,
    third_gain,
    third_shift,
):
    deep, high, wide = sizes()
    z, y, x, core = places()
    own_rows, width = inputs.shape[1:]
    own_memory = memory.shape[1]
    rows = 2 * own_rows
    head_width = query_weight.shape[1]
    hidden_width = expand_weight.shape[1]

    def exchange(value):
        keep = lax.dynamic_index_in_dim(value, core, 0, keepdims=False)
        give = lax.dynamic_index_in_dim(value, 1 - core, 0, keepdims=False)
        return keep, swap(give)

    input_pair = exchange(inputs)
    memory_pair = exchange(memory)
    cotangent_pair = exchange(cotangent)
    blocks = gather_plane(
        jnp.concatenate([input_pair[0], memory_pair[0]], axis=0),
        jnp.concatenate([input_pair[1], memory_pair[1]], axis=0),
    )
    rows_in = jnp.concatenate(input_pair, axis=0)
    wide_rows = jnp.concatenate([p[:own_rows] for b in blocks for p in b], axis=0)
    wide_memory = jnp.concatenate([p[own_rows:] for b in blocks for p in b], axis=0)

    slots = lax.dynamic_index_in_dim(positions, core, 0, keepdims=False)
    length = lax.dynamic_index_in_dim(lengths, core, 0, keepdims=False)
    memory_length = lax.dynamic_index_in_dim(memory_lengths, core, 0, keepdims=False)
    key_positions = []
    memory_slots = []
    for dx, dy in offsets():
        at_y = (y - dy + high) % high
        at_x = (x - dx + wide) % wide
        for who in (core, 1 - core):
            block = (at_y * wide + at_x) * 2 + who
            key_positions.append(lax.dynamic_slice_in_dim(slots, block * own_rows, own_rows))
            memory_slots.append(block * own_memory + jnp.arange(own_memory, dtype=jnp.int32))
    own_positions = jnp.concatenate(key_positions[:2])
    key_positions = jnp.concatenate(key_positions)
    last = positions.shape[1]
    key_positions = jnp.where(key_positions < length, key_positions, last)[:, None]
    query_positions = own_positions[None, :]
    memory_slots = jnp.concatenate(memory_slots)[:, None]
    memory_limit = jnp.broadcast_to(memory_length - 1, (1, rows))

    first_widths = [head_width] * 3
    second_widths = [head_width] * 5
    third_widths = [hidden_width] * 2
    full_query, full_key, full_value = gather_weights(
        jnp.concatenate([query_weight, key_weight, value_weight], axis=1), first_widths
    )
    full_cross_key, full_cross_value, full_output, full_cross_query, full_cross_output = (
        gather_weights(
            jnp.concatenate(
                [
                    cross_key_weight,
                    cross_value_weight,
                    output_weight.T,
                    cross_query_weight,
                    cross_output_weight.T,
                ],
                axis=1,
            ),
            second_widths,
        )
    )
    full_expand, full_reduce = gather_weights(
        jnp.concatenate([expand_weight, reduce_weight.T], axis=1), third_widths
    )

    query_low = (product(rows_in, full_query) + query_bias).astype(BF16)
    keys = product(wide_rows, full_key).astype(BF16)
    values = (product(wide_rows, full_value) + value_bias).astype(BF16)
    attended, weights, inverse = attend(query_low, keys, values, query_positions, key_positions)
    memory_key = product(wide_memory, full_cross_key).astype(BF16)
    memory_value = (product(wide_memory, full_cross_value) + cross_value_bias).astype(BF16)

    first_in = rows_in.astype(F32) + product_right(attended, full_output) + output_bias
    first_out = layer_norm(first_in, first_gain, first_shift)
    first_low = first_out.astype(BF16)
    cross_query = (product(first_low, full_cross_query) + cross_query_bias).astype(BF16)
    cross_attended, cross_weights, cross_inverse = attend(
        cross_query, memory_key, memory_value, memory_limit, memory_slots
    )
    second_in = first_out + product_right(cross_attended, full_cross_output) + cross_output_bias
    second_out = layer_norm(second_in, second_gain, second_shift)
    second_low = second_out.astype(BF16)
    expanded = product(second_low, full_expand) + expand_bias
    gate = jax.nn.sigmoid(expanded)
    activated = (expanded * gate).astype(BF16)
    third_in = second_out + product_right(activated, full_reduce) + reduce_bias
    outputs = layer_norm(third_in, third_gain, third_shift)

    grad_in = jnp.concatenate(cotangent_pair, axis=0).astype(F32)
    masked_grad = jnp.where((own_positions < length)[:, None], grad_in, 0.0)
    third_grad, third_gain_part, third_shift_part = norm_back(third_in, third_gain, masked_grad)
    third_low = third_grad.astype(BF16)
    activated_grad = product(third_low, full_reduce)
    expanded_grad = (activated_grad * gate * (1.0 + expanded * (1.0 - gate))).astype(BF16)
    third_part = [
        product_left(second_low, expanded_grad).astype(BF16),
        product_left(third_low, activated).astype(BF16),
    ]
    third_shard = scatter_weights(third_part, third_widths)

    second_grad = third_grad + product_right(expanded_grad, full_expand)
    second_in_grad, second_gain_part, second_shift_part = norm_back(
        second_in, second_gain, second_grad
    )
    second_grad_low = second_in_grad.astype(BF16)
    cross_attended_grad = product(second_grad_low, full_cross_output).astype(BF16)
    cross_query_grad, memory_key_grad, memory_value_grad = attend_back(
        cross_query,
        memory_key,
        memory_value,
        cross_weights,
        cross_inverse,
        cross_attended,
        cross_attended_grad,
    )
    first_grad = second_in_grad + product_right(cross_query_grad, full_cross_query)
    first_in_grad, first_gain_part, first_shift_part = norm_back(first_in, first_gain, first_grad)
    first_grad_low = first_in_grad.astype(BF16)
    attended_grad = product(first_grad_low, full_output).astype(BF16)
    second_part = [
        product_left(wide_memory, memory_key_grad).astype(BF16),
        product_left(wide_memory, memory_value_grad).astype(BF16),
        product_left(first_grad_low, attended).astype(BF16),
        product_left(first_low, cross_query_grad).astype(BF16),
        product_left(second_grad_low, cross_attended).astype(BF16),
    ]
    second_shard = scatter_weights(second_part, second_widths)
    memory_part = product_right(memory_key_grad, full_cross_key) + product_right(
        memory_value_grad, full_cross_value
    )

    query_grad, key_grad, value_grad = attend_back(
        query_low, keys, values, weights, inverse, attended, attended_grad
    )
    input_part = product_right(key_grad, full_key) + product_right(value_grad, full_value)
    input_own = first_in_grad + product_right(query_grad, full_query)
    first_part = [
        product_left(rows_in, query_grad).astype(BF16),
        product_left(wide_rows, key_grad).astype(BF16),
        product_left(wide_rows, value_grad).astype(BF16),
    ]
    first_shard = scatter_weights(first_part, first_widths)

    def halves(part, block_rows):
        return [
            tuple(
                part[(2 * n + h) * block_rows : (2 * n + h + 1) * block_rows] for h in range(2)
            )
            for n in range(len(offsets()))
        ]

    row_blocks = halves(input_part, own_rows)
    memory_blocks = halves(memory_part, own_memory)
    low_blocks = [
        tuple(jnp.concatenate([r, m], axis=0).astype(BF16) for r, m in zip(rb, mb))
        for rb, mb in zip(row_blocks, memory_blocks)
    ]
    left = scatter_plane(low_blocks)[1:]
    pair = [summed([part[h] for part in left]) for h in range(2)]
    input_pair = [
        input_own[h * own_rows : (h + 1) * own_rows] + row_blocks[0][h] + pair[h][:own_rows]
        for h in range(2)
    ]
    memory_pair = [memory_blocks[0][h] + pair[h][own_rows:] for h in range(2)]

    def restore(pair):
        other = swap(pair[1])
        return jnp.where(
            core == 0, jnp.stack([pair[0], other]), jnp.stack([other, pair[0]])
        )

    output_result = restore([outputs[:own_rows], outputs[own_rows:]])
    input_result = restore(input_pair)
    memory_result = restore(memory_pair)

    vectors = [
        jnp.sum(query_grad.astype(F32), axis=0),
        jnp.sum(value_grad.astype(F32), axis=0),
        jnp.sum(first_in_grad, axis=0),
        first_gain_part,
        first_shift_part,
        jnp.sum(cross_query_grad.astype(F32), axis=0),
        jnp.sum(memory_value_grad.astype(F32), axis=0),
        jnp.sum(second_in_grad, axis=0),
        second_gain_part,
        second_shift_part,
        jnp.sum(expanded_grad.astype(F32), axis=0),
        jnp.sum(third_grad, axis=0),
        third_gain_part,
        third_shift_part,
    ]
    joined = all_sum(jnp.concatenate(vectors))
    split = []
    start = 0
    for vector in vectors:
        split.append(joined[start : start + vector.shape[0]])
        start += vector.shape[0]

    def shards(packed, widths):
        start = 0
        parts = []
        for one in widths:
            parts.append(packed[:, start : start + one])
            start += one
        return parts

    g_query, g_key, g_value = shards(first_shard, first_widths)
    g_cross_key, g_cross_value, g_output, g_cross_query, g_cross_output = shards(
        second_shard, second_widths
    )
    g_expand, g_reduce = shards(third_shard, third_widths)
    return (
        output_result,
        input_result,
        memory_result,
        g_query,
        g_key,
        g_value,
        g_output.T,
        g_cross_query,
        g_cross_key,
        g_cross_value,
        g_cross_output.T,
        g_expand,
        g_reduce.T,
        *split,
    )


def solution(mesh):
    rows = P("fsdp", ("ctx", "tp"), None)
    tall = P(("fsdp", "ctx"), "tp")
    flat = P("tp", ("fsdp", "ctx"))
    weights = (tall, tall, tall, flat, tall, tall, tall, flat, tall, flat)
    return jax.shard_map(
        per_device,
        mesh=mesh,
        in_specs=(rows, rows, rows, P("fsdp", None), P("fsdp"), P("fsdp"))
        + weights
        + (P(),) * 14,
        out_specs=(rows, rows, rows) + weights + (P(),) * 14,
        check_vma=False,
    )
```

```python
import functools

import jax
import jax.numpy as jnp
from jax import lax
from jax.experimental import pallas as pl
from jax.experimental.pallas import tpu as pltpu
from jax.sharding import PartitionSpec as P

HEAD_DIM = 64
EPSILON = 1e-05
NEGATIVE = -1e30
F32 = jnp.float32
BF16 = jnp.bfloat16
SCALE = HEAD_DIM ** -0.5
VMEM_BYTES = 58 * 2 ** 20


def contract(left, right, left_dim, right_dim):
    return lax.dot_general(
        left, right, (((left_dim,), (right_dim,)), ((), ())), preferred_element_type=F32
    )


def product(left, right):
    return contract(left, right, 1, 0)


def product_left(left, right):
    return contract(left, right, 0, 0)


def product_right(left, right):
    return contract(left, right, 1, 1)


def layer_norm(values, gain, shift):
    center = values - jnp.mean(values, axis=-1, keepdims=True)
    spread = jnp.mean(center * center, axis=-1, keepdims=True)
    return center * lax.rsqrt(spread + EPSILON) * gain + shift


def norm_back(values, gain, grad):
    center = values - jnp.mean(values, axis=-1, keepdims=True)
    spread = jnp.mean(center * center, axis=-1, keepdims=True)
    rate = lax.rsqrt(spread + EPSILON)
    normal = center * rate
    scaled = grad * gain
    back = rate * (
        scaled
        - jnp.mean(scaled, axis=-1, keepdims=True)
        - normal * jnp.mean(scaled * normal, axis=-1, keepdims=True)
    )
    return back, jnp.sum(grad * normal, axis=0), jnp.sum(grad, axis=0)


def attend_kernel(heads, q, k, v, qp, kp, *refs):
    out, exact, weights, inverse = refs[-4:]
    allowed = kp[...] <= qp[...]
    for head in range(heads):
        cols = slice(head * HEAD_DIM, (head + 1) * HEAD_DIM)
        scores = contract(k[:, cols], q[:, cols] * SCALE, 1, 1)
        scores = jnp.where(allowed, scores, NEGATIVE)
        largest = jnp.max(scores, axis=0, keepdims=True)
        power = jnp.exp(scores - largest)
        rate = 1.0 / jnp.sum(power, axis=0, keepdims=True)
        low = power.astype(BF16)
        weights[head] = low
        inverse[head] = rate
        mixed = contract(v[:, cols], low, 0, 0) * rate
        exact[cols, :] = mixed
        out[:, cols] = mixed.T.astype(BF16)


def attend_back_kernel(heads, q, k, v, weights, inverse, exact, grad, *refs):
    dq, dk, dv = refs[-3:]
    for head in range(heads):
        cols = slice(head * HEAD_DIM, (head + 1) * HEAD_DIM)
        grads = grad[:, cols].astype(F32).T
        inner = jnp.sum(grads * exact[cols, :], axis=0, keepdims=True) * inverse[head]
        scaled = (grads * inverse[head]).astype(BF16)
        weight = weights[head]
        grad_weight = contract(v[:, cols], scaled, 1, 0)
        grad_scores = (weight.astype(F32) * (grad_weight - inner)).astype(BF16)
        dq[:, cols] = (contract(k[:, cols], grad_scores, 0, 0) * SCALE).T.astype(BF16)
        dv[:, cols] = contract(weight, scaled, 1, 1).astype(BF16)
        dk[:, cols] = (contract(grad_scores, q[:, cols], 1, 0) * SCALE).astype(BF16)


HEADS_PER_STEP = 2


def attend_call(body, arrays, specs, shapes, out_specs, earlier, steps, cost, name):
    given = [] if earlier is None else list(earlier)
    return pl.pallas_call(
        functools.partial(body, HEADS_PER_STEP),
        grid=(steps,),
        in_specs=specs + [pl.BlockSpec(memory_space=pl.ANY)] * len(given),
        out_specs=out_specs,
        out_shape=shapes,
        input_output_aliases={len(arrays) + i: i for i in range(len(given))},
        compiler_params=pltpu.CompilerParams(vmem_limit_bytes=VMEM_BYTES),
        cost_estimate=cost,
        name=name,
    )(*arrays, *given)


def head_specs(first):
    def columns(rows):
        return pl.BlockSpec((rows, HEADS_PER_STEP * HEAD_DIM), lambda i: (0, i + first))

    def lines(rows):
        return pl.BlockSpec((HEADS_PER_STEP * HEAD_DIM, rows), lambda i: (i + first, 0))

    def heads(*dims):
        return pl.BlockSpec((HEADS_PER_STEP,) + dims, lambda i: (i + first, 0, 0))

    return columns, lines, heads


def attend(q, k, v, qp, kp, part=0, parts=1, earlier=None):
    rows, width = q.shape
    keys = k.shape[0]
    heads = width // HEAD_DIM
    steps = heads // HEADS_PER_STEP // parts
    columns, lines, by_head = head_specs(part * steps)
    return attend_call(
        attend_kernel,
        (q, k, v, qp, kp),
        [
            columns(rows),
            columns(keys),
            columns(keys),
            pl.BlockSpec((1, rows), lambda i: (0, 0)),
            pl.BlockSpec((keys, 1), lambda i: (0, 0)),
        ],
        [
            jax.ShapeDtypeStruct((rows, width), BF16),
            jax.ShapeDtypeStruct((width, rows), F32),
            jax.ShapeDtypeStruct((heads, keys, rows), BF16),
            jax.ShapeDtypeStruct((heads, 1, rows), F32),
        ],
        [columns(rows), lines(rows), by_head(keys, rows), by_head(1, rows)],
        earlier,
        steps,
        pl.CostEstimate(
            flops=16 * rows * keys * width // parts,
            transcendentals=heads * rows * keys // parts,
            bytes_accessed=2 * heads * rows * keys // parts,
        ),
        "attend",
    )


def attend_back(q, k, v, weights, inverse, exact, grad, part=0, parts=1, earlier=None):
    rows, width = q.shape
    keys = k.shape[0]
    heads = width // HEAD_DIM
    steps = heads // HEADS_PER_STEP // parts
    columns, lines, by_head = head_specs(part * steps)
    return attend_call(
        attend_back_kernel,
        (q, k, v, weights, inverse, exact, grad),
        [
            columns(rows),
            columns(keys),
            columns(keys),
            by_head(keys, rows),
            by_head(1, rows),
            lines(rows),
            columns(rows),
        ],
        [
            jax.ShapeDtypeStruct((rows, width), BF16),
            jax.ShapeDtypeStruct((keys, width), BF16),
            jax.ShapeDtypeStruct((keys, width), BF16),
        ],
        [columns(rows), columns(keys), columns(keys)],
        earlier,
        steps,
        pl.CostEstimate(
            flops=32 * rows * keys * width // parts,
            transcendentals=0,
            bytes_accessed=2 * heads * rows * keys // parts,
        ),
        "attend_back",
    )


def move(sources, shapes, plan, name):
    def body(*refs):
        given = refs[: len(sources)]
        made = refs[len(sources) : len(sources) + len(shapes)]
        sems = refs[-1]
        copies = []
        for at, (i, a, j, b) in enumerate(plan()):
            copies.append(pltpu.make_async_copy(given[i].at[a], made[j].at[b], sems.at[at]))
        for copy in copies:
            copy.start()
        for copy in copies:
            copy.wait()

    count = move_count(plan)
    return pl.pallas_call(
        body,
        in_specs=[pl.BlockSpec(memory_space=pl.ANY)] * len(sources),
        out_specs=[pl.BlockSpec(memory_space=pltpu.VMEM)] * len(shapes),
        out_shape=[jax.ShapeDtypeStruct(shape, BF16) for shape in shapes],
        scratch_shapes=[pltpu.SemaphoreType.DMA((count,))],
        compiler_params=pltpu.CompilerParams(vmem_limit_bytes=VMEM_BYTES),
        name=name,
    )(*sources)


def move_count(plan):
    return len(plan())


def sizes():
    return lax.axis_size("fsdp"), lax.axis_size("ctx"), lax.axis_size("tp") // 2


def places():
    tp = lax.axis_index("tp")
    return lax.axis_index("fsdp"), lax.axis_index("ctx"), tp // 2, tp % 2


def swap(value):
    total = lax.axis_size("tp")
    return lax.ppermute(value, "tp", [(i, i ^ 1) for i in range(total)])


def shift_x(value, step):
    total = lax.axis_size("tp")
    return lax.ppermute(value, "tp", [(i, (i + 2 * step) % total) for i in range(total)])


def shift(value, axis, step):
    total = lax.axis_size(axis)
    return lax.ppermute(value, axis, [(i, (i + step) % total) for i in range(total)])


def offsets():
    unused, high, wide = sizes()
    return [(dx, dy) for dy in range(high) for dx in range(wide)]


def is_square():
    unused, high, wide = sizes()
    return high == 2 and wide == 2


def shift_plane(value, dx, dy):
    high, total = lax.axis_size("ctx"), lax.axis_size("tp")
    pairs = [
        (c * total + t, (c + dy) % high * total + (t + 2 * dx) % total)
        for c in range(high)
        for t in range(total)
    ]
    return lax.ppermute(value, ("ctx", "tp"), pairs)


def plane_direct(value):
    return [(value,)] + [(shift_plane(value, dx, dy),) for dx, dy in offsets()[1:]]


def sum_direct(blocks):
    moved = [(shift_plane(b[0], -dx, -dy),) for b, (dx, dy) in zip(blocks[1:], offsets()[1:])]
    return [blocks[0]] + moved


def plane_one(first, second):
    if is_square():
        side = (shift_x(first, 1), shift_x(second, 1))
        front = (shift(first, "ctx", 1), shift(second, "ctx", 1))
        return [(first, second), side, front]
    unused, high, wide = sizes()
    row = [(first, second)] + [(shift_x(first, k), shift_x(second, k)) for k in range(1, wide)]
    blocks = list(row)
    for step in range(1, high):
        blocks += [(shift(a, "ctx", step), shift(b, "ctx", step)) for a, b in row]
    return blocks


def plane_two(blocks):
    if is_square():
        own, side, front = blocks
        return [own, side, front, (shift(side[0], "ctx", 1), shift_x(front[1], 1))]
    return blocks


def add(left, right):
    return (left.astype(F32) + right.astype(F32)).astype(BF16)


def add_kernel(*refs):
    count = len(refs) // 3
    for n in range(count):
        total = refs[n][...].astype(F32) + refs[count + n][...].astype(F32)
        refs[2 * count + n][...] = total.astype(BF16)


def add_many(left, right):
    steps = left[0].shape[0]
    if sum(part.size for part in left) < 2**20:
        steps = 1

    def spec(part):
        rest = part.shape[1:]
        return pl.BlockSpec((part.shape[0] // steps,) + rest, lambda i: (i,) + (0,) * len(rest))

    return pl.pallas_call(
        add_kernel,
        grid=(steps,),
        in_specs=[spec(part) for part in left] * 2,
        out_specs=[spec(part) for part in left],
        out_shape=[jax.ShapeDtypeStruct(part.shape, BF16) for part in left],
        name="add_many",
    )(*left, *right)


def sum_one(blocks):
    if is_square():
        own, side, front, far = blocks
        return [own, side, front, (shift(far[0], "ctx", 1), shift_x(far[1], 1))]
    return blocks


def sum_adds(blocks):
    if is_square():
        own, side, front, far = blocks
        first, second = add_many([side[0], front[1]], [far[0], far[1]])
        return [own, (first, side[1]), (front[0], second)]
    return blocks


def sum_two(blocks):
    if is_square():
        own, side, front = blocks
        from_side = (shift_x(side[0], 1), shift_x(side[1], 1))
        from_front = (shift(front[0], "ctx", 1), shift(front[1], "ctx", 1))
        return [own, from_side, from_front]
    unused, high, wide = sizes()
    row = []
    for dx in range(wide):
        total = blocks[dx]
        for dy in range(1, high):
            other = blocks[dy * wide + dx]
            total = tuple(add(a, shift(b, "ctx", -dy)) for a, b in zip(total, other))
        row.append(total)
    return [row[0]] + [
        (shift_x(row[dx][0], -dx), shift_x(row[dx][1], -dx)) for dx in range(1, wide)
    ]


def summed(parts):
    return sum(part.astype(F32) for part in parts)


def spread(packed):
    return [packed] + [shift(packed, "fsdp", k) for k in range(1, lax.axis_size("fsdp"))]


def depth_blocks(pieces, cuts, name):
    deep = len(pieces)
    rows, total = pieces[0].shape
    half = rows // cuts

    def by_depth():
        at = lax.axis_index("fsdp")
        steps = []
        for k in range(deep):
            for h in range(cuts):
                steps.append((k, slice(h * half, (h + 1) * half), h, (at - k + deep) % deep))
        return steps

    return move(pieces, [(deep, half, total)] * cuts, by_depth, name)


def aligned(widths):
    return all(width % 128 == 0 for width in widths)


def column_starts(widths):
    return [sum(widths[:i]) for i in range(len(widths))]


def block_place(n, who):
    unused, high, wide = sizes()
    unused, y, x, core = places()
    dx, dy = offsets()[n]
    at_y = (y - dy + high) % high
    at_x = (x - dx + wide) % wide
    return at_y, 2 * at_x + (core if who == 0 else 1 - core)


def whole_weights(blocks, widths, name):
    deep, high, wide = sizes()
    half, total = blocks[0][0].shape[1:]
    cuts = len(blocks[0])
    rows = cuts * half
    others = [tuple(swap(part) for part in block) for block in blocks]
    starts = column_starts(widths)
    if aligned(widths):

        def into_place():
            steps = []
            for n in range(len(blocks)):
                for who in range(2):
                    at_y, at = block_place(n, who)
                    for h in range(cuts):
                        lines = slice(h * half, (h + 1) * half)
                        for j, width in enumerate(widths):
                            cols = slice(starts[j], starts[j] + width)
                            here = pl.ds(pl.multiple_of(at * width, 128), width)
                            steps.append(
                                (
                                    (cuts * n + h) + cuts * len(blocks) * who,
                                    (slice(None), slice(None), cols),
                                    j,
                                    (slice(None), at_y, lines, here),
                                )
                            )
            return steps

        made = move(
            [part for block in blocks + others for part in block],
            [(deep, high, rows, 2 * wide * width) for width in widths],
            into_place,
            name,
        )
        return [m.reshape(deep * high * rows, -1) for m in made]
    whole = jnp.zeros((high, 2 * wide, deep, rows, total), BF16)
    for n in range(len(blocks)):
        for who, part in ((0, blocks[n]), (1, others[n])):
            at = block_place(n, who) + (0, 0, 0)
            part = jnp.concatenate(part, axis=1)[None, None]
            whole = lax.dynamic_update_slice(whole, part, at)
    made = []
    for start, width in zip(starts, widths):
        part = whole[..., start : start + width]
        part = part.transpose(2, 0, 3, 1, 4)
        made.append(part.reshape(deep * high * rows, 2 * wide * width))
    return made


def split_grads(grads, widths, cuts, riders, name):
    deep, high, wide = sizes()
    rows = grads[0].shape[0] // (deep * high)
    half = rows // cuts
    total = sum(widths)
    count = len(offsets())
    starts = column_starts(widths)
    if aligned(widths):
        shaped = [g.reshape(deep, high, rows, 2 * wide * w) for g, w in zip(grads, widths)]

        def into_blocks():
            steps = []
            for n in range(count):
                for who in range(2):
                    at_y, at = block_place(n, who)
                    for h in range(cuts):
                        lines = slice(h * half, (h + 1) * half)
                        for j, width in enumerate(widths):
                            cols = slice(starts[j], starts[j] + width)
                            here = pl.ds(pl.multiple_of(at * width, 128), width)
                            steps.append(
                                (
                                    j,
                                    (slice(None), at_y, lines, here),
                                    cuts * (n + count * who) + h,
                                    (slice(None), lines_of(h), cols),
                                )
                            )
                        if h == 0 and riders is not None:
                            below = slice(half, half + riders.shape[1])
                            steps.append(
                                (
                                    len(widths),
                                    (slice(None), slice(None), slice(None)),
                                    cuts * (n + count * who),
                                    (slice(None), below, slice(None)),
                                )
                            )
            return steps

        def lines_of(h):
            return slice(0, half)

        sizes_made = [(deep, half, total)] * cuts
        if riders is not None:
            sizes_made[0] = (deep, half + riders.shape[1], total)
            shaped.append(riders)
        made = move(shaped, sizes_made * (2 * count), into_blocks, name)
        pairs = [tuple(made[cuts * n : cuts * (n + 1)]) for n in range(2 * count)]
        return pairs[:count], pairs[count:]
    whole = jnp.concatenate(
        [g.reshape(deep, high, rows, 2 * wide, w) for g, w in zip(grads, widths)], axis=-1
    ).transpose(1, 3, 0, 2, 4)

    def pick(n, who):
        at = block_place(n, who) + (0, 0, 0)
        part = lax.dynamic_slice(whole, at, (1, 1, deep, rows, total))[0, 0]
        return tuple(part[:, h * half : (h + 1) * half] for h in range(cuts))

    return [pick(n, 0) for n in range(count)], [pick(n, 1) for n in range(count)]


def swap_blocks(blocks):
    return [tuple(swap(part) for part in block) for block in blocks]


def add_blocks(blocks, others):
    made = add_many([a for x in blocks for a in x], [b for y in others for b in y])
    each = len(blocks[0])
    return [tuple(made[each * n : each * (n + 1)]) for n in range(len(blocks))]


def depth_sum(left):
    deep = lax.axis_size("fsdp")
    own = [summed([part[h] for part in left]) for h in range(len(left[0]))]
    own = jnp.concatenate(own, axis=1) if len(own) > 1 else own[0]
    low = own.astype(BF16)
    at = lax.axis_index("fsdp")
    result = lax.dynamic_index_in_dim(own, at, 0, keepdims=False)
    moved = []
    for k in range(1, deep):
        piece = lax.dynamic_index_in_dim(low, (at + k) % deep, 0, keepdims=False)
        moved.append(shift(piece, "fsdp", k))
    return result, moved


def depth_rest(result, moved, end, lines=0):
    result = result + summed(moved)
    if lines:
        rest = [result[: end - lines]] + ([result[end:]] if end < result.shape[0] else [])
        return jnp.concatenate(rest, axis=0), result[end - lines : end]
    return result


def after(value, *gates):
    return lax.optimization_barrier((value,) + gates)[0]


def gated(blocks, *gates):
    flat = [part for block in blocks for part in block]
    made = list(lax.optimization_barrier(tuple(flat) + gates))
    out = []
    for block in blocks:
        out.append(tuple(made[: len(block)]))
        made = made[len(block) :]
    return [out] + made


def regroup(first, second, third):
    made = gated(first + second + third)[0]
    at = len(first)
    return made[:at], made[at : at + len(second)], made[-1]


def row_grads_kernel(own_rows, own_memory, dk, dv, wk, wv, memory, own, own_mem, *blocks):
    n = pl.program_id(0)
    part = product_right(dk[...], wk[...]) + product_right(dv[...], wv[...])

    @pl.when(n == 0)
    def _():
        own[...] = part
        own_mem[...] = memory[...]

    for m in range(1, len(blocks) // 2 + 1):

        @pl.when(n == m)
        def _():
            for h in range(2):
                block = blocks[2 * (m - 1) + h]
                block[:own_rows] = part[h * own_rows : (h + 1) * own_rows].astype(BF16)
                lines = slice(h * own_memory, (h + 1) * own_memory)
                block[own_rows:] = memory[lines].astype(BF16)


def row_grads(dk, dv, wk, wv, memory, own_rows):
    count = len(offsets())
    width = wk.shape[0]
    own_memory = memory.shape[0] // (2 * count)

    def rows_of(size, columns):
        return pl.BlockSpec((size, columns), lambda n: (n, 0))

    def whole(*shape):
        return pl.BlockSpec(shape, lambda n: (0, 0))

    block = (own_rows + own_memory, width)
    own, own_mem, *blocks = pl.pallas_call(
        functools.partial(row_grads_kernel, own_rows, own_memory),
        grid=(count,),
        in_specs=[
            rows_of(2 * own_rows, dk.shape[1]),
            rows_of(2 * own_rows, dv.shape[1]),
            whole(*wk.shape),
            whole(*wv.shape),
            rows_of(2 * own_memory, width),
        ],
        out_specs=[whole(2 * own_rows, width), whole(2 * own_memory, width)]
        + [whole(*block)] * (2 * (count - 1)),
        out_shape=[
            jax.ShapeDtypeStruct((2 * own_rows, width), F32),
            jax.ShapeDtypeStruct((2 * own_memory, width), F32),
        ]
        + [jax.ShapeDtypeStruct(block, BF16)] * (2 * (count - 1)),
        compiler_params=pltpu.CompilerParams(vmem_limit_bytes=VMEM_BYTES),
        name="row_grads",
    )(dk, dv, wk, wv, memory)
    pairs = [(blocks[2 * n], blocks[2 * n + 1]) for n in range(count - 1)]
    return own, own_mem, [pairs[0]] + pairs


RIDER_LINES = 8


def pack_kernel(chunk, *refs):
    made = refs[-1]
    made[...] = jnp.zeros(made.shape, BF16)
    per_line = made.shape[2] // chunk
    at = 0
    for ref in refs[:-1]:
        for row in range(ref.shape[0]):
            for start in range(0, ref.shape[1], chunk):
                line, column = at // per_line, at % per_line * chunk
                value = ref[row : row + 1, start : start + chunk].astype(BF16)
                for copy in range(made.shape[0]):
                    made[copy, line : line + 1, column : column + chunk] = value
                at += 1


def pack_riders(vectors, chunk, deep, total):
    return pl.pallas_call(
        functools.partial(pack_kernel, chunk),
        out_shape=jax.ShapeDtypeStruct((deep, RIDER_LINES, total), BF16),
        name="pack_riders",
    )(*[v.reshape(-1, vectors[0].shape[0]) for v in vectors])


def unpack_riders(lines, chunk, lengths):
    per_line = lines.shape[1] // chunk
    flat = lines[:, : per_line * chunk].reshape(-1)
    starts = column_starts(lengths)
    return [flat[start : start + size] for start, size in zip(starts, lengths)]


def prologue_kernel(inputs, memory, *refs):
    weights, (keep, give, first, second) = refs[:10], refs[10:]
    core = lax.axis_index("tp") % 2
    rows = inputs.shape[1]
    keep[:rows] = inputs[core]
    keep[rows:] = memory[core]
    give[:rows] = inputs[1 - core]
    give[rows:] = memory[1 - core]
    for target, group in ((first, weights[:3]), (second, weights[3:])):
        start = 0
        for ref in group:
            target[:, start : start + ref.shape[1]] = ref[...]
            start += ref.shape[1]


def prologue(inputs, memory, weights):
    rows = weights[0].shape[0]
    widths = [w.shape[1] for w in weights]
    if not aligned(widths):
        core = lax.axis_index("tp") % 2
        both = jnp.concatenate([inputs, memory], axis=1)
        keep = lax.dynamic_index_in_dim(both, core, 0, keepdims=False)
        give = lax.dynamic_index_in_dim(both, 1 - core, 0, keepdims=False)
        return (
            keep,
            give,
            jnp.concatenate(weights[:3], axis=1),
            jnp.concatenate(weights[3:], axis=1),
        )
    block = (inputs.shape[1] + memory.shape[1], inputs.shape[2])
    return pl.pallas_call(
        prologue_kernel,
        out_shape=[
            jax.ShapeDtypeStruct(block, BF16),
            jax.ShapeDtypeStruct(block, BF16),
            jax.ShapeDtypeStruct((rows, sum(widths[:3])), BF16),
            jax.ShapeDtypeStruct((rows, sum(widths[3:])), BF16),
        ],
        compiler_params=pltpu.CompilerParams(vmem_limit_bytes=VMEM_BYTES),
        name="prologue",
    )(inputs, memory, *weights)


def all_sum(value, axes):
    for axis in axes:
        total = lax.axis_size(axis)
        step = 1
        while step < total:
            pairs = [(i, i ^ step) for i in range(total)]
            value = value + lax.ppermute(value, axis, pairs)
            step *= 2
    return value


def per_device(
    inputs,
    memory,
    cotangent,
    positions,
    lengths,
    memory_lengths,
    query_weight,
    key_weight,
    value_weight,
    output_weight,
    cross_query_weight,
    cross_key_weight,
    cross_value_weight,
    cross_output_weight,
    expand_weight,
    reduce_weight,
    query_bias,
    value_bias,
    output_bias,
    first_gain,
    first_shift,
    cross_query_bias,
    cross_value_bias,
    cross_output_bias,
    second_gain,
    second_shift,
    expand_bias,
    reduce_bias,
    third_gain,
    third_shift,
):
    deep, high, wide = sizes()
    z, y, x, core = places()
    own_rows, width = inputs.shape[1:]
    own_memory = memory.shape[1]
    rows = 2 * own_rows
    head_width = query_weight.shape[1]
    hidden_width = expand_weight.shape[1]

    keep, give, first_pack, second_pack = prologue(
        inputs,
        memory,
        [
            query_weight,
            key_weight,
            value_weight,
            cross_key_weight,
            cross_value_weight,
            output_weight.T,
            cross_query_weight,
            cross_output_weight.T,
            expand_weight,
            reduce_weight.T,
        ],
    )
    first_widths = [head_width] * 3
    second_widths = [head_width] * 5 + [hidden_width] * 2

    got = swap(give)
    first_pieces = spread(after(first_pack, got))
    blocks = plane_one(keep, got)
    first_depth = depth_blocks(first_pieces, 1, "stack_first")[0]
    *blocks, (first_depth,) = gated(blocks + [(first_depth,)])[0]
    blocks = plane_two(blocks)
    first_blocks = plane_direct(first_depth)
    second_pieces = spread(after(second_pack, *first_pieces[1:]))
    cotangent_pair = (
        lax.dynamic_index_in_dim(cotangent, core, 0, keepdims=False),
        swap(lax.dynamic_index_in_dim(cotangent, 1 - core, 0, keepdims=False)),
    )
    full_query, full_key, full_value = whole_weights(first_blocks, first_widths, "place_first")
    pieces = [p for b in blocks for p in b]

    def rows_together():
        steps = []
        for n in range(len(pieces)):
            at = n * own_rows
            steps.append((n, slice(0, own_rows), 0, slice(at, at + own_rows)))
            at = n * own_memory
            steps.append(
                (n, slice(own_rows, own_rows + own_memory), 1, slice(at, at + own_memory))
            )
        return steps

    wide_rows, wide_memory = move(
        pieces,
        [(len(pieces) * own_rows, width), (len(pieces) * own_memory, width)],
        rows_together,
        "rows_together",
    )
    rows_in = wide_rows[:rows]
    second_half = plane_one(
        *depth_blocks([after(p, wide_rows) for p in second_pieces], 2, "stack_second")
    )

    slots = lax.dynamic_index_in_dim(positions, core, 0, keepdims=False)
    length = lax.dynamic_index_in_dim(lengths, core, 0, keepdims=False)
    memory_length = lax.dynamic_index_in_dim(memory_lengths, core, 0, keepdims=False)
    key_positions = []
    memory_slots = []
    for dx, dy in offsets():
        at_y = (y - dy + high) % high
        at_x = (x - dx + wide) % wide
        for who in (core, 1 - core):
            block = (at_y * wide + at_x) * 2 + who
            key_positions.append(lax.dynamic_slice_in_dim(slots, block * own_rows, own_rows))
            memory_slots.append(block * own_memory + jnp.arange(own_memory, dtype=jnp.int32))
    own_positions = jnp.concatenate(key_positions[:2])
    key_positions = jnp.concatenate(key_positions)
    last = positions.shape[1]
    key_positions = jnp.where(key_positions < length, key_positions, last)[:, None]
    query_positions = own_positions[None, :]
    memory_slots = jnp.concatenate(memory_slots)[:, None]
    memory_limit = jnp.broadcast_to(memory_length - 1, (1, rows))

    query_low = (product(rows_in, full_query) + query_bias).astype(BF16)
    keys = product(wide_rows, full_key).astype(BF16)
    values = (product(wide_rows, full_value) + value_bias).astype(BF16)
    early = list(attend(query_low, keys, values, query_positions, key_positions, 0, 2))
    second_half, late_query, ready = gated(second_half, query_low, early[1])
    early[1] = ready
    second_blocks = plane_two(second_half)
    attended, attended_exact, weights, inverse = attend(
        late_query, keys, values, query_positions, key_positions, 1, 2, early
    )
    second_blocks, attended = gated(second_blocks, attended)
    (
        full_cross_key,
        full_cross_value,
        full_output,
        full_cross_query,
        full_cross_output,
        full_expand,
        full_reduce,
    ) = whole_weights(second_blocks, second_widths, "place_second")
    memory_key = product(wide_memory, full_cross_key).astype(BF16)
    memory_value = (product(wide_memory, full_cross_value) + cross_value_bias).astype(BF16)

    first_in = rows_in.astype(F32) + product_right(attended, full_output) + output_bias
    first_out = layer_norm(first_in, first_gain, first_shift)
    first_low = first_out.astype(BF16)
    cross_query = (product(first_low, full_cross_query) + cross_query_bias).astype(BF16)
    cross_attended, cross_exact, cross_weights, cross_inverse = attend(
        cross_query, memory_key, memory_value, memory_limit, memory_slots
    )
    second_in = first_out + product_right(cross_attended, full_cross_output) + cross_output_bias
    second_out = layer_norm(second_in, second_gain, second_shift)
    second_low = second_out.astype(BF16)
    expanded = product(second_low, full_expand) + expand_bias
    gate = jax.nn.sigmoid(expanded)
    activated = (expanded * gate).astype(BF16)
    third_in = second_out + product_right(activated, full_reduce) + reduce_bias
    outputs = layer_norm(third_in, third_gain, third_shift)

    grad_in = jnp.concatenate(cotangent_pair, axis=0).astype(F32)
    masked_grad = jnp.where((own_positions < length)[:, None], grad_in, 0.0)
    third_grad, third_gain_part, third_shift_part = norm_back(third_in, third_gain, masked_grad)
    third_low = third_grad.astype(BF16)
    activated_grad = product(third_low, full_reduce)
    expanded_grad = (activated_grad * gate * (1.0 + expanded * (1.0 - gate))).astype(BF16)
    third_part = [
        product_left(second_low, expanded_grad).astype(BF16),
        product_left(third_low, activated).astype(BF16),
    ]
    second_grad = third_grad + product_right(expanded_grad, full_expand)
    second_in_grad, second_gain_part, second_shift_part = norm_back(
        second_in, second_gain, second_grad
    )
    second_grad_low = second_in_grad.astype(BF16)
    cross_attended_grad = product(second_grad_low, full_cross_output).astype(BF16)
    cross_query_grad, memory_key_grad, memory_value_grad = attend_back(
        cross_query,
        memory_key,
        memory_value,
        cross_weights,
        cross_inverse,
        cross_exact,
        cross_attended_grad,
    )
    first_grad = second_in_grad + product_right(cross_query_grad, full_cross_query)
    first_in_grad, first_gain_part, first_shift_part = norm_back(first_in, first_gain, first_grad)
    first_grad_low = first_in_grad.astype(BF16)
    attended_grad = product(first_grad_low, full_output).astype(BF16)
    second_part = [
        product_left(wide_memory, memory_key_grad).astype(BF16),
        product_left(wide_memory, memory_value_grad).astype(BF16),
        product_left(first_grad_low, attended).astype(BF16),
        product_left(first_low, cross_query_grad).astype(BF16),
        product_left(second_grad_low, cross_attended).astype(BF16),
    ]
    early_vectors = [
        jnp.sum(first_in_grad, axis=0),
        first_gain_part,
        first_shift_part,
        jnp.sum(cross_query_grad.astype(F32), axis=0),
        jnp.sum(memory_value_grad.astype(F32), axis=0),
        jnp.sum(second_in_grad, axis=0),
        second_gain_part,
        second_shift_part,
        jnp.sum(expanded_grad.astype(F32), axis=0),
        jnp.sum(third_grad, axis=0),
        third_gain_part,
        third_shift_part,
    ]
    ride = aligned(first_widths + second_widths) and rows % 256 == 0
    early_riders = late_riders = None
    if ride:
        early_riders = pack_riders(early_vectors, 512, deep, sum(second_widths))
    second_keep, second_give = split_grads(
        second_part + third_part, second_widths, 2, early_riders, "split_second"
    )
    second_other = swap_blocks(second_give)
    memory_part = product_right(memory_key_grad, full_cross_key) + product_right(
        memory_value_grad, full_cross_value
    )

    second_blocks = add_blocks(second_keep, second_other)
    second_blocks, early_grad = gated(second_blocks, attended_grad)
    second_blocks = sum_one(second_blocks)
    early = list(
        attend_back(query_low, keys, values, weights, inverse, attended_exact, early_grad, 0, 2)
    )
    second_blocks, early[0] = gated(second_blocks, early[0])
    second_blocks = sum_adds(second_blocks)
    second_blocks, late_grad = gated(second_blocks, attended_grad)
    second_left = sum_two(second_blocks)
    query_grad, key_grad, value_grad = attend_back(
        query_low, keys, values, weights, inverse, attended_exact, late_grad, 1, 2, early
    )
    input_part, memory_own, low_blocks = row_grads(
        key_grad, value_grad, full_key, full_value, memory_part, own_rows
    )
    low_blocks, second_left, (query_late, key_late, value_late) = regroup(
        low_blocks, second_left, [(query_grad, key_grad, value_grad)]
    )
    low_blocks = sum_one(low_blocks)
    second_own, second_moved = depth_sum(second_left)
    input_own = first_in_grad + product_right(query_late, full_query)
    first_part = [
        product_left(rows_in, query_late).astype(BF16),
        product_left(wide_rows, key_late).astype(BF16),
        product_left(wide_rows, value_late).astype(BF16),
    ]
    late_vectors = [
        jnp.sum(query_late.astype(F32), axis=0),
        jnp.sum(value_late.astype(F32), axis=0),
    ]
    low_blocks = sum_adds(low_blocks)
    low_blocks, unused, first_part = regroup(low_blocks, [], [tuple(first_part)])
    left = sum_two(low_blocks)[1:]
    if ride:
        late_riders = pack_riders(late_vectors, 128, deep, sum(first_widths))
    first_keep, first_give = split_grads(first_part, first_widths, 1, late_riders, "split_first")
    first_other = swap_blocks(first_give)
    left, first_keep, unused = regroup(left, first_keep, [()])
    first_blocks = add_blocks(first_keep, first_other)
    first_left = sum_direct(first_blocks)
    first_left, unused, second_moved = regroup(first_left, [], [tuple(second_moved)])
    first_own, first_moved = depth_sum(first_left)
    ends = first_left[0][0].shape[1], second_left[0][0].shape[1]
    first_shard = depth_rest(first_own, first_moved, ends[0], RIDER_LINES if ride else 0)
    second_shard = depth_rest(second_own, second_moved, ends[1], RIDER_LINES if ride else 0)
    pair = [summed([part[h] for part in left]) for h in range(2)]
    input_pair = [
        input_own[h * own_rows : (h + 1) * own_rows]
        + input_part[h * own_rows : (h + 1) * own_rows]
        + pair[h][:own_rows]
        for h in range(2)
    ]
    memory_pair = [
        memory_own[h * own_memory : (h + 1) * own_memory] + pair[h][own_rows:] for h in range(2)
    ]

    def restore(pair):
        other = swap(pair[1])
        return jnp.where(
            core == 0, jnp.stack([pair[0], other]), jnp.stack([other, pair[0]])
        )

    output_result = restore([outputs[:own_rows], outputs[own_rows:]])
    input_result = restore(input_pair)
    memory_result = restore(memory_pair)

    vectors = late_vectors + early_vectors
    lengths = [v.shape[0] for v in vectors]
    if ride:
        first_shard, late_lines = first_shard
        second_shard, early_lines = second_shard
        split = unpack_riders(late_lines, 128, lengths[:2])
        split += unpack_riders(early_lines, 512, lengths[2:])
    else:
        joined = all_sum(jnp.concatenate(vectors), ("fsdp", "tp", "ctx"))
        starts = column_starts(lengths)
        split = [joined[start : start + size] for start, size in zip(starts, lengths)]

    def shards(packed, widths):
        start = 0
        parts = []
        for one in widths:
            parts.append(packed[:, start : start + one])
            start += one
        return parts

    g_query, g_key, g_value = shards(first_shard, first_widths)
    (
        g_cross_key,
        g_cross_value,
        g_output,
        g_cross_query,
        g_cross_output,
        g_expand,
        g_reduce,
    ) = shards(second_shard, second_widths)
    return (
        output_result,
        input_result,
        memory_result,
        g_query,
        g_key,
        g_value,
        g_output.T,
        g_cross_query,
        g_cross_key,
        g_cross_value,
        g_cross_output.T,
        g_expand,
        g_reduce.T,
        *split,
    )


def solution(mesh):
    rows = P("fsdp", ("ctx", "tp"), None)
    tall = P(("fsdp", "ctx"), "tp")
    flat = P("tp", ("fsdp", "ctx"))
    weights = (tall, tall, tall, flat, tall, tall, tall, flat, tall, flat)
    return jax.shard_map(
        per_device,
        mesh=mesh,
        in_specs=(rows, rows, rows, P("fsdp", None), P("fsdp"), P("fsdp"))
        + weights
        + (P(),) * 14,
        out_specs=(rows, rows, rows) + weights + (P(),) * 14,
        check_vma=False,
    )
```

```python
import functools

import jax
import jax.numpy as jnp
from jax import lax
from jax.experimental import pallas as pl
from jax.experimental.pallas import tpu as pltpu
from jax.sharding import PartitionSpec as P

HEAD_DIM = 64
EPSILON = 1e-05
NEGATIVE = -1e30
F32 = jnp.float32
BF16 = jnp.bfloat16
SCALE = HEAD_DIM ** -0.5
VMEM_BYTES = 58 * 2 ** 20


def contract(left, right, left_dim, right_dim):
    return lax.dot_general(
        left, right, (((left_dim,), (right_dim,)), ((), ())), preferred_element_type=F32
    )


def product(left, right):
    return contract(left, right, 1, 0)


def product_left(left, right):
    return contract(left, right, 0, 0)


def product_right(left, right):
    return contract(left, right, 1, 1)


def layer_norm(values, gain, shift):
    center = values - jnp.mean(values, axis=-1, keepdims=True)
    spread = jnp.mean(center * center, axis=-1, keepdims=True)
    return center * lax.rsqrt(spread + EPSILON) * gain + shift


def norm_back(values, gain, grad):
    center = values - jnp.mean(values, axis=-1, keepdims=True)
    spread = jnp.mean(center * center, axis=-1, keepdims=True)
    rate = lax.rsqrt(spread + EPSILON)
    normal = center * rate
    scaled = grad * gain
    back = rate * (
        scaled
        - jnp.mean(scaled, axis=-1, keepdims=True)
        - normal * jnp.mean(scaled * normal, axis=-1, keepdims=True)
    )
    return back, jnp.sum(grad * normal, axis=0), jnp.sum(grad, axis=0)


def attend_kernel(heads, q, k, v, qp, kp, *refs):
    out, exact, weights, inverse = refs[-4:]
    allowed = kp[...] <= qp[...]
    for head in range(heads):
        cols = slice(head * HEAD_DIM, (head + 1) * HEAD_DIM)
        scores = contract(k[:, cols], q[:, cols] * SCALE, 1, 1)
        scores = jnp.where(allowed, scores, NEGATIVE)
        largest = jnp.max(scores, axis=0, keepdims=True)
        power = jnp.exp(scores - largest)
        rate = 1.0 / jnp.sum(power, axis=0, keepdims=True)
        low = power.astype(BF16)
        weights[head] = low
        inverse[head] = rate
        mixed = contract(v[:, cols], low, 0, 0) * rate
        exact[cols, :] = mixed
        out[:, cols] = mixed.T.astype(BF16)


def attend_back_kernel(heads, q, k, v, weights, inverse, exact, grad, *refs):
    dq, dk, dv, dq_sum, dv_sum = refs[-5:]
    for head in range(heads):
        cols = slice(head * HEAD_DIM, (head + 1) * HEAD_DIM)
        grads = grad[:, cols].astype(F32).T
        inner = jnp.sum(grads * exact[cols, :], axis=0, keepdims=True) * inverse[head]
        scaled = (grads * inverse[head]).astype(BF16)
        weight = weights[head]
        grad_weight = contract(v[:, cols], scaled, 1, 0)
        grad_scores = (weight.astype(F32) * (grad_weight - inner)).astype(BF16)
        low = (contract(k[:, cols], grad_scores, 0, 0) * SCALE).T.astype(BF16)
        dq[:, cols] = low
        dq_sum[:, cols] = jnp.sum(low.astype(F32), axis=0, keepdims=True)
        low = contract(weight, scaled, 1, 1).astype(BF16)
        dv[:, cols] = low
        dv_sum[:, cols] = jnp.sum(low.astype(F32), axis=0, keepdims=True)
        dk[:, cols] = (contract(grad_scores, q[:, cols], 1, 0) * SCALE).astype(BF16)


HEADS_PER_STEP = 2


def attend_call(body, arrays, specs, shapes, out_specs, earlier, each, steps, cost, name):
    given = [] if earlier is None else list(earlier)
    return pl.pallas_call(
        functools.partial(body, each),
        grid=(steps,),
        in_specs=specs + [pl.BlockSpec(memory_space=pl.ANY)] * len(given),
        out_specs=out_specs,
        out_shape=shapes,
        input_output_aliases={len(arrays) + i: i for i in range(len(given))},
        compiler_params=pltpu.CompilerParams(vmem_limit_bytes=VMEM_BYTES),
        cost_estimate=cost,
        name=name,
    )(*arrays, *given)


def head_specs(first, each):
    def columns(rows):
        return pl.BlockSpec((rows, each * HEAD_DIM), lambda i: (0, i + first))

    def lines(rows):
        return pl.BlockSpec((each * HEAD_DIM, rows), lambda i: (i + first, 0))

    def heads(*dims):
        return pl.BlockSpec((each,) + dims, lambda i: (i + first, 0, 0))

    return columns, lines, heads


def attend(q, k, v, qp, kp, part=0, parts=1, earlier=None):
    rows, width = q.shape
    keys = k.shape[0]
    heads = width // HEAD_DIM
    each = HEADS_PER_STEP
    steps = heads // each // parts
    columns, lines, by_head = head_specs(part * steps, each)
    return attend_call(
        attend_kernel,
        (q, k, v, qp, kp),
        [
            columns(rows),
            columns(keys),
            columns(keys),
            pl.BlockSpec((1, rows), lambda i: (0, 0)),
            pl.BlockSpec((keys, 1), lambda i: (0, 0)),
        ],
        [
            jax.ShapeDtypeStruct((rows, width), BF16),
            jax.ShapeDtypeStruct((width, rows), F32),
            jax.ShapeDtypeStruct((heads, keys, rows), BF16),
            jax.ShapeDtypeStruct((heads, 1, rows), F32),
        ],
        [columns(rows), lines(rows), by_head(keys, rows), by_head(1, rows)],
        earlier,
        each,
        steps,
        pl.CostEstimate(
            flops=16 * rows * keys * width // parts,
            transcendentals=heads * rows * keys // parts,
            bytes_accessed=2 * heads * rows * keys // parts,
        ),
        "attend",
    )


def attend_back(q, k, v, weights, inverse, exact, grad, part=0, parts=1, earlier=None):
    rows, width = q.shape
    keys = k.shape[0]
    heads = width // HEAD_DIM
    each = HEADS_PER_STEP
    steps = heads // each // parts
    columns, lines, by_head = head_specs(part * steps, each)
    return attend_call(
        attend_back_kernel,
        (q, k, v, weights, inverse, exact, grad),
        [
            columns(rows),
            columns(keys),
            columns(keys),
            by_head(keys, rows),
            by_head(1, rows),
            lines(rows),
            columns(rows),
        ],
        [
            jax.ShapeDtypeStruct((rows, width), BF16),
            jax.ShapeDtypeStruct((keys, width), BF16),
            jax.ShapeDtypeStruct((keys, width), BF16),
            jax.ShapeDtypeStruct((1, width), F32),
            jax.ShapeDtypeStruct((1, width), F32),
        ],
        [columns(rows), columns(keys), columns(keys), columns(1), columns(1)],
        earlier,
        each,
        steps,
        pl.CostEstimate(
            flops=32 * rows * keys * width // parts,
            transcendentals=0,
            bytes_accessed=2 * heads * rows * keys // parts,
        ),
        "attend_back",
    )


def move(sources, shapes, plan, name):
    def body(*refs):
        given = refs[: len(sources)]
        made = refs[len(sources) : len(sources) + len(shapes)]
        sems = refs[-1]
        copies = []
        for at, (i, a, j, b) in enumerate(plan()):
            copies.append(pltpu.make_async_copy(given[i].at[a], made[j].at[b], sems.at[at]))
        for copy in copies:
            copy.start()
        for copy in copies:
            copy.wait()

    count = move_count(plan)
    return pl.pallas_call(
        body,
        in_specs=[pl.BlockSpec(memory_space=pl.ANY)] * len(sources),
        out_specs=[pl.BlockSpec(memory_space=pltpu.VMEM)] * len(shapes),
        out_shape=[jax.ShapeDtypeStruct(shape, BF16) for shape in shapes],
        scratch_shapes=[pltpu.SemaphoreType.DMA((count,))],
        compiler_params=pltpu.CompilerParams(vmem_limit_bytes=VMEM_BYTES),
        name=name,
    )(*sources)


def move_count(plan):
    return len(plan())


def sizes():
    return lax.axis_size("fsdp"), lax.axis_size("ctx"), lax.axis_size("tp") // 2


def places():
    tp = lax.axis_index("tp")
    return lax.axis_index("fsdp"), lax.axis_index("ctx"), tp // 2, tp % 2


def swap(value):
    total = lax.axis_size("tp")
    return lax.ppermute(value, "tp", [(i, i ^ 1) for i in range(total)])


def shift_x(value, step):
    total = lax.axis_size("tp")
    return lax.ppermute(value, "tp", [(i, (i + 2 * step) % total) for i in range(total)])


def shift(value, axis, step):
    total = lax.axis_size(axis)
    return lax.ppermute(value, axis, [(i, (i + step) % total) for i in range(total)])


def offsets():
    unused, high, wide = sizes()
    return [(dx, dy) for dy in range(high) for dx in range(wide)]


def is_square():
    unused, high, wide = sizes()
    return high == 2 and wide == 2


def shift_plane(value, dx, dy):
    high, total = lax.axis_size("ctx"), lax.axis_size("tp")
    pairs = [
        (c * total + t, (c + dy) % high * total + (t + 2 * dx) % total)
        for c in range(high)
        for t in range(total)
    ]
    return lax.ppermute(value, ("ctx", "tp"), pairs)


def plane_direct(value):
    return [(value,)] + [(shift_plane(value, dx, dy),) for dx, dy in offsets()[1:]]


def sum_direct(blocks):
    moved = [(shift_plane(b[0], -dx, -dy),) for b, (dx, dy) in zip(blocks[1:], offsets()[1:])]
    return [blocks[0]] + moved


def plane_one(first, second):
    if is_square():
        side = (shift_x(first, 1), shift_x(second, 1))
        front = (shift(first, "ctx", 1), shift(second, "ctx", 1))
        return [(first, second), side, front]
    unused, high, wide = sizes()
    row = [(first, second)] + [(shift_x(first, k), shift_x(second, k)) for k in range(1, wide)]
    blocks = list(row)
    for step in range(1, high):
        blocks += [(shift(a, "ctx", step), shift(b, "ctx", step)) for a, b in row]
    return blocks


def plane_two(blocks):
    if is_square():
        own, side, front = blocks
        return [own, side, front, (shift(side[0], "ctx", 1), shift_x(front[1], 1))]
    return blocks


def add(left, right):
    return (left.astype(F32) + right.astype(F32)).astype(BF16)


def add_kernel(*refs):
    count = len(refs) // 3
    for n in range(count):
        total = refs[n][...].astype(F32) + refs[count + n][...].astype(F32)
        refs[2 * count + n][...] = total.astype(BF16)


def add_many(left, right):
    steps = left[0].shape[0]
    if sum(part.size for part in left) < 2**20:
        steps = 1

    def spec(part):
        rest = part.shape[1:]
        return pl.BlockSpec((part.shape[0] // steps,) + rest, lambda i: (i,) + (0,) * len(rest))

    return pl.pallas_call(
        add_kernel,
        grid=(steps,),
        in_specs=[spec(part) for part in left] * 2,
        out_specs=[spec(part) for part in left],
        out_shape=[jax.ShapeDtypeStruct(part.shape, BF16) for part in left],
        name="add_many",
    )(*left, *right)


def sum_one(blocks):
    if is_square():
        own, side, front, far = blocks
        return [own, side, front, (shift(far[0], "ctx", 1), shift_x(far[1], 1))]
    return blocks


def sum_adds(blocks):
    if is_square():
        own, side, front, far = blocks
        first, second = add_many([side[0], front[1]], [far[0], far[1]])
        return [own, (first, side[1]), (front[0], second)]
    return blocks


def sum_two(blocks):
    if is_square():
        own, side, front = blocks
        from_side = (shift_x(side[0], 1), shift_x(side[1], 1))
        from_front = (shift(front[0], "ctx", 1), shift(front[1], "ctx", 1))
        return [own, from_side, from_front]
    unused, high, wide = sizes()
    row = []
    for dx in range(wide):
        total = blocks[dx]
        for dy in range(1, high):
            other = blocks[dy * wide + dx]
            total = tuple(add(a, shift(b, "ctx", -dy)) for a, b in zip(total, other))
        row.append(total)
    return [row[0]] + [
        (shift_x(row[dx][0], -dx), shift_x(row[dx][1], -dx)) for dx in range(1, wide)
    ]


def summed(parts):
    return sum(part.astype(F32) for part in parts)


def spread(packed):
    return [packed] + [shift(packed, "fsdp", k) for k in range(1, lax.axis_size("fsdp"))]


def depth_blocks(pieces, cuts, name):
    deep = len(pieces)
    rows, total = pieces[0].shape
    half = rows // cuts

    def by_depth():
        at = lax.axis_index("fsdp")
        steps = []
        for k in range(deep):
            for h in range(cuts):
                steps.append((k, slice(h * half, (h + 1) * half), h, (at - k + deep) % deep))
        return steps

    return move(pieces, [(deep, half, total)] * cuts, by_depth, name)


def aligned(widths):
    return all(width % 128 == 0 for width in widths)


def column_starts(widths):
    return [sum(widths[:i]) for i in range(len(widths))]


def block_place(n, who):
    unused, high, wide = sizes()
    unused, y, x, core = places()
    dx, dy = offsets()[n]
    at_y = (y - dy + high) % high
    at_x = (x - dx + wide) % wide
    return at_y, 2 * at_x + (core if who == 0 else 1 - core)


def whole_weights(blocks, widths, name):
    deep, high, wide = sizes()
    half, total = blocks[0][0].shape[1:]
    cuts = len(blocks[0])
    rows = cuts * half
    others = [tuple(swap(part) for part in block) for block in blocks]
    starts = column_starts(widths)
    if aligned(widths):

        def into_place():
            steps = []
            for n in range(len(blocks)):
                for who in range(2):
                    at_y, at = block_place(n, who)
                    for h in range(cuts):
                        lines = slice(h * half, (h + 1) * half)
                        for j, width in enumerate(widths):
                            cols = slice(starts[j], starts[j] + width)
                            here = pl.ds(pl.multiple_of(at * width, 128), width)
                            steps.append(
                                (
                                    (cuts * n + h) + cuts * len(blocks) * who,
                                    (slice(None), slice(None), cols),
                                    j,
                                    (slice(None), at_y, lines, here),
                                )
                            )
            return steps

        made = move(
            [part for block in blocks + others for part in block],
            [(deep, high, rows, 2 * wide * width) for width in widths],
            into_place,
            name,
        )
        return [m.reshape(deep * high * rows, -1) for m in made]
    whole = jnp.zeros((high, 2 * wide, deep, rows, total), BF16)
    for n in range(len(blocks)):
        for who, part in ((0, blocks[n]), (1, others[n])):
            at = block_place(n, who) + (0, 0, 0)
            part = jnp.concatenate(part, axis=1)[None, None]
            whole = lax.dynamic_update_slice(whole, part, at)
    made = []
    for start, width in zip(starts, widths):
        part = whole[..., start : start + width]
        part = part.transpose(2, 0, 3, 1, 4)
        made.append(part.reshape(deep * high * rows, 2 * wide * width))
    return made


def split_grads(grads, widths, cuts, riders, name):
    deep, high, wide = sizes()
    rows = grads[0].shape[0] // (deep * high)
    half = rows // cuts
    total = sum(widths)
    count = len(offsets())
    starts = column_starts(widths)
    if aligned(widths):
        shaped = [g.reshape(deep, high, rows, 2 * wide * w) for g, w in zip(grads, widths)]

        def into_blocks():
            steps = []
            for n in range(count):
                for who in range(2):
                    at_y, at = block_place(n, who)
                    for h in range(cuts):
                        lines = slice(h * half, (h + 1) * half)
                        for j, width in enumerate(widths):
                            cols = slice(starts[j], starts[j] + width)
                            here = pl.ds(pl.multiple_of(at * width, 128), width)
                            steps.append(
                                (
                                    j,
                                    (slice(None), at_y, lines, here),
                                    cuts * (n + count * who) + h,
                                    (slice(None), lines_of(h), cols),
                                )
                            )
                        if h == 0 and riders is not None:
                            below = slice(half, half + riders.shape[1])
                            steps.append(
                                (
                                    len(widths),
                                    (slice(None), slice(None), slice(None)),
                                    cuts * (n + count * who),
                                    (slice(None), below, slice(None)),
                                )
                            )
            return steps

        def lines_of(h):
            return slice(0, half)

        sizes_made = [(deep, half, total)] * cuts
        if riders is not None:
            sizes_made[0] = (deep, half + riders.shape[1], total)
            shaped.append(riders)
        made = move(shaped, sizes_made * (2 * count), into_blocks, name)
        pairs = [tuple(made[cuts * n : cuts * (n + 1)]) for n in range(2 * count)]
        return pairs[:count], pairs[count:]
    whole = jnp.concatenate(
        [g.reshape(deep, high, rows, 2 * wide, w) for g, w in zip(grads, widths)], axis=-1
    ).transpose(1, 3, 0, 2, 4)

    def pick(n, who):
        at = block_place(n, who) + (0, 0, 0)
        part = lax.dynamic_slice(whole, at, (1, 1, deep, rows, total))[0, 0]
        return tuple(part[:, h * half : (h + 1) * half] for h in range(cuts))

    return [pick(n, 0) for n in range(count)], [pick(n, 1) for n in range(count)]


def swap_blocks(blocks):
    return [tuple(swap(part) for part in block) for block in blocks]


def add_blocks(blocks, others):
    made = add_many([a for x in blocks for a in x], [b for y in others for b in y])
    each = len(blocks[0])
    return [tuple(made[each * n : each * (n + 1)]) for n in range(len(blocks))]


def depth_sum(left):
    deep = lax.axis_size("fsdp")
    own = [summed([part[h] for part in left]) for h in range(len(left[0]))]
    own = jnp.concatenate(own, axis=1) if len(own) > 1 else own[0]
    low = own.astype(BF16)
    at = lax.axis_index("fsdp")
    result = lax.dynamic_index_in_dim(own, at, 0, keepdims=False)
    moved = []
    for k in range(1, deep):
        piece = lax.dynamic_index_in_dim(low, (at + k) % deep, 0, keepdims=False)
        moved.append(shift(piece, "fsdp", k))
    return result, moved


def depth_rest(result, moved, end, lines=0):
    result = result + summed(moved)
    if lines:
        rest = [result[: end - lines]] + ([result[end:]] if end < result.shape[0] else [])
        return jnp.concatenate(rest, axis=0), result[end - lines : end]
    return result


def after(value, *gates):
    return lax.optimization_barrier((value,) + gates)[0]


def gated(blocks, *gates):
    flat = [part for block in blocks for part in block]
    made = list(lax.optimization_barrier(tuple(flat) + gates))
    out = []
    for block in blocks:
        out.append(tuple(made[: len(block)]))
        made = made[len(block) :]
    return [out] + made


def regroup(first, second, third):
    made = gated(first + second + third)[0]
    at = len(first)
    return made[:at], made[at : at + len(second)], made[-1]


def row_grads_kernel(own_rows, own_memory, dk, dv, wk, wv, memory, own, own_mem, *blocks):
    n = pl.program_id(0)
    part = product_right(dk[...], wk[...]) + product_right(dv[...], wv[...])

    @pl.when(n == 0)
    def _():
        own[...] = part
        own_mem[...] = memory[...]

    for m in range(1, len(blocks) // 2 + 1):

        @pl.when(n == m)
        def _():
            for h in range(2):
                block = blocks[2 * (m - 1) + h]
                block[:own_rows] = part[h * own_rows : (h + 1) * own_rows].astype(BF16)
                lines = slice(h * own_memory, (h + 1) * own_memory)
                block[own_rows:] = memory[lines].astype(BF16)


def row_grads(dk, dv, wk, wv, memory, own_rows):
    count = len(offsets())
    width = wk.shape[0]
    own_memory = memory.shape[0] // (2 * count)

    def rows_of(size, columns):
        return pl.BlockSpec((size, columns), lambda n: (n, 0))

    def whole(*shape):
        return pl.BlockSpec(shape, lambda n: (0, 0))

    block = (own_rows + own_memory, width)
    own, own_mem, *blocks = pl.pallas_call(
        functools.partial(row_grads_kernel, own_rows, own_memory),
        grid=(count,),
        in_specs=[
            rows_of(2 * own_rows, dk.shape[1]),
            rows_of(2 * own_rows, dv.shape[1]),
            whole(*wk.shape),
            whole(*wv.shape),
            rows_of(2 * own_memory, width),
        ],
        out_specs=[whole(2 * own_rows, width), whole(2 * own_memory, width)]
        + [whole(*block)] * (2 * (count - 1)),
        out_shape=[
            jax.ShapeDtypeStruct((2 * own_rows, width), F32),
            jax.ShapeDtypeStruct((2 * own_memory, width), F32),
        ]
        + [jax.ShapeDtypeStruct(block, BF16)] * (2 * (count - 1)),
        compiler_params=pltpu.CompilerParams(vmem_limit_bytes=VMEM_BYTES),
        name="row_grads",
    )(dk, dv, wk, wv, memory)
    pairs = [(blocks[2 * n], blocks[2 * n + 1]) for n in range(count - 1)]
    return own, own_mem, [pairs[0]] + pairs


RIDER_LINES = 8


def pack_kernel(chunk, *refs):
    made = refs[-1]
    made[...] = jnp.zeros(made.shape, BF16)
    per_line = made.shape[2] // chunk
    at = 0
    for ref in refs[:-1]:
        for row in range(ref.shape[0]):
            for start in range(0, ref.shape[1], chunk):
                line, column = at // per_line, at % per_line * chunk
                value = ref[row : row + 1, start : start + chunk].astype(BF16)
                for copy in range(made.shape[0]):
                    made[copy, line : line + 1, column : column + chunk] = value
                at += 1


def pack_riders(vectors, chunk, deep, total):
    return pl.pallas_call(
        functools.partial(pack_kernel, chunk),
        out_shape=jax.ShapeDtypeStruct((deep, RIDER_LINES, total), BF16),
        name="pack_riders",
    )(*[v.reshape(-1, vectors[0].shape[0]) for v in vectors])


def unpack_riders(lines, chunk, lengths):
    per_line = lines.shape[1] // chunk
    flat = lines[:, : per_line * chunk].reshape(-1)
    starts = column_starts(lengths)
    return [flat[start : start + size] for start, size in zip(starts, lengths)]


def prologue_kernel(inputs, memory, *refs):
    weights, (keep, give, first, second) = refs[:10], refs[10:]
    core = lax.axis_index("tp") % 2
    rows = inputs.shape[1]
    keep[:rows] = inputs[core]
    keep[rows:] = memory[core]
    give[:rows] = inputs[1 - core]
    give[rows:] = memory[1 - core]
    for target, group in ((first, weights[:3]), (second, weights[3:])):
        start = 0
        for ref in group:
            target[:, start : start + ref.shape[1]] = ref[...]
            start += ref.shape[1]


def prologue(inputs, memory, weights):
    rows = weights[0].shape[0]
    widths = [w.shape[1] for w in weights]
    if not aligned(widths):
        core = lax.axis_index("tp") % 2
        both = jnp.concatenate([inputs, memory], axis=1)
        keep = lax.dynamic_index_in_dim(both, core, 0, keepdims=False)
        give = lax.dynamic_index_in_dim(both, 1 - core, 0, keepdims=False)
        return (
            keep,
            give,
            jnp.concatenate(weights[:3], axis=1),
            jnp.concatenate(weights[3:], axis=1),
        )
    block = (inputs.shape[1] + memory.shape[1], inputs.shape[2])
    return pl.pallas_call(
        prologue_kernel,
        out_shape=[
            jax.ShapeDtypeStruct(block, BF16),
            jax.ShapeDtypeStruct(block, BF16),
            jax.ShapeDtypeStruct((rows, sum(widths[:3])), BF16),
            jax.ShapeDtypeStruct((rows, sum(widths[3:])), BF16),
        ],
        compiler_params=pltpu.CompilerParams(vmem_limit_bytes=VMEM_BYTES),
        name="prologue",
    )(inputs, memory, *weights)


def all_sum(value, axes):
    for axis in axes:
        total = lax.axis_size(axis)
        step = 1
        while step < total:
            pairs = [(i, i ^ step) for i in range(total)]
            value = value + lax.ppermute(value, axis, pairs)
            step *= 2
    return value


def per_device(
    inputs,
    memory,
    cotangent,
    positions,
    lengths,
    memory_lengths,
    query_weight,
    key_weight,
    value_weight,
    output_weight,
    cross_query_weight,
    cross_key_weight,
    cross_value_weight,
    cross_output_weight,
    expand_weight,
    reduce_weight,
    query_bias,
    value_bias,
    output_bias,
    first_gain,
    first_shift,
    cross_query_bias,
    cross_value_bias,
    cross_output_bias,
    second_gain,
    second_shift,
    expand_bias,
    reduce_bias,
    third_gain,
    third_shift,
):
    deep, high, wide = sizes()
    z, y, x, core = places()
    own_rows, width = inputs.shape[1:]
    own_memory = memory.shape[1]
    rows = 2 * own_rows
    head_width = query_weight.shape[1]
    hidden_width = expand_weight.shape[1]

    keep, give, first_pack, second_pack = prologue(
        inputs,
        memory,
        [
            query_weight,
            key_weight,
            value_weight,
            cross_key_weight,
            cross_value_weight,
            output_weight.T,
            cross_query_weight,
            cross_output_weight.T,
            expand_weight,
            reduce_weight.T,
        ],
    )
    first_widths = [head_width] * 3
    second_widths = [head_width] * 5 + [hidden_width] * 2

    got = swap(give)
    first_pieces = spread(after(first_pack, got))
    blocks = plane_one(keep, got)
    first_depth = depth_blocks(first_pieces, 1, "stack_first")[0]
    *blocks, (first_depth,) = gated(blocks + [(first_depth,)])[0]
    blocks = plane_two(blocks)
    first_blocks = plane_direct(first_depth)
    second_pieces = spread(after(second_pack, *first_pieces[1:]))
    cotangent_pair = (
        lax.dynamic_index_in_dim(cotangent, core, 0, keepdims=False),
        swap(lax.dynamic_index_in_dim(cotangent, 1 - core, 0, keepdims=False)),
    )
    full_query, full_key, full_value = whole_weights(first_blocks, first_widths, "place_first")
    pieces = [p for b in blocks for p in b]

    def rows_together():
        steps = []
        for n in range(len(pieces)):
            at = n * own_rows
            steps.append((n, slice(0, own_rows), 0, slice(at, at + own_rows)))
            at = n * own_memory
            steps.append(
                (n, slice(own_rows, own_rows + own_memory), 1, slice(at, at + own_memory))
            )
        return steps

    wide_rows, wide_memory = move(
        pieces,
        [(len(pieces) * own_rows, width), (len(pieces) * own_memory, width)],
        rows_together,
        "rows_together",
    )
    rows_in = wide_rows[:rows]
    second_blocks = plane_direct(
        depth_blocks([after(p, wide_rows) for p in second_pieces], 1, "stack_second")[0]
    )

    slots = lax.dynamic_index_in_dim(positions, core, 0, keepdims=False)
    length = lax.dynamic_index_in_dim(lengths, core, 0, keepdims=False)
    memory_length = lax.dynamic_index_in_dim(memory_lengths, core, 0, keepdims=False)
    key_positions = []
    memory_slots = []
    for dx, dy in offsets():
        at_y = (y - dy + high) % high
        at_x = (x - dx + wide) % wide
        for who in (core, 1 - core):
            block = (at_y * wide + at_x) * 2 + who
            key_positions.append(lax.dynamic_slice_in_dim(slots, block * own_rows, own_rows))
            memory_slots.append(block * own_memory + jnp.arange(own_memory, dtype=jnp.int32))
    own_positions = jnp.concatenate(key_positions[:2])
    key_positions = jnp.concatenate(key_positions)
    last = positions.shape[1]
    key_positions = jnp.where(key_positions < length, key_positions, last)[:, None]
    query_positions = own_positions[None, :]
    memory_slots = jnp.concatenate(memory_slots)[:, None]
    memory_limit = jnp.broadcast_to(memory_length - 1, (1, rows))

    query_low = (product(rows_in, full_query) + query_bias).astype(BF16)
    keys = product(wide_rows, full_key).astype(BF16)
    values = (product(wide_rows, full_value) + value_bias).astype(BF16)
    attended, attended_exact, weights, inverse = attend(
        query_low, keys, values, query_positions, key_positions
    )
    second_blocks, attended = gated(second_blocks, attended)
    (
        full_cross_key,
        full_cross_value,
        full_output,
        full_cross_query,
        full_cross_output,
        full_expand,
        full_reduce,
    ) = whole_weights(second_blocks, second_widths, "place_second")
    memory_key = product(wide_memory, full_cross_key).astype(BF16)
    memory_value = (product(wide_memory, full_cross_value) + cross_value_bias).astype(BF16)

    first_in = rows_in.astype(F32) + product_right(attended, full_output) + output_bias
    first_out = layer_norm(first_in, first_gain, first_shift)
    first_low = first_out.astype(BF16)
    cross_query = (product(first_low, full_cross_query) + cross_query_bias).astype(BF16)
    cross_attended, cross_exact, cross_weights, cross_inverse = attend(
        cross_query, memory_key, memory_value, memory_limit, memory_slots
    )
    second_in = first_out + product_right(cross_attended, full_cross_output) + cross_output_bias
    second_out = layer_norm(second_in, second_gain, second_shift)
    second_low = second_out.astype(BF16)
    expanded = product(second_low, full_expand) + expand_bias
    gate = jax.nn.sigmoid(expanded)
    activated = (expanded * gate).astype(BF16)
    third_in = second_out + product_right(activated, full_reduce) + reduce_bias
    outputs = layer_norm(third_in, third_gain, third_shift)

    grad_in = jnp.concatenate(cotangent_pair, axis=0).astype(F32)
    masked_grad = jnp.where((own_positions < length)[:, None], grad_in, 0.0)
    third_grad, third_gain_part, third_shift_part = norm_back(third_in, third_gain, masked_grad)
    third_low = third_grad.astype(BF16)
    activated_grad = product(third_low, full_reduce)
    expanded_grad = (activated_grad * gate * (1.0 + expanded * (1.0 - gate))).astype(BF16)
    third_part = [
        product_left(second_low, expanded_grad).astype(BF16),
        product_left(third_low, activated).astype(BF16),
    ]
    second_grad = third_grad + product_right(expanded_grad, full_expand)
    second_in_grad, second_gain_part, second_shift_part = norm_back(
        second_in, second_gain, second_grad
    )
    second_grad_low = second_in_grad.astype(BF16)
    cross_attended_grad = product(second_grad_low, full_cross_output).astype(BF16)
    cross_query_grad, memory_key_grad, memory_value_grad, *cross_sums = attend_back(
        cross_query,
        memory_key,
        memory_value,
        cross_weights,
        cross_inverse,
        cross_exact,
        cross_attended_grad,
    )
    first_grad = second_in_grad + product_right(cross_query_grad, full_cross_query)
    first_in_grad, first_gain_part, first_shift_part = norm_back(first_in, first_gain, first_grad)
    first_grad_low = first_in_grad.astype(BF16)
    attended_grad = product(first_grad_low, full_output).astype(BF16)
    second_part = [
        product_left(wide_memory, memory_key_grad).astype(BF16),
        product_left(wide_memory, memory_value_grad).astype(BF16),
        product_left(first_grad_low, attended).astype(BF16),
        product_left(first_low, cross_query_grad).astype(BF16),
        product_left(second_grad_low, cross_attended).astype(BF16),
    ]
    early_vectors = [
        jnp.sum(first_in_grad, axis=0),
        first_gain_part,
        first_shift_part,
        cross_sums[0].reshape(-1),
        cross_sums[1].reshape(-1),
        jnp.sum(second_in_grad, axis=0),
        second_gain_part,
        second_shift_part,
        jnp.sum(expanded_grad.astype(F32), axis=0),
        jnp.sum(third_grad, axis=0),
        third_gain_part,
        third_shift_part,
    ]
    ride = aligned(first_widths + second_widths) and rows % 256 == 0
    early_riders = late_riders = None
    if ride:
        early_riders = pack_riders(early_vectors, 512, deep, sum(second_widths))
    second_keep, second_give = split_grads(
        second_part + third_part, second_widths, 2, early_riders, "split_second"
    )
    second_other = swap_blocks(second_give)
    memory_part = product_right(memory_key_grad, full_cross_key) + product_right(
        memory_value_grad, full_cross_value
    )

    second_blocks = add_blocks(second_keep, second_other)
    second_blocks, early_grad = gated(second_blocks, attended_grad)
    second_blocks = sum_one(second_blocks)
    early = list(
        attend_back(query_low, keys, values, weights, inverse, attended_exact, early_grad, 0, 2)
    )
    second_blocks, early[0] = gated(second_blocks, early[0])
    second_blocks = sum_adds(second_blocks)
    second_blocks, late_grad = gated(second_blocks, attended_grad)
    second_left = sum_two(second_blocks)
    query_grad, key_grad, value_grad, *self_sums = attend_back(
        query_low, keys, values, weights, inverse, attended_exact, late_grad, 1, 2, early
    )
    input_part, memory_own, low_blocks = row_grads(
        key_grad, value_grad, full_key, full_value, memory_part, own_rows
    )
    low_blocks, second_left, (query_late, key_late, value_late) = regroup(
        low_blocks, second_left, [(query_grad, key_grad, value_grad)]
    )
    low_blocks = sum_one(low_blocks)
    second_own, second_moved = depth_sum(second_left)
    input_own = first_in_grad + product_right(query_late, full_query)
    first_part = [
        product_left(rows_in, query_late).astype(BF16),
        product_left(wide_rows, key_late).astype(BF16),
        product_left(wide_rows, value_late).astype(BF16),
    ]
    late_vectors = [self_sums[0].reshape(-1), self_sums[1].reshape(-1)]
    low_blocks = sum_adds(low_blocks)
    low_blocks, unused, first_part = regroup(low_blocks, [], [tuple(first_part)])
    left = sum_two(low_blocks)[1:]
    if ride:
        late_riders = pack_riders(late_vectors, 128, deep, sum(first_widths))
    first_keep, first_give = split_grads(first_part, first_widths, 1, late_riders, "split_first")
    first_other = swap_blocks(first_give)
    left, first_keep, unused = regroup(left, first_keep, [()])
    first_blocks = add_blocks(first_keep, first_other)
    first_left = sum_direct(first_blocks)
    first_left, unused, second_moved = regroup(first_left, [], [tuple(second_moved)])
    first_own, first_moved = depth_sum(first_left)
    ends = first_left[0][0].shape[1], second_left[0][0].shape[1]
    first_shard = depth_rest(first_own, first_moved, ends[0], RIDER_LINES if ride else 0)
    second_shard = depth_rest(second_own, second_moved, ends[1], RIDER_LINES if ride else 0)
    pair = [summed([part[h] for part in left]) for h in range(2)]
    input_pair = [
        input_own[h * own_rows : (h + 1) * own_rows]
        + input_part[h * own_rows : (h + 1) * own_rows]
        + pair[h][:own_rows]
        for h in range(2)
    ]
    memory_pair = [
        memory_own[h * own_memory : (h + 1) * own_memory] + pair[h][own_rows:] for h in range(2)
    ]

    def restore(pair):
        other = swap(pair[1])
        return jnp.where(
            core == 0, jnp.stack([pair[0], other]), jnp.stack([other, pair[0]])
        )

    output_result = restore([outputs[:own_rows], outputs[own_rows:]])
    input_result = restore(input_pair)
    memory_result = restore(memory_pair)

    vectors = late_vectors + early_vectors
    lengths = [v.shape[0] for v in vectors]
    if ride:
        first_shard, late_lines = first_shard
        second_shard, early_lines = second_shard
        split = unpack_riders(late_lines, 128, lengths[:2])
        split += unpack_riders(early_lines, 512, lengths[2:])
    else:
        joined = all_sum(jnp.concatenate(vectors), ("fsdp", "tp", "ctx"))
        starts = column_starts(lengths)
        split = [joined[start : start + size] for start, size in zip(starts, lengths)]

    def shards(packed, widths):
        start = 0
        parts = []
        for one in widths:
            parts.append(packed[:, start : start + one])
            start += one
        return parts

    g_query, g_key, g_value = shards(first_shard, first_widths)
    (
        g_cross_key,
        g_cross_value,
        g_output,
        g_cross_query,
        g_cross_output,
        g_expand,
        g_reduce,
    ) = shards(second_shard, second_widths)
    return (
        output_result,
        input_result,
        memory_result,
        g_query,
        g_key,
        g_value,
        g_output.T,
        g_cross_query,
        g_cross_key,
        g_cross_value,
        g_cross_output.T,
        g_expand,
        g_reduce.T,
        *split,
    )


def solution(mesh):
    rows = P("fsdp", ("ctx", "tp"), None)
    tall = P(("fsdp", "ctx"), "tp")
    flat = P("tp", ("fsdp", "ctx"))
    weights = (tall, tall, tall, flat, tall, tall, tall, flat, tall, flat)
    return jax.shard_map(
        per_device,
        mesh=mesh,
        in_specs=(rows, rows, rows, P("fsdp", None), P("fsdp"), P("fsdp"))
        + weights
        + (P(),) * 14,
        out_specs=(rows, rows, rows) + weights + (P(),) * 14,
        check_vma=False,
    )
```

```python
import functools

import jax
import jax.numpy as jnp
from jax import lax
from jax.experimental import pallas as pl
from jax.experimental.pallas import tpu as pltpu
from jax.sharding import PartitionSpec as P

HEAD_DIM = 64
EPSILON = 1e-05
NEGATIVE = -1e30
F32 = jnp.float32
BF16 = jnp.bfloat16
SCALE = HEAD_DIM ** -0.5
VMEM_BYTES = 58 * 2 ** 20


def contract(left, right, left_dim, right_dim):
    return lax.dot_general(
        left, right, (((left_dim,), (right_dim,)), ((), ())), preferred_element_type=F32
    )


def product(left, right):
    return contract(left, right, 1, 0)


def product_left(left, right):
    return contract(left, right, 0, 0)


def product_right(left, right):
    return contract(left, right, 1, 1)


def layer_norm(values, gain, shift):
    center = values - jnp.mean(values, axis=-1, keepdims=True)
    spread = jnp.mean(center * center, axis=-1, keepdims=True)
    return center * lax.rsqrt(spread + EPSILON) * gain + shift


def norm_back(values, gain, grad):
    center = values - jnp.mean(values, axis=-1, keepdims=True)
    spread = jnp.mean(center * center, axis=-1, keepdims=True)
    rate = lax.rsqrt(spread + EPSILON)
    normal = center * rate
    scaled = grad * gain
    back = rate * (
        scaled
        - jnp.mean(scaled, axis=-1, keepdims=True)
        - normal * jnp.mean(scaled * normal, axis=-1, keepdims=True)
    )
    return back, jnp.sum(grad * normal, axis=0), jnp.sum(grad, axis=0)


def attend_kernel(heads, q, k, v, qp, kp, *refs):
    out, exact, weights = refs[-3:]
    allowed = kp[...] <= qp[...]
    for head in range(heads):
        cols = slice(head * HEAD_DIM, (head + 1) * HEAD_DIM)
        scores = contract(k[:, cols], q[:, cols] * SCALE, 1, 1)
        scores = jnp.where(allowed, scores, NEGATIVE)
        largest = jnp.max(scores, axis=0, keepdims=True)
        power = jnp.exp(scores - largest)
        rate = 1.0 / jnp.sum(power, axis=0, keepdims=True)
        low = (power * rate).astype(BF16)
        weights[head] = low
        mixed = contract(v[:, cols], low, 0, 0)
        exact[cols, :] = mixed
        out[:, cols] = mixed.T.astype(BF16)


def attend_back_kernel(heads, q, k, v, weights, exact, grad, *refs):
    dq, dk, dv, dq_sum, dv_sum = refs[-5:]
    for head in range(heads):
        cols = slice(head * HEAD_DIM, (head + 1) * HEAD_DIM)
        grads = grad[:, cols].astype(F32).T
        inner = jnp.sum(grads * exact[cols, :], axis=0, keepdims=True)
        weight = weights[head]
        grad_weight = contract(v[:, cols], grad[:, cols], 1, 1)
        grad_scores = (weight.astype(F32) * (grad_weight - inner)).astype(BF16)
        low = (contract(k[:, cols], grad_scores, 0, 0) * SCALE).T.astype(BF16)
        dq[:, cols] = low
        dq_sum[:, cols] = jnp.sum(low.astype(F32), axis=0, keepdims=True)
        low = contract(weight, grad[:, cols], 1, 0).astype(BF16)
        dv[:, cols] = low
        dv_sum[:, cols] = jnp.sum(low.astype(F32), axis=0, keepdims=True)
        dk[:, cols] = (contract(grad_scores, q[:, cols], 1, 0) * SCALE).astype(BF16)


HEADS_PER_STEP = 2


def attend_call(body, arrays, specs, shapes, out_specs, earlier, each, steps, cost, name):
    given = [] if earlier is None else list(earlier)
    return pl.pallas_call(
        functools.partial(body, each),
        grid=(steps,),
        in_specs=specs + [pl.BlockSpec(memory_space=pl.ANY)] * len(given),
        out_specs=out_specs,
        out_shape=shapes,
        input_output_aliases={len(arrays) + i: i for i in range(len(given))},
        compiler_params=pltpu.CompilerParams(vmem_limit_bytes=VMEM_BYTES),
        cost_estimate=cost,
        name=name,
    )(*arrays, *given)


def head_specs(first, each):
    def columns(rows):
        return pl.BlockSpec((rows, each * HEAD_DIM), lambda i: (0, i + first))

    def lines(rows):
        return pl.BlockSpec((each * HEAD_DIM, rows), lambda i: (i + first, 0))

    def heads(*dims):
        return pl.BlockSpec((each,) + dims, lambda i: (i + first, 0, 0))

    return columns, lines, heads


def attend(q, k, v, qp, kp, part=0, parts=1, earlier=None):
    rows, width = q.shape
    keys = k.shape[0]
    heads = width // HEAD_DIM
    each = HEADS_PER_STEP
    steps = heads // each // parts
    columns, lines, by_head = head_specs(part * steps, each)
    return attend_call(
        attend_kernel,
        (q, k, v, qp, kp),
        [
            columns(rows),
            columns(keys),
            columns(keys),
            pl.BlockSpec((1, rows), lambda i: (0, 0)),
            pl.BlockSpec((keys, 1), lambda i: (0, 0)),
        ],
        [
            jax.ShapeDtypeStruct((rows, width), BF16),
            jax.ShapeDtypeStruct((width, rows), F32),
            jax.ShapeDtypeStruct((heads, keys, rows), BF16),
        ],
        [columns(rows), lines(rows), by_head(keys, rows)],
        earlier,
        each,
        steps,
        pl.CostEstimate(
            flops=16 * rows * keys * width // parts,
            transcendentals=heads * rows * keys // parts,
            bytes_accessed=2 * heads * rows * keys // parts,
        ),
        "attend",
    )


def attend_back(q, k, v, weights, exact, grad, part=0, parts=1, earlier=None):
    rows, width = q.shape
    keys = k.shape[0]
    heads = width // HEAD_DIM
    each = HEADS_PER_STEP
    steps = heads // each // parts
    columns, lines, by_head = head_specs(part * steps, each)
    return attend_call(
        attend_back_kernel,
        (q, k, v, weights, exact, grad),
        [
            columns(rows),
            columns(keys),
            columns(keys),
            by_head(keys, rows),
            lines(rows),
            columns(rows),
        ],
        [
            jax.ShapeDtypeStruct((rows, width), BF16),
            jax.ShapeDtypeStruct((keys, width), BF16),
            jax.ShapeDtypeStruct((keys, width), BF16),
            jax.ShapeDtypeStruct((1, width), F32),
            jax.ShapeDtypeStruct((1, width), F32),
        ],
        [columns(rows), columns(keys), columns(keys), columns(1), columns(1)],
        earlier,
        each,
        steps,
        pl.CostEstimate(
            flops=32 * rows * keys * width // parts,
            transcendentals=0,
            bytes_accessed=2 * heads * rows * keys // parts,
        ),
        "attend_back",
    )


def move(sources, shapes, plan, name):
    def body(*refs):
        given = refs[: len(sources)]
        made = refs[len(sources) : len(sources) + len(shapes)]
        sems = refs[-1]
        copies = []
        for at, (i, a, j, b) in enumerate(plan()):
            copies.append(pltpu.make_async_copy(given[i].at[a], made[j].at[b], sems.at[at]))
        for copy in copies:
            copy.start()
        for copy in copies:
            copy.wait()

    count = move_count(plan)
    return pl.pallas_call(
        body,
        in_specs=[pl.BlockSpec(memory_space=pl.ANY)] * len(sources),
        out_specs=[pl.BlockSpec(memory_space=pltpu.VMEM)] * len(shapes),
        out_shape=[jax.ShapeDtypeStruct(shape, BF16) for shape in shapes],
        scratch_shapes=[pltpu.SemaphoreType.DMA((count,))],
        compiler_params=pltpu.CompilerParams(vmem_limit_bytes=VMEM_BYTES),
        name=name,
    )(*sources)


def move_count(plan):
    return len(plan())


def sizes():
    return lax.axis_size("fsdp"), lax.axis_size("ctx"), lax.axis_size("tp") // 2


def places():
    tp = lax.axis_index("tp")
    return lax.axis_index("fsdp"), lax.axis_index("ctx"), tp // 2, tp % 2


def swap(value):
    total = lax.axis_size("tp")
    return lax.ppermute(value, "tp", [(i, i ^ 1) for i in range(total)])


def shift_x(value, step):
    total = lax.axis_size("tp")
    return lax.ppermute(value, "tp", [(i, (i + 2 * step) % total) for i in range(total)])


def shift(value, axis, step):
    total = lax.axis_size(axis)
    return lax.ppermute(value, axis, [(i, (i + step) % total) for i in range(total)])


def offsets():
    unused, high, wide = sizes()
    return [(dx, dy) for dy in range(high) for dx in range(wide)]


def is_square():
    unused, high, wide = sizes()
    return high == 2 and wide == 2


def shift_plane(value, dx, dy):
    high, total = lax.axis_size("ctx"), lax.axis_size("tp")
    pairs = [
        (c * total + t, (c + dy) % high * total + (t + 2 * dx) % total)
        for c in range(high)
        for t in range(total)
    ]
    return lax.ppermute(value, ("ctx", "tp"), pairs)


def plane_direct(value):
    return [(value,)] + [(shift_plane(value, dx, dy),) for dx, dy in offsets()[1:]]


def sum_direct(blocks):
    moved = [(shift_plane(b[0], -dx, -dy),) for b, (dx, dy) in zip(blocks[1:], offsets()[1:])]
    return [blocks[0]] + moved


def plane_one(first, second):
    if is_square():
        side = (shift_x(first, 1), shift_x(second, 1))
        front = (shift(first, "ctx", 1), shift(second, "ctx", 1))
        return [(first, second), side, front]
    unused, high, wide = sizes()
    row = [(first, second)] + [(shift_x(first, k), shift_x(second, k)) for k in range(1, wide)]
    blocks = list(row)
    for step in range(1, high):
        blocks += [(shift(a, "ctx", step), shift(b, "ctx", step)) for a, b in row]
    return blocks


def plane_two(blocks):
    if is_square():
        own, side, front = blocks
        return [own, side, front, (shift(side[0], "ctx", 1), shift_x(front[1], 1))]
    return blocks


def add(left, right):
    return (left.astype(F32) + right.astype(F32)).astype(BF16)


def add_kernel(*refs):
    count = len(refs) // 3
    for n in range(count):
        total = refs[n][...].astype(F32) + refs[count + n][...].astype(F32)
        refs[2 * count + n][...] = total.astype(BF16)


def add_many(left, right):
    steps = left[0].shape[0]
    if sum(part.size for part in left) < 2**20:
        steps = 1

    def spec(part):
        rest = part.shape[1:]
        return pl.BlockSpec((part.shape[0] // steps,) + rest, lambda i: (i,) + (0,) * len(rest))

    return pl.pallas_call(
        add_kernel,
        grid=(steps,),
        in_specs=[spec(part) for part in left] * 2,
        out_specs=[spec(part) for part in left],
        out_shape=[jax.ShapeDtypeStruct(part.shape, BF16) for part in left],
        name="add_many",
    )(*left, *right)


def sum_one(blocks):
    if is_square():
        own, side, front, far = blocks
        return [own, side, front, (shift(far[0], "ctx", 1), shift_x(far[1], 1))]
    return blocks


def sum_adds(blocks):
    if is_square():
        own, side, front, far = blocks
        first, second = add_many([side[0], front[1]], [far[0], far[1]])
        return [own, (first, side[1]), (front[0], second)]
    return blocks


def sum_two(blocks):
    if is_square():
        own, side, front = blocks
        from_side = (shift_x(side[0], 1), shift_x(side[1], 1))
        from_front = (shift(front[0], "ctx", 1), shift(front[1], "ctx", 1))
        return [own, from_side, from_front]
    unused, high, wide = sizes()
    row = []
    for dx in range(wide):
        total = blocks[dx]
        for dy in range(1, high):
            other = blocks[dy * wide + dx]
            total = tuple(add(a, shift(b, "ctx", -dy)) for a, b in zip(total, other))
        row.append(total)
    return [row[0]] + [
        (shift_x(row[dx][0], -dx), shift_x(row[dx][1], -dx)) for dx in range(1, wide)
    ]


def summed(parts):
    return sum(part.astype(F32) for part in parts)


def spread(packed):
    return [packed] + [shift(packed, "fsdp", k) for k in range(1, lax.axis_size("fsdp"))]


def depth_blocks(pieces, cuts, name):
    deep = len(pieces)
    rows, total = pieces[0].shape
    half = rows // cuts

    def by_depth():
        at = lax.axis_index("fsdp")
        steps = []
        for k in range(deep):
            for h in range(cuts):
                steps.append((k, slice(h * half, (h + 1) * half), h, (at - k + deep) % deep))
        return steps

    return move(pieces, [(deep, half, total)] * cuts, by_depth, name)


def aligned(widths):
    return all(width % 128 == 0 for width in widths)


def column_starts(widths):
    return [sum(widths[:i]) for i in range(len(widths))]


def block_place(n, who):
    unused, high, wide = sizes()
    unused, y, x, core = places()
    dx, dy = offsets()[n]
    at_y = (y - dy + high) % high
    at_x = (x - dx + wide) % wide
    return at_y, 2 * at_x + (core if who == 0 else 1 - core)


def whole_weights(blocks, widths, name):
    deep, high, wide = sizes()
    half, total = blocks[0][0].shape[1:]
    cuts = len(blocks[0])
    rows = cuts * half
    others = [tuple(swap(part) for part in block) for block in blocks]
    starts = column_starts(widths)
    if aligned(widths):

        def into_place():
            steps = []
            for n in range(len(blocks)):
                for who in range(2):
                    at_y, at = block_place(n, who)
                    for h in range(cuts):
                        lines = slice(h * half, (h + 1) * half)
                        for j, width in enumerate(widths):
                            cols = slice(starts[j], starts[j] + width)
                            here = pl.ds(pl.multiple_of(at * width, 128), width)
                            steps.append(
                                (
                                    (cuts * n + h) + cuts * len(blocks) * who,
                                    (slice(None), slice(None), cols),
                                    j,
                                    (slice(None), at_y, lines, here),
                                )
                            )
            return steps

        made = move(
            [part for block in blocks + others for part in block],
            [(deep, high, rows, 2 * wide * width) for width in widths],
            into_place,
            name,
        )
        return [m.reshape(deep * high * rows, -1) for m in made]
    whole = jnp.zeros((high, 2 * wide, deep, rows, total), BF16)
    for n in range(len(blocks)):
        for who, part in ((0, blocks[n]), (1, others[n])):
            at = block_place(n, who) + (0, 0, 0)
            part = jnp.concatenate(part, axis=1)[None, None]
            whole = lax.dynamic_update_slice(whole, part, at)
    made = []
    for start, width in zip(starts, widths):
        part = whole[..., start : start + width]
        part = part.transpose(2, 0, 3, 1, 4)
        made.append(part.reshape(deep * high * rows, 2 * wide * width))
    return made


def split_grads(grads, widths, cuts, riders, name):
    deep, high, wide = sizes()
    rows = grads[0].shape[0] // (deep * high)
    half = rows // cuts
    total = sum(widths)
    count = len(offsets())
    starts = column_starts(widths)
    if aligned(widths):
        shaped = [g.reshape(deep, high, rows, 2 * wide * w) for g, w in zip(grads, widths)]

        def into_blocks():
            steps = []
            for n in range(count):
                for who in range(2):
                    at_y, at = block_place(n, who)
                    for h in range(cuts):
                        lines = slice(h * half, (h + 1) * half)
                        for j, width in enumerate(widths):
                            cols = slice(starts[j], starts[j] + width)
                            here = pl.ds(pl.multiple_of(at * width, 128), width)
                            steps.append(
                                (
                                    j,
                                    (slice(None), at_y, lines, here),
                                    cuts * (n + count * who) + h,
                                    (slice(None), lines_of(h), cols),
                                )
                            )
                        if h == 0 and riders is not None:
                            below = slice(half, half + riders.shape[1])
                            steps.append(
                                (
                                    len(widths),
                                    (slice(None), slice(None), slice(None)),
                                    cuts * (n + count * who),
                                    (slice(None), below, slice(None)),
                                )
                            )
            return steps

        def lines_of(h):
            return slice(0, half)

        sizes_made = [(deep, half, total)] * cuts
        if riders is not None:
            sizes_made[0] = (deep, half + riders.shape[1], total)
            shaped.append(riders)
        made = move(shaped, sizes_made * (2 * count), into_blocks, name)
        pairs = [tuple(made[cuts * n : cuts * (n + 1)]) for n in range(2 * count)]
        return pairs[:count], pairs[count:]
    whole = jnp.concatenate(
        [g.reshape(deep, high, rows, 2 * wide, w) for g, w in zip(grads, widths)], axis=-1
    ).transpose(1, 3, 0, 2, 4)

    def pick(n, who):
        at = block_place(n, who) + (0, 0, 0)
        part = lax.dynamic_slice(whole, at, (1, 1, deep, rows, total))[0, 0]
        return tuple(part[:, h * half : (h + 1) * half] for h in range(cuts))

    return [pick(n, 0) for n in range(count)], [pick(n, 1) for n in range(count)]


def swap_blocks(blocks):
    return [tuple(swap(part) for part in block) for block in blocks]


def add_blocks(blocks, others):
    made = add_many([a for x in blocks for a in x], [b for y in others for b in y])
    each = len(blocks[0])
    return [tuple(made[each * n : each * (n + 1)]) for n in range(len(blocks))]


def depth_sum(left):
    deep = lax.axis_size("fsdp")
    own = [summed([part[h] for part in left]) for h in range(len(left[0]))]
    own = jnp.concatenate(own, axis=1) if len(own) > 1 else own[0]
    low = own.astype(BF16)
    at = lax.axis_index("fsdp")
    result = lax.dynamic_index_in_dim(low, at, 0, keepdims=False).astype(F32)
    moved = []
    for k in range(1, deep):
        piece = lax.dynamic_index_in_dim(low, (at + k) % deep, 0, keepdims=False)
        moved.append(shift(piece, "fsdp", k))
    return result, moved


def depth_rest(result, moved, end, lines=0):
    result = result + summed(moved)
    if lines:
        rest = [result[: end - lines]] + ([result[end:]] if end < result.shape[0] else [])
        return jnp.concatenate(rest, axis=0), result[end - lines : end]
    return result


def after(value, *gates):
    return lax.optimization_barrier((value,) + gates)[0]


def gated(blocks, *gates):
    flat = [part for block in blocks for part in block]
    made = list(lax.optimization_barrier(tuple(flat) + gates))
    out = []
    for block in blocks:
        out.append(tuple(made[: len(block)]))
        made = made[len(block) :]
    return [out] + made


def regroup(first, second, third):
    made = gated(first + second + third)[0]
    at = len(first)
    return made[:at], made[at : at + len(second)], made[-1]


def row_grads_kernel(own_rows, own_memory, dk, dv, wk, wv, memory, own, own_mem, *blocks):
    n = pl.program_id(0)
    part = product_right(dk[...], wk[...]) + product_right(dv[...], wv[...])

    @pl.when(n == 0)
    def _():
        own[...] = part
        own_mem[...] = memory[...]

    for m in range(1, len(blocks) // 2 + 1):

        @pl.when(n == m)
        def _():
            for h in range(2):
                block = blocks[2 * (m - 1) + h]
                block[:own_rows] = part[h * own_rows : (h + 1) * own_rows].astype(BF16)
                lines = slice(h * own_memory, (h + 1) * own_memory)
                block[own_rows:] = memory[lines].astype(BF16)


def row_grads(dk, dv, wk, wv, memory, own_rows):
    count = len(offsets())
    width = wk.shape[0]
    own_memory = memory.shape[0] // (2 * count)

    def rows_of(size, columns):
        return pl.BlockSpec((size, columns), lambda n: (n, 0))

    def whole(*shape):
        return pl.BlockSpec(shape, lambda n: (0, 0))

    block = (own_rows + own_memory, width)
    own, own_mem, *blocks = pl.pallas_call(
        functools.partial(row_grads_kernel, own_rows, own_memory),
        grid=(count,),
        in_specs=[
            rows_of(2 * own_rows, dk.shape[1]),
            rows_of(2 * own_rows, dv.shape[1]),
            whole(*wk.shape),
            whole(*wv.shape),
            rows_of(2 * own_memory, width),
        ],
        out_specs=[whole(2 * own_rows, width), whole(2 * own_memory, width)]
        + [whole(*block)] * (2 * (count - 1)),
        out_shape=[
            jax.ShapeDtypeStruct((2 * own_rows, width), F32),
            jax.ShapeDtypeStruct((2 * own_memory, width), F32),
        ]
        + [jax.ShapeDtypeStruct(block, BF16)] * (2 * (count - 1)),
        compiler_params=pltpu.CompilerParams(vmem_limit_bytes=VMEM_BYTES),
        name="row_grads",
    )(dk, dv, wk, wv, memory)
    pairs = [(blocks[2 * n], blocks[2 * n + 1]) for n in range(count - 1)]
    return own, own_mem, [pairs[0]] + pairs


RIDER_LINES = 8


def pack_kernel(chunk, *refs):
    made = refs[-1]
    made[...] = jnp.zeros(made.shape, BF16)
    per_line = made.shape[2] // chunk
    at = 0
    for ref in refs[:-1]:
        for row in range(ref.shape[0]):
            for start in range(0, ref.shape[1], chunk):
                line, column = at // per_line, at % per_line * chunk
                value = ref[row : row + 1, start : start + chunk].astype(BF16)
                for copy in range(made.shape[0]):
                    made[copy, line : line + 1, column : column + chunk] = value
                at += 1


def pack_riders(vectors, chunk, deep, total):
    return pl.pallas_call(
        functools.partial(pack_kernel, chunk),
        out_shape=jax.ShapeDtypeStruct((deep, RIDER_LINES, total), BF16),
        name="pack_riders",
    )(*[v.reshape(-1, vectors[0].shape[0]) for v in vectors])


def unpack_riders(lines, chunk, lengths):
    per_line = lines.shape[1] // chunk
    flat = lines[:, : per_line * chunk].reshape(-1)
    starts = column_starts(lengths)
    return [flat[start : start + size] for start, size in zip(starts, lengths)]


def prologue_kernel(inputs, memory, *refs):
    weights, (keep, give, first, second) = refs[:10], refs[10:]
    core = lax.axis_index("tp") % 2
    rows = inputs.shape[1]
    keep[:rows] = inputs[core]
    keep[rows:] = memory[core]
    give[:rows] = inputs[1 - core]
    give[rows:] = memory[1 - core]
    for target, group in ((first, weights[:3]), (second, weights[3:])):
        start = 0
        for ref in group:
            target[:, start : start + ref.shape[1]] = ref[...]
            start += ref.shape[1]


def prologue(inputs, memory, weights):
    rows = weights[0].shape[0]
    widths = [w.shape[1] for w in weights]
    if not aligned(widths):
        core = lax.axis_index("tp") % 2
        both = jnp.concatenate([inputs, memory], axis=1)
        keep = lax.dynamic_index_in_dim(both, core, 0, keepdims=False)
        give = lax.dynamic_index_in_dim(both, 1 - core, 0, keepdims=False)
        return (
            keep,
            give,
            jnp.concatenate(weights[:3], axis=1),
            jnp.concatenate(weights[3:], axis=1),
        )
    block = (inputs.shape[1] + memory.shape[1], inputs.shape[2])
    return pl.pallas_call(
        prologue_kernel,
        out_shape=[
            jax.ShapeDtypeStruct(block, BF16),
            jax.ShapeDtypeStruct(block, BF16),
            jax.ShapeDtypeStruct((rows, sum(widths[:3])), BF16),
            jax.ShapeDtypeStruct((rows, sum(widths[3:])), BF16),
        ],
        compiler_params=pltpu.CompilerParams(vmem_limit_bytes=VMEM_BYTES),
        name="prologue",
    )(inputs, memory, *weights)


def all_sum(value, axes):
    for axis in axes:
        total = lax.axis_size(axis)
        step = 1
        while step < total:
            pairs = [(i, i ^ step) for i in range(total)]
            value = value + lax.ppermute(value, axis, pairs)
            step *= 2
    return value


def per_device(
    inputs,
    memory,
    cotangent,
    positions,
    lengths,
    memory_lengths,
    query_weight,
    key_weight,
    value_weight,
    output_weight,
    cross_query_weight,
    cross_key_weight,
    cross_value_weight,
    cross_output_weight,
    expand_weight,
    reduce_weight,
    query_bias,
    value_bias,
    output_bias,
    first_gain,
    first_shift,
    cross_query_bias,
    cross_value_bias,
    cross_output_bias,
    second_gain,
    second_shift,
    expand_bias,
    reduce_bias,
    third_gain,
    third_shift,
):
    deep, high, wide = sizes()
    z, y, x, core = places()
    own_rows, width = inputs.shape[1:]
    own_memory = memory.shape[1]
    rows = 2 * own_rows
    head_width = query_weight.shape[1]
    hidden_width = expand_weight.shape[1]

    keep, give, first_pack, second_pack = prologue(
        inputs,
        memory,
        [
            query_weight,
            key_weight,
            value_weight,
            cross_key_weight,
            cross_value_weight,
            output_weight.T,
            cross_query_weight,
            cross_output_weight.T,
            expand_weight,
            reduce_weight.T,
        ],
    )
    first_widths = [head_width] * 3
    second_widths = [head_width] * 5 + [hidden_width] * 2

    got = swap(give)
    first_pieces = spread(after(first_pack, got))
    blocks = plane_one(keep, got)
    first_depth = depth_blocks(first_pieces, 1, "stack_first")[0]
    positions = after(positions, first_depth)
    *blocks, (first_depth,) = gated(blocks + [(first_depth,)])[0]
    blocks = plane_two(blocks)
    first_blocks = plane_direct(first_depth)
    second_pieces = spread(after(second_pack, *first_pieces[1:]))
    cotangent_pair = (
        lax.dynamic_index_in_dim(cotangent, core, 0, keepdims=False),
        swap(lax.dynamic_index_in_dim(cotangent, 1 - core, 0, keepdims=False)),
    )
    full_query, full_key, full_value = whole_weights(first_blocks, first_widths, "place_first")
    pieces = [p for b in blocks for p in b]

    def rows_together():
        steps = []
        for n in range(len(pieces)):
            at = n * own_rows
            steps.append((n, slice(0, own_rows), 0, slice(at, at + own_rows)))
            at = n * own_memory
            steps.append(
                (n, slice(own_rows, own_rows + own_memory), 1, slice(at, at + own_memory))
            )
        return steps

    wide_rows, wide_memory = move(
        pieces,
        [(len(pieces) * own_rows, width), (len(pieces) * own_memory, width)],
        rows_together,
        "rows_together",
    )
    rows_in = wide_rows[:rows]
    second_blocks = plane_direct(
        depth_blocks([after(p, wide_rows) for p in second_pieces], 1, "stack_second")[0]
    )

    slots = lax.dynamic_index_in_dim(positions, core, 0, keepdims=False)
    length = lax.dynamic_index_in_dim(lengths, core, 0, keepdims=False)
    memory_length = lax.dynamic_index_in_dim(memory_lengths, core, 0, keepdims=False)
    key_positions = []
    memory_slots = []
    for dx, dy in offsets():
        at_y = (y - dy + high) % high
        at_x = (x - dx + wide) % wide
        for who in (core, 1 - core):
            block = (at_y * wide + at_x) * 2 + who
            key_positions.append(lax.dynamic_slice_in_dim(slots, block * own_rows, own_rows))
            memory_slots.append(block * own_memory + jnp.arange(own_memory, dtype=jnp.int32))
    own_positions = jnp.concatenate(key_positions[:2])
    key_positions = jnp.concatenate(key_positions)
    last = positions.shape[1]
    key_positions = jnp.where(key_positions < length, key_positions, last)[:, None]
    query_positions = own_positions[None, :]
    memory_slots = jnp.concatenate(memory_slots)[:, None]
    memory_limit = jnp.broadcast_to(memory_length - 1, (1, rows))

    query_low = (product(rows_in, full_query) + query_bias).astype(BF16)
    keys = product(wide_rows, full_key).astype(BF16)
    values = (product(wide_rows, full_value) + value_bias).astype(BF16)
    attended, attended_exact, weights = attend(
        query_low, keys, values, query_positions, key_positions
    )
    second_blocks, attended = gated(second_blocks, attended)
    (
        full_cross_key,
        full_cross_value,
        full_output,
        full_cross_query,
        full_cross_output,
        full_expand,
        full_reduce,
    ) = whole_weights(second_blocks, second_widths, "place_second")
    memory_key = product(wide_memory, full_cross_key).astype(BF16)
    memory_value = (product(wide_memory, full_cross_value) + cross_value_bias).astype(BF16)

    first_in = rows_in.astype(F32) + product_right(attended, full_output) + output_bias
    first_out = layer_norm(first_in, first_gain, first_shift)
    first_low = first_out.astype(BF16)
    cross_query = (product(first_low, full_cross_query) + cross_query_bias).astype(BF16)
    cross_attended, cross_exact, cross_weights = attend(
        cross_query, memory_key, memory_value, memory_limit, memory_slots
    )
    second_in = first_out + product_right(cross_attended, full_cross_output) + cross_output_bias
    second_out = layer_norm(second_in, second_gain, second_shift)
    second_low = second_out.astype(BF16)
    expanded = product(second_low, full_expand) + expand_bias
    gate = jax.nn.sigmoid(expanded)
    activated = (expanded * gate).astype(BF16)
    third_in = second_out + product_right(activated, full_reduce) + reduce_bias
    outputs = layer_norm(third_in, third_gain, third_shift)

    grad_in = jnp.concatenate(cotangent_pair, axis=0).astype(F32)
    masked_grad = jnp.where((own_positions < length)[:, None], grad_in, 0.0)
    third_grad, third_gain_part, third_shift_part = norm_back(third_in, third_gain, masked_grad)
    third_low = third_grad.astype(BF16)
    activated_grad = product(third_low, full_reduce)
    expanded_grad = (activated_grad * gate * (1.0 + expanded * (1.0 - gate))).astype(BF16)
    third_part = [
        product_left(second_low, expanded_grad).astype(BF16),
        product_left(third_low, activated).astype(BF16),
    ]
    second_grad = third_grad + product_right(expanded_grad, full_expand)
    second_in_grad, second_gain_part, second_shift_part = norm_back(
        second_in, second_gain, second_grad
    )
    second_grad_low = second_in_grad.astype(BF16)
    cross_attended_grad = product(second_grad_low, full_cross_output).astype(BF16)
    cross_query_grad, memory_key_grad, memory_value_grad, *cross_sums = attend_back(
        cross_query,
        memory_key,
        memory_value,
        cross_weights,
        cross_exact,
        cross_attended_grad,
    )
    first_grad = second_in_grad + product_right(cross_query_grad, full_cross_query)
    first_in_grad, first_gain_part, first_shift_part = norm_back(first_in, first_gain, first_grad)
    first_grad_low = first_in_grad.astype(BF16)
    attended_grad = product(first_grad_low, full_output).astype(BF16)
    second_part = [
        product_left(wide_memory, memory_key_grad).astype(BF16),
        product_left(wide_memory, memory_value_grad).astype(BF16),
        product_left(first_grad_low, attended).astype(BF16),
        product_left(first_low, cross_query_grad).astype(BF16),
        product_left(second_grad_low, cross_attended).astype(BF16),
    ]
    early_vectors = [
        jnp.sum(first_in_grad, axis=0),
        first_gain_part,
        first_shift_part,
        cross_sums[0].reshape(-1),
        cross_sums[1].reshape(-1),
        jnp.sum(second_in_grad, axis=0),
        second_gain_part,
        second_shift_part,
        jnp.sum(expanded_grad.astype(F32), axis=0),
        jnp.sum(third_grad, axis=0),
        third_gain_part,
        third_shift_part,
    ]
    ride = aligned(first_widths + second_widths) and rows % 256 == 0
    early_riders = late_riders = None
    if ride:
        early_riders = pack_riders(early_vectors, 512, deep, sum(second_widths))
    second_keep, second_give = split_grads(
        second_part + third_part, second_widths, 2, early_riders, "split_second"
    )
    second_other = swap_blocks(second_give)
    memory_part = product_right(memory_key_grad, full_cross_key) + product_right(
        memory_value_grad, full_cross_value
    )

    second_blocks = add_blocks(second_keep, second_other)
    second_blocks, early_grad = gated(second_blocks, attended_grad)
    second_blocks = sum_one(second_blocks)
    early = list(
        attend_back(query_low, keys, values, weights, attended_exact, early_grad, 0, 2)
    )
    second_blocks, early[0] = gated(second_blocks, early[0])
    second_blocks = sum_adds(second_blocks)
    second_blocks, late_grad = gated(second_blocks, attended_grad)
    second_left = sum_two(second_blocks)
    query_grad, key_grad, value_grad, *self_sums = attend_back(
        query_low, keys, values, weights, attended_exact, late_grad, 1, 2, early
    )
    input_part, memory_own, low_blocks = row_grads(
        key_grad, value_grad, full_key, full_value, memory_part, own_rows
    )
    low_blocks, second_left, (query_late, key_late, value_late) = regroup(
        low_blocks, second_left, [(query_grad, key_grad, value_grad)]
    )
    low_blocks = sum_one(low_blocks)
    second_own, second_moved = depth_sum(second_left)
    input_own = first_in_grad + product_right(query_late, full_query)
    first_part = [
        product_left(rows_in, query_late).astype(BF16),
        product_left(wide_rows, key_late).astype(BF16),
        product_left(wide_rows, value_late).astype(BF16),
    ]
    late_vectors = [self_sums[0].reshape(-1), self_sums[1].reshape(-1)]
    low_blocks = sum_adds(low_blocks)
    low_blocks, unused, first_part = regroup(low_blocks, [], [tuple(first_part)])
    left = sum_two(low_blocks)[1:]
    if ride:
        late_riders = pack_riders(late_vectors, 128, deep, sum(first_widths))
    first_keep, first_give = split_grads(first_part, first_widths, 1, late_riders, "split_first")
    first_other = swap_blocks(first_give)
    left, first_keep, unused = regroup(left, first_keep, [()])
    first_blocks = add_blocks(first_keep, first_other)
    first_left = sum_direct(first_blocks)
    first_left, unused, second_moved = regroup(first_left, [], [tuple(second_moved)])
    first_own, first_moved = depth_sum(first_left)
    ends = first_left[0][0].shape[1], second_left[0][0].shape[1]
    first_shard = depth_rest(first_own, first_moved, ends[0], RIDER_LINES if ride else 0)
    second_shard = depth_rest(second_own, second_moved, ends[1], RIDER_LINES if ride else 0)
    pair = [summed([part[h] for part in left]) for h in range(2)]
    input_pair = [
        input_own[h * own_rows : (h + 1) * own_rows]
        + input_part[h * own_rows : (h + 1) * own_rows]
        + pair[h][:own_rows]
        for h in range(2)
    ]
    memory_pair = [
        memory_own[h * own_memory : (h + 1) * own_memory] + pair[h][own_rows:] for h in range(2)
    ]

    def restore(pair):
        other = swap(pair[1])
        return jnp.where(
            core == 0, jnp.stack([pair[0], other]), jnp.stack([other, pair[0]])
        )

    output_result = restore([outputs[:own_rows], outputs[own_rows:]])
    input_result = restore(input_pair)
    memory_result = restore(memory_pair)

    vectors = late_vectors + early_vectors
    lengths = [v.shape[0] for v in vectors]
    if ride:
        first_shard, late_lines = first_shard
        second_shard, early_lines = second_shard
        split = unpack_riders(late_lines, 128, lengths[:2])
        split += unpack_riders(early_lines, 512, lengths[2:])
    else:
        joined = all_sum(jnp.concatenate(vectors), ("fsdp", "tp", "ctx"))
        starts = column_starts(lengths)
        split = [joined[start : start + size] for start, size in zip(starts, lengths)]

    def shards(packed, widths):
        start = 0
        parts = []
        for one in widths:
            parts.append(packed[:, start : start + one])
            start += one
        return parts

    g_query, g_key, g_value = shards(first_shard, first_widths)
    (
        g_cross_key,
        g_cross_value,
        g_output,
        g_cross_query,
        g_cross_output,
        g_expand,
        g_reduce,
    ) = shards(second_shard, second_widths)
    return (
        output_result,
        input_result,
        memory_result,
        g_query,
        g_key,
        g_value,
        g_output.T,
        g_cross_query,
        g_cross_key,
        g_cross_value,
        g_cross_output.T,
        g_expand,
        g_reduce.T,
        *split,
    )


def solution(mesh):
    rows = P("fsdp", ("ctx", "tp"), None)
    tall = P(("fsdp", "ctx"), "tp")
    flat = P("tp", ("fsdp", "ctx"))
    weights = (tall, tall, tall, flat, tall, tall, tall, flat, tall, flat)
    return jax.shard_map(
        per_device,
        mesh=mesh,
        in_specs=(rows, rows, rows, P("fsdp", None), P("fsdp"), P("fsdp"))
        + weights
        + (P(),) * 14,
        out_specs=(rows, rows, rows) + weights + (P(),) * 14,
        check_vma=False,
    )
```

```python
import functools

import jax
import jax.numpy as jnp
from jax import lax
from jax.experimental import pallas as pl
from jax.experimental.pallas import tpu as pltpu
from jax.sharding import PartitionSpec as P

HEAD_DIM = 64
EPSILON = 1e-05
NEGATIVE = -1e30
F32 = jnp.float32
BF16 = jnp.bfloat16
SCALE = HEAD_DIM ** -0.5
VMEM_BYTES = 58 * 2 ** 20


def contract(left, right, left_dim, right_dim):
    return lax.dot_general(
        left, right, (((left_dim,), (right_dim,)), ((), ())), preferred_element_type=F32
    )


def product(left, right):
    return contract(left, right, 1, 0)


def product_left(left, right):
    return contract(left, right, 0, 0)


def product_right(left, right):
    return contract(left, right, 1, 1)


def layer_norm(values, gain, shift):
    center = values - jnp.mean(values, axis=-1, keepdims=True)
    spread = jnp.mean(center * center, axis=-1, keepdims=True)
    return center * lax.rsqrt(spread + EPSILON) * gain + shift


def norm_back(values, gain, grad):
    center = values - jnp.mean(values, axis=-1, keepdims=True)
    spread = jnp.mean(center * center, axis=-1, keepdims=True)
    rate = lax.rsqrt(spread + EPSILON)
    normal = center * rate
    scaled = grad * gain
    back = rate * (
        scaled
        - jnp.mean(scaled, axis=-1, keepdims=True)
        - normal * jnp.mean(scaled * normal, axis=-1, keepdims=True)
    )
    return back, jnp.sum(grad * normal, axis=0), jnp.sum(grad, axis=0)


def attend_kernel(heads, q, k, v, qp, kp, *refs):
    out, exact, weights = refs[-3:]
    allowed = kp[...] <= qp[...]
    for head in range(heads):
        cols = slice(head * HEAD_DIM, (head + 1) * HEAD_DIM)
        scores = contract(k[:, cols], q[:, cols] * SCALE, 1, 1)
        scores = jnp.where(allowed, scores, NEGATIVE)
        largest = jnp.max(scores, axis=0, keepdims=True)
        power = jnp.exp(scores - largest)
        rate = 1.0 / jnp.sum(power, axis=0, keepdims=True)
        low = (power * rate).astype(BF16)
        weights[head] = low
        mixed = contract(v[:, cols], low, 0, 0)
        exact[cols, :] = mixed
        out[:, cols] = mixed.T.astype(BF16)


def attend_back_kernel(heads, q, k, v, weights, exact, grad, *refs):
    dq, dk, dv, dq_sum, dv_sum = refs[-5:]
    for head in range(heads):
        cols = slice(head * HEAD_DIM, (head + 1) * HEAD_DIM)
        grads = grad[:, cols].astype(F32).T
        inner = jnp.sum(grads * exact[cols, :], axis=0, keepdims=True)
        weight = weights[head]
        grad_weight = contract(v[:, cols], grad[:, cols], 1, 1)
        grad_scores = (weight.astype(F32) * (grad_weight - inner)).astype(BF16)
        low = (contract(k[:, cols], grad_scores, 0, 0) * SCALE).T.astype(BF16)
        dq[:, cols] = low
        dq_sum[:, cols] = jnp.sum(low.astype(F32), axis=0, keepdims=True)
        low = contract(weight, grad[:, cols], 1, 0).astype(BF16)
        dv[:, cols] = low
        dv_sum[:, cols] = jnp.sum(low.astype(F32), axis=0, keepdims=True)
        dk[:, cols] = (contract(grad_scores, q[:, cols], 1, 0) * SCALE).astype(BF16)


HEADS_PER_STEP = 2


def attend_call(body, arrays, specs, shapes, out_specs, earlier, each, steps, cost, name):
    given = [] if earlier is None else list(earlier)
    return pl.pallas_call(
        functools.partial(body, each),
        grid=(steps,),
        in_specs=specs + [pl.BlockSpec(memory_space=pl.ANY)] * len(given),
        out_specs=out_specs,
        out_shape=shapes,
        input_output_aliases={len(arrays) + i: i for i in range(len(given))},
        compiler_params=pltpu.CompilerParams(vmem_limit_bytes=VMEM_BYTES),
        cost_estimate=cost,
        name=name,
    )(*arrays, *given)


def head_specs(first, each):
    def columns(rows):
        return pl.BlockSpec((rows, each * HEAD_DIM), lambda i: (0, i + first))

    def lines(rows):
        return pl.BlockSpec((each * HEAD_DIM, rows), lambda i: (i + first, 0))

    def heads(*dims):
        return pl.BlockSpec((each,) + dims, lambda i: (i + first, 0, 0))

    return columns, lines, heads


def attend(q, k, v, qp, kp, part=0, parts=1, earlier=None):
    rows, width = q.shape
    keys = k.shape[0]
    heads = width // HEAD_DIM
    each = HEADS_PER_STEP
    steps = heads // each // parts
    columns, lines, by_head = head_specs(part * steps, each)
    return attend_call(
        attend_kernel,
        (q, k, v, qp, kp),
        [
            columns(rows),
            columns(keys),
            columns(keys),
            pl.BlockSpec((1, rows), lambda i: (0, 0)),
            pl.BlockSpec((keys, 1), lambda i: (0, 0)),
        ],
        [
            jax.ShapeDtypeStruct((rows, width), BF16),
            jax.ShapeDtypeStruct((width, rows), F32),
            jax.ShapeDtypeStruct((heads, keys, rows), BF16),
        ],
        [columns(rows), lines(rows), by_head(keys, rows)],
        earlier,
        each,
        steps,
        pl.CostEstimate(
            flops=16 * rows * keys * width // parts,
            transcendentals=heads * rows * keys // parts,
            bytes_accessed=2 * heads * rows * keys // parts,
        ),
        "attend",
    )


def attend_back(q, k, v, weights, exact, grad, part=0, parts=1, earlier=None):
    rows, width = q.shape
    keys = k.shape[0]
    heads = width // HEAD_DIM
    each = HEADS_PER_STEP
    steps = heads // each // parts
    columns, lines, by_head = head_specs(part * steps, each)
    return attend_call(
        attend_back_kernel,
        (q, k, v, weights, exact, grad),
        [
            columns(rows),
            columns(keys),
            columns(keys),
            by_head(keys, rows),
            lines(rows),
            columns(rows),
        ],
        [
            jax.ShapeDtypeStruct((rows, width), BF16),
            jax.ShapeDtypeStruct((keys, width), BF16),
            jax.ShapeDtypeStruct((keys, width), BF16),
            jax.ShapeDtypeStruct((1, width), F32),
            jax.ShapeDtypeStruct((1, width), F32),
        ],
        [columns(rows), columns(keys), columns(keys), columns(1), columns(1)],
        earlier,
        each,
        steps,
        pl.CostEstimate(
            flops=32 * rows * keys * width // parts,
            transcendentals=0,
            bytes_accessed=2 * heads * rows * keys // parts,
        ),
        "attend_back",
    )


def move(sources, shapes, plan, name):
    def body(*refs):
        given = refs[: len(sources)]
        made = refs[len(sources) : len(sources) + len(shapes)]
        sems = refs[-1]
        copies = []
        for at, (i, a, j, b) in enumerate(plan()):
            copies.append(pltpu.make_async_copy(given[i].at[a], made[j].at[b], sems.at[at]))
        for copy in copies:
            copy.start()
        for copy in copies:
            copy.wait()

    count = move_count(plan)
    return pl.pallas_call(
        body,
        in_specs=[pl.BlockSpec(memory_space=pl.ANY)] * len(sources),
        out_specs=[pl.BlockSpec(memory_space=pltpu.VMEM)] * len(shapes),
        out_shape=[jax.ShapeDtypeStruct(shape, BF16) for shape in shapes],
        scratch_shapes=[pltpu.SemaphoreType.DMA((count,))],
        compiler_params=pltpu.CompilerParams(vmem_limit_bytes=VMEM_BYTES),
        name=name,
    )(*sources)


def move_count(plan):
    return len(plan())


def sizes():
    return lax.axis_size("fsdp"), lax.axis_size("ctx"), lax.axis_size("tp") // 2


def places():
    tp = lax.axis_index("tp")
    return lax.axis_index("fsdp"), lax.axis_index("ctx"), tp // 2, tp % 2


def swap(value):
    total = lax.axis_size("tp")
    return lax.ppermute(value, "tp", [(i, i ^ 1) for i in range(total)])


def shift_x(value, step):
    total = lax.axis_size("tp")
    return lax.ppermute(value, "tp", [(i, (i + 2 * step) % total) for i in range(total)])


def shift(value, axis, step):
    total = lax.axis_size(axis)
    return lax.ppermute(value, axis, [(i, (i + step) % total) for i in range(total)])


def offsets():
    unused, high, wide = sizes()
    return [(dx, dy) for dy in range(high) for dx in range(wide)]


def is_square():
    unused, high, wide = sizes()
    return high == 2 and wide == 2


def shift_plane(value, dx, dy):
    high, total = lax.axis_size("ctx"), lax.axis_size("tp")
    pairs = [
        (c * total + t, (c + dy) % high * total + (t + 2 * dx) % total)
        for c in range(high)
        for t in range(total)
    ]
    return lax.ppermute(value, ("ctx", "tp"), pairs)


def plane_direct(value):
    return [(value,)] + [(shift_plane(value, dx, dy),) for dx, dy in offsets()[1:]]


def sum_direct(blocks):
    moved = [(shift_plane(b[0], -dx, -dy),) for b, (dx, dy) in zip(blocks[1:], offsets()[1:])]
    return [blocks[0]] + moved


def plane_one(first, second):
    if is_square():
        side = (shift_x(first, 1), shift_x(second, 1))
        front = (shift(first, "ctx", 1), shift(second, "ctx", 1))
        return [(first, second), side, front]
    unused, high, wide = sizes()
    row = [(first, second)] + [(shift_x(first, k), shift_x(second, k)) for k in range(1, wide)]
    blocks = list(row)
    for step in range(1, high):
        blocks += [(shift(a, "ctx", step), shift(b, "ctx", step)) for a, b in row]
    return blocks


def plane_two(blocks):
    if is_square():
        own, side, front = blocks
        return [own, side, front, (shift(side[0], "ctx", 1), shift_x(front[1], 1))]
    return blocks


def add(left, right):
    return (left.astype(F32) + right.astype(F32)).astype(BF16)


def add_kernel(*refs):
    count = len(refs) // 3
    for n in range(count):
        total = refs[n][...].astype(F32) + refs[count + n][...].astype(F32)
        refs[2 * count + n][...] = total.astype(BF16)


def add_many(left, right):
    steps = max(1, left[0].shape[0] // 2)
    if sum(part.size for part in left) < 2**20:
        steps = 1

    def spec(part):
        rest = part.shape[1:]
        return pl.BlockSpec((part.shape[0] // steps,) + rest, lambda i: (i,) + (0,) * len(rest))

    return pl.pallas_call(
        add_kernel,
        grid=(steps,),
        in_specs=[spec(part) for part in left] * 2,
        out_specs=[spec(part) for part in left],
        out_shape=[jax.ShapeDtypeStruct(part.shape, BF16) for part in left],
        name="add_many",
    )(*left, *right)


def sum_one(blocks):
    if is_square():
        own, side, front, far = blocks
        return [own, side, front, (shift(far[0], "ctx", 1), shift_x(far[1], 1))]
    return blocks


def sum_adds(blocks):
    if is_square():
        own, side, front, far = blocks
        first, second = add_many([side[0], front[1]], [far[0], far[1]])
        return [own, (first, side[1]), (front[0], second)]
    return blocks


def sum_two(blocks):
    if is_square():
        own, side, front = blocks
        from_side = (shift_x(side[0], 1), shift_x(side[1], 1))
        from_front = (shift(front[0], "ctx", 1), shift(front[1], "ctx", 1))
        return [own, from_side, from_front]
    unused, high, wide = sizes()
    row = []
    for dx in range(wide):
        total = blocks[dx]
        for dy in range(1, high):
            other = blocks[dy * wide + dx]
            total = tuple(add(a, shift(b, "ctx", -dy)) for a, b in zip(total, other))
        row.append(total)
    return [row[0]] + [
        (shift_x(row[dx][0], -dx), shift_x(row[dx][1], -dx)) for dx in range(1, wide)
    ]


def summed(parts):
    return sum(part.astype(F32) for part in parts)


def spread(packed):
    return [packed] + [shift(packed, "fsdp", k) for k in range(1, lax.axis_size("fsdp"))]


def depth_blocks(pieces, cuts, name):
    deep = len(pieces)
    rows, total = pieces[0].shape
    half = rows // cuts

    def by_depth():
        at = lax.axis_index("fsdp")
        steps = []
        for k in range(deep):
            for h in range(cuts):
                steps.append((k, slice(h * half, (h + 1) * half), h, (at - k + deep) % deep))
        return steps

    return move(pieces, [(deep, half, total)] * cuts, by_depth, name)


def aligned(widths):
    return all(width % 128 == 0 for width in widths)


def column_starts(widths):
    return [sum(widths[:i]) for i in range(len(widths))]


def block_place(n, who):
    unused, high, wide = sizes()
    unused, y, x, core = places()
    dx, dy = offsets()[n]
    at_y = (y - dy + high) % high
    at_x = (x - dx + wide) % wide
    return at_y, 2 * at_x + (core if who == 0 else 1 - core)


def whole_weights(blocks, widths, name):
    deep, high, wide = sizes()
    half, total = blocks[0][0].shape[1:]
    cuts = len(blocks[0])
    rows = cuts * half
    others = [tuple(swap(part) for part in block) for block in blocks]
    starts = column_starts(widths)
    if aligned(widths):

        def into_place():
            steps = []
            for n in range(len(blocks)):
                for who in range(2):
                    at_y, at = block_place(n, who)
                    for h in range(cuts):
                        lines = slice(h * half, (h + 1) * half)
                        for j, width in enumerate(widths):
                            cols = slice(starts[j], starts[j] + width)
                            here = pl.ds(pl.multiple_of(at * width, 128), width)
                            steps.append(
                                (
                                    (cuts * n + h) + cuts * len(blocks) * who,
                                    (slice(None), slice(None), cols),
                                    j,
                                    (slice(None), at_y, lines, here),
                                )
                            )
            return steps

        made = move(
            [part for block in blocks + others for part in block],
            [(deep, high, rows, 2 * wide * width) for width in widths],
            into_place,
            name,
        )
        return [m.reshape(deep * high * rows, -1) for m in made]
    whole = jnp.zeros((high, 2 * wide, deep, rows, total), BF16)
    for n in range(len(blocks)):
        for who, part in ((0, blocks[n]), (1, others[n])):
            at = block_place(n, who) + (0, 0, 0)
            part = jnp.concatenate(part, axis=1)[None, None]
            whole = lax.dynamic_update_slice(whole, part, at)
    made = []
    for start, width in zip(starts, widths):
        part = whole[..., start : start + width]
        part = part.transpose(2, 0, 3, 1, 4)
        made.append(part.reshape(deep * high * rows, 2 * wide * width))
    return made


def split_grads(grads, widths, cuts, riders, name):
    deep, high, wide = sizes()
    rows = grads[0].shape[0] // (deep * high)
    half = rows // cuts
    total = sum(widths)
    count = len(offsets())
    starts = column_starts(widths)
    if aligned(widths):
        shaped = [g.reshape(deep, high, rows, 2 * wide * w) for g, w in zip(grads, widths)]

        def into_blocks():
            steps = []
            for n in range(count):
                for who in range(2):
                    at_y, at = block_place(n, who)
                    for h in range(cuts):
                        lines = slice(h * half, (h + 1) * half)
                        for j, width in enumerate(widths):
                            cols = slice(starts[j], starts[j] + width)
                            here = pl.ds(pl.multiple_of(at * width, 128), width)
                            steps.append(
                                (
                                    j,
                                    (slice(None), at_y, lines, here),
                                    cuts * (n + count * who) + h,
                                    (slice(None), lines_of(h), cols),
                                )
                            )
                        if h == 0 and riders is not None:
                            below = slice(half, half + riders.shape[1])
                            steps.append(
                                (
                                    len(widths),
                                    (slice(None), slice(None), slice(None)),
                                    cuts * (n + count * who),
                                    (slice(None), below, slice(None)),
                                )
                            )
            return steps

        def lines_of(h):
            return slice(0, half)

        sizes_made = [(deep, half, total)] * cuts
        if riders is not None:
            sizes_made[0] = (deep, half + riders.shape[1], total)
            shaped.append(riders)
        made = move(shaped, sizes_made * (2 * count), into_blocks, name)
        pairs = [tuple(made[cuts * n : cuts * (n + 1)]) for n in range(2 * count)]
        return pairs[:count], pairs[count:]
    whole = jnp.concatenate(
        [g.reshape(deep, high, rows, 2 * wide, w) for g, w in zip(grads, widths)], axis=-1
    ).transpose(1, 3, 0, 2, 4)

    def pick(n, who):
        at = block_place(n, who) + (0, 0, 0)
        part = lax.dynamic_slice(whole, at, (1, 1, deep, rows, total))[0, 0]
        return tuple(part[:, h * half : (h + 1) * half] for h in range(cuts))

    return [pick(n, 0) for n in range(count)], [pick(n, 1) for n in range(count)]


def swap_blocks(blocks):
    return [tuple(swap(part) for part in block) for block in blocks]


def add_blocks(blocks, others):
    made = add_many([a for x in blocks for a in x], [b for y in others for b in y])
    each = len(blocks[0])
    return [tuple(made[each * n : each * (n + 1)]) for n in range(len(blocks))]


def depth_sum(left):
    deep = lax.axis_size("fsdp")
    own = [summed([part[h] for part in left]) for h in range(len(left[0]))]
    own = jnp.concatenate(own, axis=1) if len(own) > 1 else own[0]
    low = own.astype(BF16)
    at = lax.axis_index("fsdp")
    result = lax.dynamic_index_in_dim(low, at, 0, keepdims=False).astype(F32)
    moved = []
    for k in range(1, deep):
        piece = lax.dynamic_index_in_dim(low, (at + k) % deep, 0, keepdims=False)
        moved.append(shift(piece, "fsdp", k))
    return result, moved


def depth_rest(result, moved, end, lines=0):
    result = result + summed(moved)
    if lines:
        rest = [result[: end - lines]] + ([result[end:]] if end < result.shape[0] else [])
        return jnp.concatenate(rest, axis=0), result[end - lines : end]
    return result


def after(value, *gates):
    return lax.optimization_barrier((value,) + gates)[0]


def gated(blocks, *gates):
    flat = [part for block in blocks for part in block]
    made = list(lax.optimization_barrier(tuple(flat) + gates))
    out = []
    for block in blocks:
        out.append(tuple(made[: len(block)]))
        made = made[len(block) :]
    return [out] + made


def regroup(first, second, third):
    made = gated(first + second + third)[0]
    at = len(first)
    return made[:at], made[at : at + len(second)], made[-1]


def row_grads_kernel(own_rows, own_memory, dk, dv, wk, wv, memory, own, own_mem, *blocks):
    n = pl.program_id(0)
    part = product_right(dk[...], wk[...]) + product_right(dv[...], wv[...])

    @pl.when(n == 0)
    def _():
        own[...] = part
        own_mem[...] = memory[...]

    for m in range(1, len(blocks) // 2 + 1):

        @pl.when(n == m)
        def _():
            for h in range(2):
                block = blocks[2 * (m - 1) + h]
                block[:own_rows] = part[h * own_rows : (h + 1) * own_rows].astype(BF16)
                lines = slice(h * own_memory, (h + 1) * own_memory)
                block[own_rows:] = memory[lines].astype(BF16)


def row_grads(dk, dv, wk, wv, memory, own_rows):
    count = len(offsets())
    width = wk.shape[0]
    own_memory = memory.shape[0] // (2 * count)

    def rows_of(size, columns):
        return pl.BlockSpec((size, columns), lambda n: (n, 0))

    def whole(*shape):
        return pl.BlockSpec(shape, lambda n: (0, 0))

    block = (own_rows + own_memory, width)
    own, own_mem, *blocks = pl.pallas_call(
        functools.partial(row_grads_kernel, own_rows, own_memory),
        grid=(count,),
        in_specs=[
            rows_of(2 * own_rows, dk.shape[1]),
            rows_of(2 * own_rows, dv.shape[1]),
            whole(*wk.shape),
            whole(*wv.shape),
            rows_of(2 * own_memory, width),
        ],
        out_specs=[whole(2 * own_rows, width), whole(2 * own_memory, width)]
        + [whole(*block)] * (2 * (count - 1)),
        out_shape=[
            jax.ShapeDtypeStruct((2 * own_rows, width), F32),
            jax.ShapeDtypeStruct((2 * own_memory, width), F32),
        ]
        + [jax.ShapeDtypeStruct(block, BF16)] * (2 * (count - 1)),
        compiler_params=pltpu.CompilerParams(vmem_limit_bytes=VMEM_BYTES),
        name="row_grads",
    )(dk, dv, wk, wv, memory)
    pairs = [(blocks[2 * n], blocks[2 * n + 1]) for n in range(count - 1)]
    return own, own_mem, [pairs[0]] + pairs


RIDER_LINES = 8


def pack_kernel(chunk, *refs):
    made = refs[-1]
    made[...] = jnp.zeros(made.shape, BF16)
    per_line = made.shape[2] // chunk
    at = 0
    for ref in refs[:-1]:
        for row in range(ref.shape[0]):
            for start in range(0, ref.shape[1], chunk):
                line, column = at // per_line, at % per_line * chunk
                value = ref[row : row + 1, start : start + chunk].astype(BF16)
                for copy in range(made.shape[0]):
                    made[copy, line : line + 1, column : column + chunk] = value
                at += 1


def pack_riders(vectors, chunk, deep, total):
    return pl.pallas_call(
        functools.partial(pack_kernel, chunk),
        out_shape=jax.ShapeDtypeStruct((deep, RIDER_LINES, total), BF16),
        name="pack_riders",
    )(*[v.reshape(-1, vectors[0].shape[0]) for v in vectors])


def unpack_riders(lines, chunk, lengths):
    per_line = lines.shape[1] // chunk
    flat = lines[:, : per_line * chunk].reshape(-1)
    starts = column_starts(lengths)
    return [flat[start : start + size] for start, size in zip(starts, lengths)]


def prologue_kernel(inputs, memory, *refs):
    weights, (keep, give, first, second) = refs[:10], refs[10:]
    core = lax.axis_index("tp") % 2
    rows = inputs.shape[1]
    keep[:rows] = inputs[core]
    keep[rows:] = memory[core]
    give[:rows] = inputs[1 - core]
    give[rows:] = memory[1 - core]
    for target, group in ((first, weights[:3]), (second, weights[3:])):
        start = 0
        for ref in group:
            target[:, start : start + ref.shape[1]] = ref[...]
            start += ref.shape[1]


def prologue(inputs, memory, weights):
    rows = weights[0].shape[0]
    widths = [w.shape[1] for w in weights]
    if not aligned(widths):
        core = lax.axis_index("tp") % 2
        both = jnp.concatenate([inputs, memory], axis=1)
        keep = lax.dynamic_index_in_dim(both, core, 0, keepdims=False)
        give = lax.dynamic_index_in_dim(both, 1 - core, 0, keepdims=False)
        return (
            keep,
            give,
            jnp.concatenate(weights[:3], axis=1),
            jnp.concatenate(weights[3:], axis=1),
        )
    block = (inputs.shape[1] + memory.shape[1], inputs.shape[2])
    return pl.pallas_call(
        prologue_kernel,
        out_shape=[
            jax.ShapeDtypeStruct(block, BF16),
            jax.ShapeDtypeStruct(block, BF16),
            jax.ShapeDtypeStruct((rows, sum(widths[:3])), BF16),
            jax.ShapeDtypeStruct((rows, sum(widths[3:])), BF16),
        ],
        compiler_params=pltpu.CompilerParams(vmem_limit_bytes=VMEM_BYTES),
        name="prologue",
    )(inputs, memory, *weights)


def all_sum(value, axes):
    for axis in axes:
        total = lax.axis_size(axis)
        step = 1
        while step < total:
            pairs = [(i, i ^ step) for i in range(total)]
            value = value + lax.ppermute(value, axis, pairs)
            step *= 2
    return value


def per_device(
    inputs,
    memory,
    cotangent,
    positions,
    lengths,
    memory_lengths,
    query_weight,
    key_weight,
    value_weight,
    output_weight,
    cross_query_weight,
    cross_key_weight,
    cross_value_weight,
    cross_output_weight,
    expand_weight,
    reduce_weight,
    query_bias,
    value_bias,
    output_bias,
    first_gain,
    first_shift,
    cross_query_bias,
    cross_value_bias,
    cross_output_bias,
    second_gain,
    second_shift,
    expand_bias,
    reduce_bias,
    third_gain,
    third_shift,
):
    deep, high, wide = sizes()
    z, y, x, core = places()
    own_rows, width = inputs.shape[1:]
    own_memory = memory.shape[1]
    rows = 2 * own_rows
    head_width = query_weight.shape[1]
    hidden_width = expand_weight.shape[1]

    keep, give, first_pack, second_pack = prologue(
        inputs,
        memory,
        [
            query_weight,
            key_weight,
            value_weight,
            cross_key_weight,
            cross_value_weight,
            output_weight.T,
            cross_query_weight,
            cross_output_weight.T,
            expand_weight,
            reduce_weight.T,
        ],
    )
    first_widths = [head_width] * 3
    second_widths = [head_width] * 5 + [hidden_width] * 2

    got = swap(give)
    first_pieces = spread(after(first_pack, got))
    blocks = plane_one(keep, got)
    first_depth = depth_blocks(first_pieces, 1, "stack_first")[0]
    positions = after(positions, first_depth)
    *blocks, (first_depth,) = gated(blocks + [(first_depth,)])[0]
    blocks = plane_two(blocks)
    first_blocks = plane_direct(first_depth)
    second_pieces = spread(after(second_pack, *first_pieces[1:]))
    cotangent_pair = (
        lax.dynamic_index_in_dim(cotangent, core, 0, keepdims=False),
        swap(lax.dynamic_index_in_dim(cotangent, 1 - core, 0, keepdims=False)),
    )
    full_query, full_key, full_value = whole_weights(first_blocks, first_widths, "place_first")
    pieces = [p for b in blocks for p in b]

    def rows_together():
        steps = []
        for n in range(len(pieces)):
            at = n * own_rows
            steps.append((n, slice(0, own_rows), 0, slice(at, at + own_rows)))
            at = n * own_memory
            steps.append(
                (n, slice(own_rows, own_rows + own_memory), 1, slice(at, at + own_memory))
            )
        return steps

    wide_rows, wide_memory = move(
        pieces,
        [(len(pieces) * own_rows, width), (len(pieces) * own_memory, width)],
        rows_together,
        "rows_together",
    )
    rows_in = wide_rows[:rows]
    second_blocks = plane_direct(
        depth_blocks([after(p, wide_rows) for p in second_pieces], 1, "stack_second")[0]
    )

    slots = lax.dynamic_index_in_dim(positions, core, 0, keepdims=False)
    length = lax.dynamic_index_in_dim(lengths, core, 0, keepdims=False)
    memory_length = lax.dynamic_index_in_dim(memory_lengths, core, 0, keepdims=False)
    key_positions = []
    memory_slots = []
    for dx, dy in offsets():
        at_y = (y - dy + high) % high
        at_x = (x - dx + wide) % wide
        for who in (core, 1 - core):
            block = (at_y * wide + at_x) * 2 + who
            key_positions.append(lax.dynamic_slice_in_dim(slots, block * own_rows, own_rows))
            memory_slots.append(block * own_memory + jnp.arange(own_memory, dtype=jnp.int32))
    own_positions = jnp.concatenate(key_positions[:2])
    key_positions = jnp.concatenate(key_positions)
    last = positions.shape[1]
    key_positions = jnp.where(key_positions < length, key_positions, last)[:, None]
    query_positions = own_positions[None, :]
    memory_slots = jnp.concatenate(memory_slots)[:, None]
    memory_limit = jnp.broadcast_to(memory_length - 1, (1, rows))

    query_low = (product(rows_in, full_query) + query_bias).astype(BF16)
    keys = product(wide_rows, full_key).astype(BF16)
    values = (product(wide_rows, full_value) + value_bias).astype(BF16)
    attended, attended_exact, weights = attend(
        query_low, keys, values, query_positions, key_positions
    )
    second_blocks, attended = gated(second_blocks, attended)
    (
        full_cross_key,
        full_cross_value,
        full_output,
        full_cross_query,
        full_cross_output,
        full_expand,
        full_reduce,
    ) = whole_weights(second_blocks, second_widths, "place_second")
    memory_key = product(wide_memory, full_cross_key).astype(BF16)
    memory_value = (product(wide_memory, full_cross_value) + cross_value_bias).astype(BF16)

    first_in = rows_in.astype(F32) + product_right(attended, full_output) + output_bias
    first_out = layer_norm(first_in, first_gain, first_shift)
    first_low = first_out.astype(BF16)
    cross_query = (product(first_low, full_cross_query) + cross_query_bias).astype(BF16)
    cross_attended, cross_exact, cross_weights = attend(
        cross_query, memory_key, memory_value, memory_limit, memory_slots
    )
    second_in = first_out + product_right(cross_attended, full_cross_output) + cross_output_bias
    second_out = layer_norm(second_in, second_gain, second_shift)
    second_low = second_out.astype(BF16)
    expanded = product(second_low, full_expand) + expand_bias
    gate = jax.nn.sigmoid(expanded)
    activated = (expanded * gate).astype(BF16)
    third_in = second_out + product_right(activated, full_reduce) + reduce_bias
    outputs = layer_norm(third_in, third_gain, third_shift)

    grad_in = jnp.concatenate(cotangent_pair, axis=0).astype(F32)
    masked_grad = jnp.where((own_positions < length)[:, None], grad_in, 0.0)
    third_grad, third_gain_part, third_shift_part = norm_back(third_in, third_gain, masked_grad)
    third_low = third_grad.astype(BF16)
    activated_grad = product(third_low, full_reduce)
    expanded_grad = (activated_grad * gate * (1.0 + expanded * (1.0 - gate))).astype(BF16)
    third_part = [
        product_left(second_low, expanded_grad).astype(BF16),
        product_left(third_low, activated).astype(BF16),
    ]
    second_grad = third_grad + product_right(expanded_grad, full_expand)
    second_in_grad, second_gain_part, second_shift_part = norm_back(
        second_in, second_gain, second_grad
    )
    second_grad_low = second_in_grad.astype(BF16)
    cross_attended_grad = product(second_grad_low, full_cross_output).astype(BF16)
    cross_query_grad, memory_key_grad, memory_value_grad, *cross_sums = attend_back(
        cross_query,
        memory_key,
        memory_value,
        cross_weights,
        cross_exact,
        cross_attended_grad,
    )
    first_grad = second_in_grad + product_right(cross_query_grad, full_cross_query)
    first_in_grad, first_gain_part, first_shift_part = norm_back(first_in, first_gain, first_grad)
    first_grad_low = first_in_grad.astype(BF16)
    attended_grad = product(first_grad_low, full_output).astype(BF16)
    second_part = [
        product_left(wide_memory, memory_key_grad).astype(BF16),
        product_left(wide_memory, memory_value_grad).astype(BF16),
        product_left(first_grad_low, attended).astype(BF16),
        product_left(first_low, cross_query_grad).astype(BF16),
        product_left(second_grad_low, cross_attended).astype(BF16),
    ]
    early_vectors = [
        jnp.sum(first_in_grad, axis=0),
        first_gain_part,
        first_shift_part,
        cross_sums[0].reshape(-1),
        cross_sums[1].reshape(-1),
        jnp.sum(second_in_grad, axis=0),
        second_gain_part,
        second_shift_part,
        jnp.sum(expanded_grad.astype(F32), axis=0),
        jnp.sum(third_grad, axis=0),
        third_gain_part,
        third_shift_part,
    ]
    ride = aligned(first_widths + second_widths) and rows % 256 == 0
    early_riders = late_riders = None
    if ride:
        early_riders = pack_riders(early_vectors, 512, deep, sum(second_widths))
    second_keep, second_give = split_grads(
        second_part + third_part, second_widths, 2, early_riders, "split_second"
    )
    second_other = swap_blocks(second_give)
    memory_part = product_right(memory_key_grad, full_cross_key) + product_right(
        memory_value_grad, full_cross_value
    )

    second_blocks = add_blocks(second_keep, second_other)
    second_blocks, early_grad = gated(second_blocks, attended_grad)
    second_blocks = sum_one(second_blocks)
    early = list(
        attend_back(query_low, keys, values, weights, attended_exact, early_grad, 0, 2)
    )
    second_blocks, early[0] = gated(second_blocks, early[0])
    second_blocks = sum_adds(second_blocks)
    second_blocks, late_grad = gated(second_blocks, attended_grad)
    second_left = sum_two(second_blocks)
    query_grad, key_grad, value_grad, *self_sums = attend_back(
        query_low, keys, values, weights, attended_exact, late_grad, 1, 2, early
    )
    input_part, memory_own, low_blocks = row_grads(
        key_grad, value_grad, full_key, full_value, memory_part, own_rows
    )
    low_blocks, second_left, (query_late, key_late, value_late) = regroup(
        low_blocks, second_left, [(query_grad, key_grad, value_grad)]
    )
    low_blocks = sum_one(low_blocks)
    second_own, second_moved = depth_sum(second_left)
    input_own = first_in_grad + product_right(query_late, full_query)
    first_part = [
        product_left(rows_in, query_late).astype(BF16),
        product_left(wide_rows, key_late).astype(BF16),
        product_left(wide_rows, value_late).astype(BF16),
    ]
    late_vectors = [self_sums[0].reshape(-1), self_sums[1].reshape(-1)]
    low_blocks = sum_adds(low_blocks)
    low_blocks, unused, first_part = regroup(low_blocks, [], [tuple(first_part)])
    left = sum_two(low_blocks)[1:]
    if ride:
        late_riders = pack_riders(late_vectors, 128, deep, sum(first_widths))
    first_keep, first_give = split_grads(first_part, first_widths, 1, late_riders, "split_first")
    first_other = swap_blocks(first_give)
    left, first_keep, unused = regroup(left, first_keep, [()])
    first_blocks = add_blocks(first_keep, first_other)
    first_left = sum_direct(first_blocks)
    first_left, unused, second_moved = regroup(first_left, [], [tuple(second_moved)])
    first_own, first_moved = depth_sum(first_left)
    ends = first_left[0][0].shape[1], second_left[0][0].shape[1]
    first_shard = depth_rest(first_own, first_moved, ends[0], RIDER_LINES if ride else 0)
    second_shard = depth_rest(second_own, second_moved, ends[1], RIDER_LINES if ride else 0)
    pair = [summed([part[h] for part in left]) for h in range(2)]
    input_pair = [
        input_own[h * own_rows : (h + 1) * own_rows]
        + input_part[h * own_rows : (h + 1) * own_rows]
        + pair[h][:own_rows]
        for h in range(2)
    ]
    memory_pair = [
        memory_own[h * own_memory : (h + 1) * own_memory] + pair[h][own_rows:] for h in range(2)
    ]

    def restore(pair):
        other = swap(pair[1])
        return jnp.where(
            core == 0, jnp.stack([pair[0], other]), jnp.stack([other, pair[0]])
        )

    output_result = restore([outputs[:own_rows], outputs[own_rows:]])
    input_result = restore(input_pair)
    memory_result = restore(memory_pair)

    vectors = late_vectors + early_vectors
    lengths = [v.shape[0] for v in vectors]
    if ride:
        first_shard, late_lines = first_shard
        second_shard, early_lines = second_shard
        split = unpack_riders(late_lines, 128, lengths[:2])
        split += unpack_riders(early_lines, 512, lengths[2:])
    else:
        joined = all_sum(jnp.concatenate(vectors), ("fsdp", "tp", "ctx"))
        starts = column_starts(lengths)
        split = [joined[start : start + size] for start, size in zip(starts, lengths)]

    def shards(packed, widths):
        start = 0
        parts = []
        for one in widths:
            parts.append(packed[:, start : start + one])
            start += one
        return parts

    g_query, g_key, g_value = shards(first_shard, first_widths)
    (
        g_cross_key,
        g_cross_value,
        g_output,
        g_cross_query,
        g_cross_output,
        g_expand,
        g_reduce,
    ) = shards(second_shard, second_widths)
    return (
        output_result,
        input_result,
        memory_result,
        g_query,
        g_key,
        g_value,
        g_output.T,
        g_cross_query,
        g_cross_key,
        g_cross_value,
        g_cross_output.T,
        g_expand,
        g_reduce.T,
        *split,
    )


def solution(mesh):
    rows = P("fsdp", ("ctx", "tp"), None)
    tall = P(("fsdp", "ctx"), "tp")
    flat = P("tp", ("fsdp", "ctx"))
    weights = (tall, tall, tall, flat, tall, tall, tall, flat, tall, flat)
    return jax.shard_map(
        per_device,
        mesh=mesh,
        in_specs=(rows, rows, rows, P("fsdp", None), P("fsdp"), P("fsdp"))
        + weights
        + (P(),) * 14,
        out_specs=(rows, rows, rows) + weights + (P(),) * 14,
        check_vma=False,
    )
```
